32 devices in a mesh: dp: 8 (over z, y), inner: 4 (over x, core).
Axes of the slice: x: 2, y: 2, z: 4, core: 2. Of those that a mesh axis runs over, the one named last changes fastest.
Arguments:
- tokens: bfloat16 [32768, 512], P(('dp', 'inner')), may hold values from -6 to 6
- segments: int32 [32768], P(('dp', 'inner')), may hold values from 0 to 32767, as said below
- positions: int32 [32768], P(('dp', 'inner')), may hold values from 0 to 1023, as said below
- cotangent: bfloat16 [32768, 512], P(('dp', 'inner')), may hold values from -6 to 6
- attn_weight: float32 [4, 512, 512], P(None, ('dp', 'inner')), may hold values from -0.53033009 to 0.53033009
- attn_m: float32 [4, 512, 512], P(None, ('dp', 'inner')), may hold values from -0.0007324219 to 0.0007324219
- attn_v: float32 [4, 512, 512], P(None, ('dp', 'inner')), may hold values from 1.0882435e-09 to 4.352974e-09
- gate_weight: float32 [2, 512, 512], P(None, ('dp', 'inner')), may hold values from -0.25 to 0.25
- gate_m: float32 [2, 512, 512], P(None, ('dp', 'inner')), may hold values from -0.00036621094 to 0.00036621094
- gate_v: float32 [2, 512, 512], P(None, ('dp', 'inner')), may hold values from 2.7206087e-10 to 1.0882435e-09
- in_weight: float32 [512, 2048], P(('dp', 'inner')), may hold values from -0.25 to 0.25
- in_m: float32 [512, 2048], P(('dp', 'inner')), may hold values from -0.00036621094 to 0.00036621094
- in_v: float32 [512, 2048], P(('dp', 'inner')), may hold values from 2.7206087e-10 to 1.0882435e-09
- out_weight: float32 [2048, 512], P(('dp', 'inner')), may hold values from -0.125 to 0.125
- out_m: float32 [2048, 512], P(('dp', 'inner')), may hold values from -0.00036621094 to 0.00036621094
- out_v: float32 [2048, 512], P(('dp', 'inner')), may hold values from 2.7206087e-10 to 1.0882435e-09
- norm_params: float32 [7, 512], P(None, ('dp', 'inner'))
- norm_m: float32 [7, 512], P(None, ('dp', 'inner')), may hold values from -0.0014648438 to 0.0014648438
- norm_v: float32 [7, 512], P(None, ('dp', 'inner')), may hold values from 4.352974e-09 to 1.7411896e-08
- in_bias: float32 [2048], P(('dp', 'inner')), may hold values from -1.75 to 1.75
- bias_m: float32 [2048], P(('dp', 'inner')), may hold values from -0.00024414062 to 0.00024414062
- bias_v: float32 [2048], P(('dp', 'inner')), may hold values from 1.7411896e-10 to 7.073583e-10
Outputs:
- layer_out: bfloat16 [32768, 512], P(('dp', 'inner'))
- input_grad: bfloat16 [32768, 512], P(('dp', 'inner'))
- grad_norm: float32 [], replicated
- attn_new: float32 [4, 512, 512], P(None, ('dp', 'inner'))
- attn_m_new: float32 [4, 512, 512], P(None, ('dp', 'inner'))
- attn_v_new: float32 [4, 512, 512], P(None, ('dp', 'inner'))
- gate_new: float32 [2, 512, 512], P(None, ('dp', 'inner'))
- gate_m_new: float32 [2, 512, 512], P(None, ('dp', 'inner'))
- gate_v_new: float32 [2, 512, 512], P(None, ('dp', 'inner'))
- in_new: float32 [512, 2048], P(('dp', 'inner'))
- in_m_new: float32 [512, 2048], P(('dp', 'inner'))
- in_v_new: float32 [512, 2048], P(('dp', 'inner'))
- out_new: float32 [2048, 512], P(('dp', 'inner'))
- out_m_new: float32 [2048, 512], P(('dp', 'inner'))
- out_v_new: float32 [2048, 512], P(('dp', 'inner'))
- norm_new: float32 [7, 512], P(None, ('dp', 'inner'))
- norm_m_new: float32 [7, 512], P(None, ('dp', 'inner'))
- norm_v_new: float32 [7, 512], P(None, ('dp', 'inner'))
- bias_new: float32 [2048], P(('dp', 'inner'))
- bias_m_new: float32 [2048], P(('dp', 'inner'))
- bias_v_new: float32 [2048], P(('dp', 'inner'))
The draws below stay inside these ranges and needn't reach their ends.
Inputs may be any that keep to these rules, and one draw needn't show every extreme that they name: `segments`: a token's segment number is the index of its document's first token, so segment numbers never fall; a new document begins at every sequence start (every 1024 tokens); the first sequence is one document; the last token forms a document of its own. positions restart at 0 with every new segment number.
All inputs are finite; a program needn't handle non-finite values.
Results may differ from the reference program's by a relative error of at most 0.033.
The reference program's roundings to bfloat16 on the way count: a program that leaves them out, or rounds other values in their place, can miss the bound.
Values may be sent and summed in bfloat16 or wider, within the bound.
No kernel may reach another device: no remote copies, remote signals or barrier semaphores. Data moves between devices by JAX's collectives and lax.ppermute only.
A program may use at most 192 MiB of HBM per device.

```python
import math
import jax
import jax.numpy as jnp
from jax import lax

D = 512
HEADS = 8
HEAD = 64
FF = 2048
TOK_DEV = 1024
DOC_MEAN = 256
STEP = 10
TOKENS = 32768
NPARAM = 3675648
N_DP = 8
N_INNER = 4


def document_layout(key):
    sub_key = jax.random.fold_in(key, 7)
    token_index = jnp.arange(TOKENS, dtype=jnp.int32)
    new_starts = jax.random.randint(sub_key, (TOKENS,), 0, DOC_MEAN) == 0
    starts = new_starts & (token_index >= TOK_DEV) | (token_index % TOK_DEV == 0) | (token_index == TOKENS - 1)
    begins = lax.cummax(jnp.where(starts, token_index, 0), axis=0)
    return (begins.astype(jnp.int32), (token_index - begins).astype(jnp.int32))


def draw_segments(key, part):
    return document_layout(key)[0]


def draw_positions(key, part):
    return document_layout(key)[1]


def draw_attn_weight(key, part):
    base_draw = jnp.clip(jax.random.normal(key, (4, D, D), jnp.float32), -3.0, 3.0)
    out_boost = jnp.where(jnp.arange(4)[:, None, None] == 3, 4.0, 1.0)
    return base_draw * out_boost / math.sqrt(D)


def draw_norm_params(key, part):
    sub_keys = jax.random.split(key, 2)
    gain_ramp = jnp.exp(jnp.log(3.0) * jnp.arange(D, dtype=jnp.float32) / D)
    jitter = jax.random.uniform(sub_keys[0], (7, D), jnp.float32, 0.8, 1.2)
    bias_noise = jnp.clip(jax.random.normal(sub_keys[1], (7, D), jnp.float32) * 0.35, -1.2, 1.2)
    gain_rows = 0.6 * gain_ramp[None, :] * jitter
    is_gain = (jnp.arange(7) == 0) | (jnp.arange(7) == 2)
    return jnp.where(is_gain[:, None], gain_rows, bias_noise)


def spiked(array, own_key, source, target, parts, factor):
    owner, partner = [(jnp.arange(array.shape[dim]) // (array.shape[dim] // parts)).reshape([-1 if axis == dim else 1 for axis in range(array.ndim)]) for dim in (source, target)]
    chosen = jax.random.permutation(own_key, parts)[partner]
    strong = (owner == chosen) | (owner == (partner + parts // 2) % parts)
    return jnp.where(strong, factor * array, array)


def steps_of(own_key, shape, cuts, low, largest):
    level = 1.0
    for axis_at, parts in cuts:
        draws = jax.random.uniform(jax.random.fold_in(jax.random.fold_in(own_key, 6), axis_at), (parts,), jnp.float32, low / len(cuts), largest / len(cuts))
        level = level * jnp.repeat(jnp.exp(draws), shape[axis_at] // parts).reshape((-1,) + (1,) * (len(shape) - 1 - axis_at))
    return level


def normal_values(key, extent, width, bound, cuts=(), kind=jnp.bfloat16):
    values = width * jax.random.normal(key, extent, jnp.float32)
    if cuts:
        values = values * steps_of(key, extent, cuts, -0.22, 0.18)
    return jnp.clip(values, -bound, bound).astype(kind)


def bell_draw_with(rng, shape, scale, reach, cuts, heavy, kind=jnp.bfloat16):
    values = scale * jax.random.normal(rng, shape, jnp.float32)
    if cuts:
        values = values * steps_of(rng, shape, cuts, -0.22, 0.18)
    return jnp.clip(spiked(values, jax.random.fold_in(rng, 3), *heavy), -reach, reach).astype(kind)


def setup_inputs(seed: int = 0) -> dict:
    arg_keys = jax.random.split(jax.random.key(seed), 23)
    tokens = bell_draw_with(arg_keys[0], (TOKENS, D), 1.0, 6.0, ((0, 32),), (0, 1, 32, 2.75))
    segments = draw_segments(jax.random.fold_in(arg_keys[22], 71), 0)
    positions = draw_positions(jax.random.fold_in(arg_keys[22], 71), 0)
    cotangent = normal_values(arg_keys[3], (TOKENS, D), 1.0, 6.0, ((0, 32),))
    attn_weight = draw_attn_weight(jax.random.fold_in(arg_keys[22], 71), 0)
    attn_m = normal_values(arg_keys[5], (4, D, D), (0.22 / NPARAM ** 0.5), 0.0007324219, ((1, 32),), jnp.float32)
    attn_v = jnp.clip(jnp.exp(math.log(4.35297398126977e-09) - 1.3862944 * jax.random.uniform(arg_keys[6], (4, D, D), jnp.float32) ** steps_of(arg_keys[6], (4, D, D), ((1, 32),), -0.2, 0.2)), 1.0882434953174425e-09, 4.35297398126977e-09)
    gate_weight = normal_values(arg_keys[7], (2, D, D), D ** -0.5, 0.25, ((1, 32),), jnp.float32)
    gate_m = normal_values(arg_keys[8], (2, D, D), (0.11 / NPARAM ** 0.5), 0.00036621094, ((1, 32),), jnp.float32)
    gate_v = jnp.clip(jnp.exp(math.log(1.0882434953174425e-09) - 1.3862944 * jax.random.uniform(arg_keys[9], (2, D, D), jnp.float32) ** steps_of(arg_keys[9], (2, D, D), ((1, 32),), -0.2, 0.2)), 2.720608738293606e-10, 1.0882434953174425e-09)
    in_weight = normal_values(arg_keys[10], (D, FF), D ** -0.5, 0.25, ((0, 32),), jnp.float32)
    in_m = normal_values(arg_keys[11], (D, FF), (0.11 / NPARAM ** 0.5), 0.00036621094, ((0, 32),), jnp.float32)
    in_v = jnp.clip(jnp.exp(math.log(1.0882434953174425e-09) - 1.3862944 * jax.random.uniform(arg_keys[12], (D, FF), jnp.float32) ** steps_of(arg_keys[12], (D, FF), ((0, 32),), -0.2, 0.2)), 2.720608738293606e-10, 1.0882434953174425e-09)
    out_weight = normal_values(arg_keys[13], (FF, D), FF ** -0.5, 0.125, ((0, 32),), jnp.float32)
    out_m = normal_values(arg_keys[14], (FF, D), (0.11 / NPARAM ** 0.5), 0.00036621094, ((0, 32),), jnp.float32)
    out_v = jnp.clip(jnp.exp(math.log(1.0882434953174425e-09) - 1.3862944 * jax.random.uniform(arg_keys[15], (FF, D), jnp.float32) ** steps_of(arg_keys[15], (FF, D), ((0, 32),), -0.2, 0.2)), 2.720608738293606e-10, 1.0882434953174425e-09)
    norm_params = draw_norm_params(jax.random.fold_in(arg_keys[22], 71), 0)
    norm_m = normal_values(arg_keys[17], (7, D), (0.44 / NPARAM ** 0.5), 0.0014648438, ((1, 32),), jnp.float32)
    norm_v = jnp.clip(jnp.exp(math.log(1.741189592507908e-08) - 1.3862944 * jax.random.uniform(arg_keys[18], (7, D), jnp.float32) ** steps_of(arg_keys[18], (7, D), ((1, 32),), -0.2, 0.2)), 4.35297398126977e-09, 1.741189592507908e-08)
    in_bias = normal_values(arg_keys[19], (FF,), 0.3, 1.75, ((0, 32),), jnp.float32)
    bias_m = normal_values(arg_keys[20], (FF,), (0.08 / NPARAM ** 0.5), 0.00024414062, ((0, 32),), jnp.float32)
    bias_v = jnp.clip(jnp.exp(math.log(7.073582830585678e-10) - 1.4017986 * jax.random.uniform(arg_keys[21], (FF,), jnp.float32) ** steps_of(arg_keys[21], (FF,), ((0, 32),), -0.2, 0.2)), 1.741189553650102e-10, 7.073582830585678e-10)
    return dict(tokens=tokens, segments=segments, positions=positions, cotangent=cotangent, attn_weight=attn_weight, attn_m=attn_m, attn_v=attn_v, gate_weight=gate_weight, gate_m=gate_m, gate_v=gate_v, in_weight=in_weight, in_m=in_m, in_v=in_v, out_weight=out_weight, out_m=out_m, out_v=out_v, norm_params=norm_params, norm_m=norm_m, norm_v=norm_v, in_bias=in_bias, bias_m=bias_m, bias_v=bias_v)


@jax.custom_vjp
def low(v):
    return lax.optimization_barrier(v.astype(jnp.bfloat16)).astype(jnp.float32)

@jax.custom_vjp
def low_back(v):
    return v

def low_keep(v):
    return (low(v), None)

def low_pass(kept, grad):
    return (grad,)

def back_keep(v):
    return (v, None)

def back_low(kept, grad):
    return (low(grad),)
low.defvjp(low_keep, low_pass)
low_back.defvjp(back_keep, back_low)
norm_eps = 1e-05
first_decay = 0.9
second_decay = 0.999
adam_eps = 1e-08
learn_rate = 0.05
vector_rate = 0.8
weight_decay = 0.1
clip_norm = 1.0
masked_score = -1e+30

def precise(left_side, right_side):
    return jnp.matmul(left_side, right_side, precision=lax.Precision.HIGHEST)

def normalize(values, gain_row, bias_row):
    centred = values - lax.optimization_barrier(jnp.mean(values, -1, keepdims=True))
    spread = lax.optimization_barrier(jnp.mean(centred * centred, -1, keepdims=True))
    return centred * lax.rsqrt(spread + norm_eps) * gain_row + bias_row

def forward(params, inputs, segments, positions):
    attn_w, gate_w, in_w, out_w, vectors, hidden_bias = [low(element) for element in params]
    groups, length, model_width = inputs.shape
    normed = low(normalize(inputs, vectors[0], vectors[1]))

    def split_heads(values):
        return values.reshape(groups, length, HEADS, HEAD)
    queries = low(low_back(precise(normed, attn_w[0])))
    key_rows = low(low_back(precise(normed, attn_w[1])))
    value_rows = low(low_back(precise(normed, attn_w[2])))
    raw_scores = low_back(jnp.einsum('gqhe,gkhe->ghqk', split_heads(queries), split_heads(key_rows), precision=lax.Precision.HIGHEST))
    allowed = (segments[:, :, None] == segments[:, None, :]) & (positions[:, None, :] <= positions[:, :, None])
    scores = jnp.where(allowed[:, None], raw_scores * HEAD ** (-0.5), masked_score)
    row_max = lax.optimization_barrier(jnp.max(scores, -1, keepdims=True))
    weights = jnp.exp(scores - row_max)
    attn_probs = low(weights / lax.optimization_barrier(jnp.sum(weights, -1, keepdims=True)))
    mixed_heads = jnp.einsum('ghqk,gkhe->gqhe', attn_probs, split_heads(value_rows), precision=lax.Precision.HIGHEST)
    mixed_heads = low(low_back(mixed_heads.reshape(groups, length, model_width)))
    attended = low_back(precise(mixed_heads, attn_w[3]))
    attn_gate = jax.nn.sigmoid(low_back(precise(normed, gate_w[0])) + vectors[4])
    middle = attn_gate * attended + (1.0 - attn_gate) * inputs
    normed_two = low(normalize(middle, vectors[2], vectors[3]))
    hidden = low_back(precise(normed_two, in_w)) + hidden_bias
    active = low(jnp.maximum(hidden, 0.0))
    branch = low_back(precise(active, out_w)) + vectors[6]
    ffn_gate = jax.nn.sigmoid(low_back(precise(normed_two, gate_w[1])) + vectors[5])
    return ffn_gate * branch + (1.0 - ffn_gate) * middle

def adam_update(weight, first_moment, second_moment, gradient, factor, step_rate):
    clipped = gradient * factor
    first_new = first_decay * first_moment + (1.0 - first_decay) * clipped
    second_new = second_decay * second_moment + (1.0 - second_decay) * clipped * clipped
    corrected = first_new / (1.0 - first_decay ** STEP)
    spread = second_new / (1.0 - second_decay ** STEP)
    weight_new = weight - step_rate * (corrected / (jnp.sqrt(spread) + adam_eps) + weight_decay * weight)
    return (weight_new, first_new, second_new)

def reference(tokens, segments, positions, cotangent, attn_weight, attn_m, attn_v, gate_weight, gate_m, gate_v, in_weight, in_m, in_v, out_weight, out_m, out_v, norm_params, norm_m, norm_v, in_bias, bias_m, bias_v):
    sequences = N_DP * N_INNER
    per_group = min(sequences, max(1, 4096 // TOK_DEV))
    group_count = sequences // per_group
    params = (attn_weight, gate_weight, in_weight, out_weight, norm_params, in_bias)
    input_groups = tokens.astype(jnp.float32).reshape(group_count, per_group, TOK_DEV, D)
    cot_groups = cotangent.astype(jnp.float32).reshape(group_count, per_group, TOK_DEV, D)
    seg_groups = segments.reshape(group_count, per_group, TOK_DEV)
    pos_groups = positions.reshape(group_count, per_group, TOK_DEV)

    def seq_step(grad_total, element):
        inputs, cot_part, seg_part, pos_part = element
        outputs, pull_back = jax.vjp(lambda params_in, inputs_in: forward(params_in, inputs_in, seg_part, pos_part), params, inputs)
        param_grads, input_part = pull_back(cot_part)
        grad_total = jax.tree.map(jnp.add, grad_total, param_grads)
        return (grad_total, (outputs.astype(jnp.bfloat16), input_part.astype(jnp.bfloat16)))
    zero_grads = tuple((jnp.zeros_like(element, dtype=jnp.float32) for element in params))
    weight_grads, (out_groups, grad_groups) = lax.scan(seq_step, zero_grads, (input_groups, cot_groups, seg_groups, pos_groups))
    squares = sum((jnp.sum(element * element) for element in weight_grads))
    grad_norm = jnp.sqrt(squares)
    factor = jnp.minimum(1.0, clip_norm / (grad_norm + 1e-06))
    states = ((attn_weight, attn_m, attn_v), (gate_weight, gate_m, gate_v), (in_weight, in_m, in_v), (out_weight, out_m, out_v), (norm_params, norm_m, norm_v), (in_bias, bias_m, bias_v))
    step_rates = (learn_rate, learn_rate, learn_rate, learn_rate, vector_rate, vector_rate)
    updated = [adam_update(state[0], state[1], state[2], gradient, factor, step_rate) for state, gradient, step_rate in zip(states, weight_grads, step_rates)]
    layer_out = out_groups.reshape(TOKENS, D)
    input_grad = grad_groups.reshape(TOKENS, D)
    return (layer_out, input_grad, grad_norm, updated[0][0], updated[0][1], updated[0][2], updated[1][0], updated[1][1], updated[1][2], updated[2][0], updated[2][1], updated[2][2], updated[3][0], updated[3][1], updated[3][2], updated[4][0], updated[4][1], updated[4][2], updated[5][0], updated[5][1], updated[5][2])
```

```python
import functools
import jax
import jax.numpy as jnp
from jax import lax
from jax.sharding import PartitionSpec as P

AXES = ("dp", "inner")
HEADS = 8
HEAD = 64
STEP = 10


norm_eps = 1e-05
first_decay = 0.9
second_decay = 0.999
adam_eps = 1e-08
learn_rate = 0.05
vector_rate = 0.8
weight_decay = 0.1
clip_norm = 1.0
masked_score = -1e30


def normalize_parts(values, gain_row, bias_row):
    centred = values - jnp.mean(values, -1, keepdims=True)
    spread = jnp.mean(centred * centred, -1, keepdims=True)
    scale_row = lax.rsqrt(spread + norm_eps)
    unit_rows = centred * scale_row
    return (unit_rows * gain_row + bias_row, unit_rows, scale_row)


def normalize_back(grad_rows, unit_rows, scale_row, gain_row):
    grad_unit = grad_rows * gain_row
    return scale_row * (
        grad_unit
        - jnp.mean(grad_unit, -1, keepdims=True)
        - unit_rows * jnp.mean(grad_unit * unit_rows, -1, keepdims=True)
    )


def bit_groups(sizes):
    dp_bits = sizes["dp"].bit_length() - 1
    inner_bits = sizes["inner"].bit_length() - 1
    y_bits = dp_bits // 2
    plane_bits = (inner_bits - 1) + y_bits
    return (1, plane_bits, dp_bits - y_bits)


def swap_with(array, offset, count):
    return lax.ppermute(array, AXES, [(source, source ^ offset) for source in range(count)])


def gather_chunk(shard, groups):
    count = 2 ** sum(groups)
    full = shard[None]
    low_bits = groups[0] + groups[1]
    for first_bit, bits in ((low_bits, groups[2]), (groups[0], groups[1]), (0, groups[0])):
        parts = [full] + [
            swap_with(full, offset << first_bit, count) for offset in range(1, 2**bits)
        ]
        full = jnp.stack(parts, 1)
        full = full.reshape((-1,) + shard.shape)
    return full


def reduce_chunk(blocks, groups):
    count = 2 ** sum(groups)
    first_bit = 0
    current = blocks
    for bits in groups:
        split = current.reshape((-1, 2**bits) + blocks.shape[1:])
        total = split[:, 0].astype(jnp.float32)
        for offset in range(1, 2**bits):
            sent = split[:, offset].astype(jnp.bfloat16)
            total = total + swap_with(sent, offset << first_bit, count).astype(jnp.float32)
        first_bit += bits
        current = total
    return current[0]


def sum_all(value, groups):
    count = 2 ** sum(groups)
    first_bit = 0
    for bits in groups:
        value = sum(
            [value] + [swap_with(value, offset << first_bit, count) for offset in range(1, 2**bits)]
        )
        first_bit += bits
    return value


def pack(arrays, count):
    attn, gate, w_in, w_out, vec, bias = arrays
    width = 512
    step = attn.shape[1] // count
    parts = []
    for matrix in [attn[0], attn[1], attn[2], gate[0], attn[3], gate[1]]:
        parts.append(matrix.reshape(count, step, width))
    for column in range(4):
        parts.append(w_in[:, column * width : (column + 1) * width].reshape(count, step, width))
    parts.append(w_out.reshape(count, 4 * step, width))
    small = jnp.concatenate(
        [vec.reshape(7, count, step).transpose(1, 0, 2).reshape(count, 7 * step), bias.reshape(count, 4 * step)], 1
    )
    small = jnp.pad(small, ((0, 0), (0, width - small.shape[1])))
    parts.append(small[:, None])
    return jnp.concatenate([part.astype(jnp.bfloat16) for part in parts], 1)


def unpack(rows, count):
    width = 512
    step = (rows.shape[1] - 1) // 14
    pieces = [rows[:, step * index : step * (index + 1)].reshape(count * step, width) for index in range(10)]
    attn = jnp.stack([pieces[0], pieces[1], pieces[2], pieces[4]])
    gate = jnp.stack([pieces[3], pieces[5]])
    w_in = jnp.concatenate(pieces[6:10], 1)
    w_out = rows[:, 10 * step : 14 * step].reshape(count * step * 4, width)
    small = rows[:, 14 * step]
    vec = small[:, : 7 * step].reshape(count, 7, step).transpose(1, 0, 2).reshape(7, count * step)
    bias = small[:, 7 * step : 11 * step].reshape(-1)
    return (attn, gate, w_in, w_out, vec, bias)


def score_block(queries, key_heads, segments, positions, first_row, block_size):
    query_part = lax.slice_in_dim(queries, first_row, first_row + block_size, axis=0)
    raw_scores = jnp.einsum(
        "qhe,khe->hqk", query_part, key_heads, preferred_element_type=jnp.float32
    )
    own_segments = lax.slice_in_dim(segments, first_row, first_row + block_size, axis=0)
    own_positions = lax.slice_in_dim(positions, first_row, first_row + block_size, axis=0)
    allowed = (own_segments[:, None] == segments[None, :]) & (
        positions[None, :] <= own_positions[:, None]
    )
    return (jnp.where(allowed[None], raw_scores * HEAD ** (-0.5), masked_score), query_part)


def attend(triple, segments, positions):
    row_count = triple.shape[1]
    block_size = min(512, row_count)
    queries = triple[0].reshape(row_count, HEADS, HEAD)
    key_heads = triple[1].reshape(row_count, HEADS, HEAD)
    value_heads = triple[2].reshape(row_count, HEADS, HEAD)
    mixed_parts = []
    total_parts = []
    for first_row in range(0, row_count, block_size):
        scores, query_part = score_block(
            queries, key_heads, segments, positions, first_row, block_size
        )
        row_max = jnp.max(scores, -1, keepdims=True)
        weights = jnp.exp(scores - row_max)
        exp_total = jnp.sum(weights, -1, keepdims=True)
        attn_probs = (weights / exp_total).astype(jnp.bfloat16)
        mixed_block = jnp.einsum(
            "hqk,khe->qhe", attn_probs, value_heads, preferred_element_type=jnp.float32
        )
        mixed_parts.append(mixed_block.reshape(block_size, HEADS * HEAD))
        total_parts.append(row_max + jnp.log(exp_total))
    mixed_heads = jnp.concatenate(mixed_parts, 0).astype(jnp.bfloat16)
    return (mixed_heads, jnp.concatenate(total_parts, 1))


def attend_back(triple, grad_mixed, log_total, segments, positions):
    row_count = triple.shape[1]
    block_size = min(512, row_count)
    queries = triple[0].reshape(row_count, HEADS, HEAD)
    key_heads = triple[1].reshape(row_count, HEADS, HEAD)
    value_heads = triple[2].reshape(row_count, HEADS, HEAD)
    grad_heads = grad_mixed.reshape(row_count, HEADS, HEAD)
    query_grads = []
    grad_keys = jnp.zeros((row_count, HEADS, HEAD), jnp.float32)
    grad_values = jnp.zeros((row_count, HEADS, HEAD), jnp.float32)
    for first_row in range(0, row_count, block_size):
        scores, query_part = score_block(
            queries, key_heads, segments, positions, first_row, block_size
        )
        attn_probs = jnp.exp(
            scores - lax.slice_in_dim(log_total, first_row, first_row + block_size, axis=1)
        )
        grad_part = lax.slice_in_dim(grad_heads, first_row, first_row + block_size, axis=0)
        grad_probs = jnp.einsum(
            "qhe,khe->hqk", grad_part, value_heads, preferred_element_type=jnp.float32
        )
        row_inner = jnp.sum(attn_probs * grad_probs, -1, keepdims=True)
        grad_raw = (attn_probs * (grad_probs - row_inner) * HEAD ** (-0.5)).astype(jnp.bfloat16)
        query_grads.append(
            jnp.einsum(
                "hqk,khe->qhe", grad_raw, key_heads, preferred_element_type=jnp.float32
            ).reshape(block_size, HEADS * HEAD)
        )
        grad_keys = grad_keys + jnp.einsum(
            "hqk,qhe->khe", grad_raw, query_part, preferred_element_type=jnp.float32
        )
        grad_values = grad_values + jnp.einsum(
            "hqk,qhe->khe",
            attn_probs.astype(jnp.bfloat16),
            grad_part,
            preferred_element_type=jnp.float32,
        )
    grad_query_rows = jnp.concatenate(query_grads, 0)
    stacked = jnp.stack(
        [
            grad_query_rows,
            grad_keys.reshape(row_count, HEADS * HEAD),
            grad_values.reshape(row_count, HEADS * HEAD),
        ]
    )
    return stacked.astype(jnp.bfloat16)


def attn_branch(weights, normed, segments, positions):
    triple = jnp.einsum(
        "td,jde->jte", normed, weights[0][:3], preferred_element_type=jnp.float32
    ).astype(jnp.bfloat16)
    mixed_heads, log_total = attend(triple, segments, positions)
    attended = jnp.dot(mixed_heads, weights[0][3], preferred_element_type=jnp.float32)
    return (triple, mixed_heads, log_total, attended)


def ffn_branch(weights, normed_two):
    hidden = jnp.dot(normed_two, weights[2], preferred_element_type=jnp.float32) + weights[
        5
    ].astype(jnp.float32)
    active = jnp.maximum(hidden, 0.0).astype(jnp.bfloat16)
    branch = jnp.dot(active, weights[3], preferred_element_type=jnp.float32) + weights[4][6].astype(
        jnp.float32
    )
    return (hidden, active, branch)


def adam_update(weight, first_moment, second_moment, gradient, factor, step_rate):
    clipped = gradient * factor
    first_new = first_decay * first_moment + (1.0 - first_decay) * clipped
    second_new = second_decay * second_moment + (1.0 - second_decay) * clipped * clipped
    corrected = first_new / (1.0 - first_decay**STEP)
    spread = second_new / (1.0 - second_decay**STEP)
    weight_new = weight - step_rate * (
        corrected / (jnp.sqrt(spread) + adam_eps) + weight_decay * weight
    )
    return (weight_new, first_new, second_new)


def body(
    groups,
    tokens,
    segments,
    positions,
    cotangent,
    attn_weight,
    attn_m,
    attn_v,
    gate_weight,
    gate_m,
    gate_v,
    in_weight,
    in_m,
    in_v,
    out_weight,
    out_m,
    out_v,
    norm_params,
    norm_m,
    norm_v,
    in_bias,
    bias_m,
    bias_v,
):
    shards = (attn_weight, gate_weight, in_weight, out_weight, norm_params, in_bias)
    count = 2 ** sum(groups)
    own = lax.axis_index(AXES)
    order = jnp.arange(count) ^ own
    shard_rows = pack(shards, 1)[0]
    gathered = gather_chunk(shard_rows, groups)
    weights = unpack(jnp.take(gathered, order, axis=0), count)
    vectors = weights[4].astype(jnp.float32)
    inputs = tokens.astype(jnp.float32)
    normed_full, unit_one, scale_one = normalize_parts(inputs, vectors[0], vectors[1])
    normed = normed_full.astype(jnp.bfloat16)
    triple, mixed_heads, log_total, attended = attn_branch(weights, normed, segments, positions)
    attn_gate = jax.nn.sigmoid(
        jnp.dot(normed, weights[1][0], preferred_element_type=jnp.float32) + vectors[4]
    )
    middle = attn_gate * attended + (1.0 - attn_gate) * inputs
    normed_two_full, unit_two, scale_two = normalize_parts(middle, vectors[2], vectors[3])
    normed_two = normed_two_full.astype(jnp.bfloat16)
    hidden, active, branch = ffn_branch(weights, normed_two)
    ffn_gate = jax.nn.sigmoid(
        jnp.dot(normed_two, weights[1][1], preferred_element_type=jnp.float32) + vectors[5]
    )
    layer_out = (ffn_gate * branch + (1.0 - ffn_gate) * middle).astype(jnp.bfloat16)
    grad_out = cotangent.astype(jnp.float32)
    grad_branch = grad_out * ffn_gate
    grad_fgate = grad_out * (branch - middle) * ffn_gate * (1.0 - ffn_gate)
    grad_middle = grad_out * (1.0 - ffn_gate)
    branch_low = grad_branch.astype(jnp.bfloat16)
    grad_w_out = jnp.einsum("tf,td->fd", active, branch_low, preferred_element_type=jnp.float32)
    grad_active = jnp.einsum(
        "td,fd->tf", branch_low, weights[3], preferred_element_type=jnp.float32
    )
    grad_hidden = jnp.where(hidden > 0.0, grad_active, 0.0)
    hidden_low = grad_hidden.astype(jnp.bfloat16)
    grad_w_in = jnp.einsum("td,tf->df", normed_two, hidden_low, preferred_element_type=jnp.float32)
    fgate_low = grad_fgate.astype(jnp.bfloat16)
    grad_w_fgate = jnp.einsum(
        "td,te->de", normed_two, fgate_low, preferred_element_type=jnp.float32
    )
    grad_normed_two = jnp.einsum(
        "tf,df->td", hidden_low, weights[2], preferred_element_type=jnp.float32
    )
    grad_normed_two = grad_normed_two + jnp.einsum(
        "te,de->td", fgate_low, weights[1][1], preferred_element_type=jnp.float32
    )
    grad_gain_two = jnp.sum(grad_normed_two * unit_two, 0)
    grad_shift_two = jnp.sum(grad_normed_two, 0)
    grad_middle = grad_middle + normalize_back(grad_normed_two, unit_two, scale_two, vectors[2])
    grad_attended = grad_middle * attn_gate
    grad_agate = grad_middle * (attended - inputs) * attn_gate * (1.0 - attn_gate)
    grad_inputs = grad_middle * (1.0 - attn_gate)
    attended_low = grad_attended.astype(jnp.bfloat16)
    grad_w_o = jnp.einsum(
        "td,te->de", mixed_heads, attended_low, preferred_element_type=jnp.float32
    )
    grad_mixed = jnp.einsum(
        "te,de->td", attended_low, weights[0][3], preferred_element_type=jnp.float32
    ).astype(jnp.bfloat16)
    triple_grad = attend_back(triple, grad_mixed, log_total, segments, positions)
    grad_w_qkv = jnp.einsum("td,jte->jde", normed, triple_grad, preferred_element_type=jnp.float32)
    agate_low = grad_agate.astype(jnp.bfloat16)
    grad_w_agate = jnp.einsum("td,te->de", normed, agate_low, preferred_element_type=jnp.float32)
    grad_normed = jnp.einsum(
        "jte,jde->td", triple_grad, weights[0][:3], preferred_element_type=jnp.float32
    )
    grad_normed = grad_normed + jnp.einsum(
        "te,de->td", agate_low, weights[1][0], preferred_element_type=jnp.float32
    )
    grad_gain_one = jnp.sum(grad_normed * unit_one, 0)
    grad_shift_one = jnp.sum(grad_normed, 0)
    grad_inputs = grad_inputs + normalize_back(grad_normed, unit_one, scale_one, vectors[0])
    input_grad = grad_inputs.astype(jnp.bfloat16)
    grad_attn = jnp.concatenate([grad_w_qkv, grad_w_o[None]], 0)
    grad_gates = jnp.stack([grad_w_agate, grad_w_fgate])
    grad_vectors = jnp.stack(
        [
            grad_gain_one,
            grad_shift_one,
            grad_gain_two,
            grad_shift_two,
            jnp.sum(grad_agate, 0),
            jnp.sum(grad_fgate, 0),
            jnp.sum(grad_branch, 0),
        ]
    )
    grad_bias = jnp.sum(grad_hidden, 0)
    packed = pack((grad_attn, grad_gates, grad_w_in, grad_w_out, grad_vectors, grad_bias), count)
    reduced = reduce_chunk(jnp.take(packed, order, axis=0), groups)
    owned = unpack(reduced[None], 1)
    local_squares = sum((jnp.sum(element * element) for element in owned))
    grad_norm = jnp.sqrt(sum_all(local_squares, groups))
    factor = jnp.minimum(1.0, clip_norm / (grad_norm + 1e-06))
    states = (
        (attn_weight, attn_m, attn_v),
        (gate_weight, gate_m, gate_v),
        (in_weight, in_m, in_v),
        (out_weight, out_m, out_v),
        (norm_params, norm_m, norm_v),
        (in_bias, bias_m, bias_v),
    )
    step_rates = (learn_rate, learn_rate, learn_rate, learn_rate, vector_rate, vector_rate)
    updated = [
        adam_update(state[0], state[1], state[2], gradient, factor, step_rate)
        for state, gradient, step_rate in zip(states, owned, step_rates)
    ]
    return (
        layer_out,
        input_grad,
        grad_norm,
        updated[0][0],
        updated[0][1],
        updated[0][2],
        updated[1][0],
        updated[1][1],
        updated[1][2],
        updated[2][0],
        updated[2][1],
        updated[2][2],
        updated[3][0],
        updated[3][1],
        updated[3][2],
        updated[4][0],
        updated[4][1],
        updated[4][2],
        updated[5][0],
        updated[5][1],
        updated[5][2],
    )


def solution(mesh):
    return jax.shard_map(
        functools.partial(body, bit_groups(mesh.shape)),
        mesh=mesh,
        in_specs=(
            P(("dp", "inner"), None),
            P(("dp", "inner")),
            P(("dp", "inner")),
            P(("dp", "inner"), None),
            P(None, ("dp", "inner"), None),
            P(None, ("dp", "inner"), None),
            P(None, ("dp", "inner"), None),
            P(None, ("dp", "inner"), None),
            P(None, ("dp", "inner"), None),
            P(None, ("dp", "inner"), None),
            P(("dp", "inner"), None),
            P(("dp", "inner"), None),
            P(("dp", "inner"), None),
            P(("dp", "inner"), None),
            P(("dp", "inner"), None),
            P(("dp", "inner"), None),
            P(None, ("dp", "inner")),
            P(None, ("dp", "inner")),
            P(None, ("dp", "inner")),
            P(("dp", "inner")),
            P(("dp", "inner")),
            P(("dp", "inner")),
        ),
        out_specs=(
            P(("dp", "inner"), None),
            P(("dp", "inner"), None),
            P(),
            P(None, ("dp", "inner"), None),
            P(None, ("dp", "inner"), None),
            P(None, ("dp", "inner"), None),
            P(None, ("dp", "inner"), None),
            P(None, ("dp", "inner"), None),
            P(None, ("dp", "inner"), None),
            P(("dp", "inner"), None),
            P(("dp", "inner"), None),
            P(("dp", "inner"), None),
            P(("dp", "inner"), None),
            P(("dp", "inner"), None),
            P(("dp", "inner"), None),
            P(None, ("dp", "inner")),
            P(None, ("dp", "inner")),
            P(None, ("dp", "inner")),
            P(("dp", "inner")),
            P(("dp", "inner")),
            P(("dp", "inner")),
        ),
        check_vma=False,
    )
```

```python
import functools
import jax
import jax.numpy as jnp
from jax import lax
from jax.experimental import pallas as pl
from jax.experimental.pallas import tpu as pltpu
from jax.sharding import PartitionSpec as P

AXES = ("dp", "inner")
HEADS = 8
HEAD = 64
STEP = 10
LOG2E = 1.4426950408889634
BLOCK = 256


norm_eps = 1e-05
first_decay = 0.9
second_decay = 0.999
adam_eps = 1e-08
learn_rate = 0.05
vector_rate = 0.8
weight_decay = 0.1
clip_norm = 1.0
masked_score = -1e30


def normalize_parts(values, gain_row, bias_row):
    centred = values - jnp.mean(values, -1, keepdims=True)
    spread = jnp.mean(centred * centred, -1, keepdims=True)
    scale_row = lax.rsqrt(spread + norm_eps)
    unit_rows = centred * scale_row
    return (unit_rows * gain_row + bias_row, unit_rows, scale_row)


def normalize_back(grad_rows, unit_rows, scale_row, gain_row):
    grad_unit = grad_rows * gain_row
    return scale_row * (
        grad_unit
        - jnp.mean(grad_unit, -1, keepdims=True)
        - unit_rows * jnp.mean(grad_unit * unit_rows, -1, keepdims=True)
    )


def bit_groups(sizes):
    dp_bits = sizes["dp"].bit_length() - 1
    inner_bits = sizes["inner"].bit_length() - 1
    y_bits = dp_bits // 2
    plane_bits = (inner_bits - 1) + y_bits
    return (1, plane_bits, dp_bits - y_bits)


def swap_with(array, offset, count):
    return lax.ppermute(array, AXES, [(source, source ^ offset) for source in range(count)])


def gather_chunk(shard, groups):
    count = 2 ** sum(groups)
    full = shard[None]
    low_bits = groups[0] + groups[1]
    for first_bit, bits in ((low_bits, groups[2]), (groups[0], groups[1]), (0, groups[0])):
        parts = [full] + [
            swap_with(full, offset << first_bit, count) for offset in range(1, 2**bits)
        ]
        full = jnp.stack(parts, 1)
        full = full.reshape((-1,) + shard.shape)
    return full


def reduce_chunk(blocks, groups):
    count = 2 ** sum(groups)
    first_bit = 0
    current = blocks
    for bits in groups:
        split = current.reshape((-1, 2**bits) + blocks.shape[1:])
        total = split[:, 0].astype(jnp.float32)
        for offset in range(1, 2**bits):
            sent = split[:, offset].astype(jnp.bfloat16)
            total = total + swap_with(sent, offset << first_bit, count).astype(jnp.float32)
        first_bit += bits
        current = total
    return current[0]


def sum_all(value, groups):
    count = 2 ** sum(groups)
    first_bit = 0
    for bits in groups:
        value = sum(
            [value] + [swap_with(value, offset << first_bit, count) for offset in range(1, 2**bits)]
        )
        first_bit += bits
    return value


def pack(arrays, count):
    attn, gate, w_in, w_out, vec, bias = arrays
    width = 512
    step = attn.shape[1] // count
    parts = []
    for matrix in [attn[0], attn[1], attn[2], gate[0], attn[3], gate[1]]:
        parts.append(matrix.reshape(count, step, width))
    for column in range(4):
        parts.append(w_in[:, column * width : (column + 1) * width].reshape(count, step, width))
    parts.append(w_out.reshape(count, 4 * step, width))
    small = jnp.concatenate(
        [vec.reshape(7, count, step).transpose(1, 0, 2).reshape(count, 7 * step), bias.reshape(count, 4 * step)], 1
    )
    small = jnp.pad(small, ((0, 0), (0, width - small.shape[1])))
    parts.append(small[:, None])
    return jnp.concatenate([part.astype(jnp.bfloat16) for part in parts], 1)


def unpack(rows, count):
    width = 512
    step = (rows.shape[1] - 1) // 14
    pieces = [rows[:, step * index : step * (index + 1)].reshape(count * step, width) for index in range(10)]
    attn = jnp.stack([pieces[0], pieces[1], pieces[2], pieces[4]])
    gate = jnp.stack([pieces[3], pieces[5]])
    w_in = jnp.concatenate(pieces[6:10], 1)
    w_out = rows[:, 10 * step : 14 * step].reshape(count * step * 4, width)
    small = rows[:, 14 * step]
    vec = small[:, : 7 * step].reshape(count, 7, step).transpose(1, 0, 2).reshape(7, count * step)
    bias = small[:, 7 * step : 11 * step].reshape(-1)
    return (attn, gate, w_in, w_out, vec, bias)


def mat(a,b,dims):
    return lax.dot_general(a,b,(dims,((),())),preferred_element_type=jnp.float32)

def fill_bias(bias_ref, seg_col, pos_col, seg_row, pos_row):
    rows=bias_ref.shape[0]
    step=min(BLOCK,rows)
    for first in range(0,rows,step):
        sc=seg_col[first:first+step,:]; pc=pos_col[first:first+step,:]
        sr=seg_row[:,first:]; pr=pos_row[:,first:]
        allowed=(sc==sr)&(pc<=pr)
        bias_ref[first:first+step,first:]=jnp.where(allowed,0.0,masked_score)

def head_lanes(shape, which):
    lane=lax.broadcasted_iota(jnp.int32,shape,1)
    return (lane//HEAD)==which

def attn_fwd_kernel(segc,posc,segr,posr,q_ref,k_ref,v_ref,o_ref,lse_ref,bias_ref):
    @pl.when(pl.program_id(0)==0)
    def _():
        fill_bias(bias_ref,segc,posc,segr,posr)
    rows=q_ref.shape[0]; step=min(BLOCK,rows)
    pair=q_ref.shape[1]//HEAD
    const=HEAD**-0.5*LOG2E
    for first in range(0,rows,step):
        keys=first+step
        q=q_ref[first:keys,:]
        mixed=None
        for which in range(pair):
            own=head_lanes(q.shape,which)
            qh=jnp.where(own,q,jnp.zeros_like(q))
            s=mat(k_ref[:keys,:],qh,((1,),(1,)))*const+bias_ref[:keys,first:keys]
            m=jnp.max(s,0,keepdims=True)
            w=jnp.exp2(s-m)
            total=jnp.sum(w,0,keepdims=True)
            p=(w*(1.0/total)).astype(jnp.bfloat16)
            o=mat(p,v_ref[:keys,:],((0,),(0,)))
            mixed=o if mixed is None else jnp.where(own,o,mixed)
            lse_ref[0,which:which+1,first:keys]=m+jnp.log2(total)
        o_ref[first:keys,:]=mixed.astype(jnp.bfloat16)

def attn_bwd_kernel(segc,posc,segr,posr,q_ref,k_ref,v_ref,do_ref,lse_ref,dq_ref,dk_ref,dv_ref,bias_ref,dk_acc,dv_acc):
    @pl.when(pl.program_id(0)==0)
    def _():
        fill_bias(bias_ref,segc,posc,segr,posr)
    rows=q_ref.shape[0]; step=min(BLOCK,rows)
    pair=q_ref.shape[1]//HEAD
    const=HEAD**-0.5*LOG2E
    scale=HEAD**-0.5
    dk_acc[...]=jnp.zeros_like(dk_acc); dv_acc[...]=jnp.zeros_like(dv_acc)
    for first in range(0,rows,step):
        keys=first+step
        q=q_ref[first:keys,:]; do=do_ref[first:keys,:]
        dq=None
        for which in range(pair):
            own=head_lanes(q.shape,which)
            qh=jnp.where(own,q,jnp.zeros_like(q))
            doh=jnp.where(own,do,jnp.zeros_like(do))
            s=mat(k_ref[:keys,:],qh,((1,),(1,)))
            p=jnp.exp2(s*const+(bias_ref[:keys,first:keys]-lse_ref[0,which:which+1,first:keys]))
            dp=mat(v_ref[:keys,:],doh,((1,),(1,)))
            inner=jnp.sum(p*dp,0,keepdims=True)
            ds=(p*(dp-inner)).astype(jnp.bfloat16)
            dv_acc[:keys,:]+=mat(p.astype(jnp.bfloat16),doh,((1,),(0,)))
            dk_acc[:keys,:]+=mat(ds,qh,((1,),(0,)))
            d=mat(ds,k_ref[:keys,:],((0,),(0,)))
            dq=d if dq is None else jnp.where(own,d,dq)
        dq_ref[first:keys,:]=(dq*scale).astype(jnp.bfloat16)
    dk_ref[...]=(dk_acc[...]*scale).astype(jnp.bfloat16)
    dv_ref[...]=dv_acc[...].astype(jnp.bfloat16)

def const_map(*_): return (0,0)

def seg_args(segments,positions):
    return (segments[:,None],positions[:,None],segments[None],positions[None])

def attend(q,k,v,segments,positions):
    rows,width=q.shape
    pairs=width//128
    blk=pl.BlockSpec((rows,128),lambda j:(0,j))
    col=pl.BlockSpec((rows,1),const_map); row=pl.BlockSpec((1,rows),const_map)
    return pl.pallas_call(attn_fwd_kernel,grid=(pairs,),
        in_specs=[col,col,row,row,blk,blk,blk],
        out_specs=[blk,pl.BlockSpec((1,2,rows),lambda j:(j,0,0))],
        out_shape=[jax.ShapeDtypeStruct((rows,width),jnp.bfloat16),jax.ShapeDtypeStruct((pairs,2,rows),jnp.float32)],
        scratch_shapes=[pltpu.VMEM((rows,rows),jnp.float32)],
        name="attn_fwd",
    )(*seg_args(segments,positions),q,k,v)

def attend_back(q,k,v,do,lse,segments,positions):
    rows,width=q.shape
    pairs=width//128
    blk=pl.BlockSpec((rows,128),lambda j:(0,j))
    col=pl.BlockSpec((rows,1),const_map); row=pl.BlockSpec((1,rows),const_map)
    out=jax.ShapeDtypeStruct((rows,width),jnp.bfloat16)
    return pl.pallas_call(attn_bwd_kernel,grid=(pairs,),
        in_specs=[col,col,row,row,blk,blk,blk,blk,pl.BlockSpec((1,2,rows),lambda j:(j,0,0))],
        out_specs=[blk,blk,blk],
        out_shape=[out,out,out],
        scratch_shapes=[pltpu.VMEM((rows,rows),jnp.float32),pltpu.VMEM((rows,128),jnp.float32),pltpu.VMEM((rows,128),jnp.float32)],
        name="attn_bwd",
    )(*seg_args(segments,positions),q,k,v,do,lse)


def attn_branch(weights, normed, segments, positions):
    triple = jnp.einsum(
        "td,jde->jte", normed, weights[0][:3], preferred_element_type=jnp.float32
    ).astype(jnp.bfloat16)
    mixed_heads, log_total = attend(triple[0], triple[1], triple[2], segments, positions)
    attended = jnp.dot(mixed_heads, weights[0][3], preferred_element_type=jnp.float32)
    return (triple, mixed_heads, log_total, attended)


def ffn_branch(weights, normed_two):
    hidden = jnp.dot(normed_two, weights[2], preferred_element_type=jnp.float32) + weights[
        5
    ].astype(jnp.float32)
    active = jnp.maximum(hidden, 0.0).astype(jnp.bfloat16)
    branch = jnp.dot(active, weights[3], preferred_element_type=jnp.float32) + weights[4][6].astype(
        jnp.float32
    )
    return (hidden, active, branch)


def adam_update(weight, first_moment, second_moment, gradient, factor, step_rate):
    clipped = gradient * factor
    first_new = first_decay * first_moment + (1.0 - first_decay) * clipped
    second_new = second_decay * second_moment + (1.0 - second_decay) * clipped * clipped
    corrected = first_new / (1.0 - first_decay**STEP)
    spread = second_new / (1.0 - second_decay**STEP)
    weight_new = weight - step_rate * (
        corrected / (jnp.sqrt(spread) + adam_eps) + weight_decay * weight
    )
    return (weight_new, first_new, second_new)


def body(
    groups,
    tokens,
    segments,
    positions,
    cotangent,
    attn_weight,
    attn_m,
    attn_v,
    gate_weight,
    gate_m,
    gate_v,
    in_weight,
    in_m,
    in_v,
    out_weight,
    out_m,
    out_v,
    norm_params,
    norm_m,
    norm_v,
    in_bias,
    bias_m,
    bias_v,
):
    shards = (attn_weight, gate_weight, in_weight, out_weight, norm_params, in_bias)
    count = 2 ** sum(groups)
    own = lax.axis_index(AXES)
    order = jnp.arange(count) ^ own
    shard_rows = pack(shards, 1)[0]
    gathered = gather_chunk(shard_rows, groups)
    weights = unpack(jnp.take(gathered, order, axis=0), count)
    vectors = weights[4].astype(jnp.float32)
    inputs = tokens.astype(jnp.float32)
    normed_full, unit_one, scale_one = normalize_parts(inputs, vectors[0], vectors[1])
    normed = normed_full.astype(jnp.bfloat16)
    triple, mixed_heads, log_total, attended = attn_branch(weights, normed, segments, positions)
    attn_gate = jax.nn.sigmoid(
        jnp.dot(normed, weights[1][0], preferred_element_type=jnp.float32) + vectors[4]
    )
    middle = attn_gate * attended + (1.0 - attn_gate) * inputs
    normed_two_full, unit_two, scale_two = normalize_parts(middle, vectors[2], vectors[3])
    normed_two = normed_two_full.astype(jnp.bfloat16)
    hidden, active, branch = ffn_branch(weights, normed_two)
    ffn_gate = jax.nn.sigmoid(
        jnp.dot(normed_two, weights[1][1], preferred_element_type=jnp.float32) + vectors[5]
    )
    layer_out = (ffn_gate * branch + (1.0 - ffn_gate) * middle).astype(jnp.bfloat16)
    grad_out = cotangent.astype(jnp.float32)
    grad_branch = grad_out * ffn_gate
    grad_fgate = grad_out * (branch - middle) * ffn_gate * (1.0 - ffn_gate)
    grad_middle = grad_out * (1.0 - ffn_gate)
    branch_low = grad_branch.astype(jnp.bfloat16)
    grad_w_out = jnp.einsum("tf,td->fd", active, branch_low, preferred_element_type=jnp.float32)
    grad_active = jnp.einsum(
        "td,fd->tf", branch_low, weights[3], preferred_element_type=jnp.float32
    )
    grad_hidden = jnp.where(hidden > 0.0, grad_active, 0.0)
    hidden_low = grad_hidden.astype(jnp.bfloat16)
    grad_w_in = jnp.einsum("td,tf->df", normed_two, hidden_low, preferred_element_type=jnp.float32)
    fgate_low = grad_fgate.astype(jnp.bfloat16)
    grad_w_fgate = jnp.einsum(
        "td,te->de", normed_two, fgate_low, preferred_element_type=jnp.float32
    )
    grad_normed_two = jnp.einsum(
        "tf,df->td", hidden_low, weights[2], preferred_element_type=jnp.float32
    )
    grad_normed_two = grad_normed_two + jnp.einsum(
        "te,de->td", fgate_low, weights[1][1], preferred_element_type=jnp.float32
    )
    grad_gain_two = jnp.sum(grad_normed_two * unit_two, 0)
    grad_shift_two = jnp.sum(grad_normed_two, 0)
    grad_middle = grad_middle + normalize_back(grad_normed_two, unit_two, scale_two, vectors[2])
    grad_attended = grad_middle * attn_gate
    grad_agate = grad_middle * (attended - inputs) * attn_gate * (1.0 - attn_gate)
    grad_inputs = grad_middle * (1.0 - attn_gate)
    attended_low = grad_attended.astype(jnp.bfloat16)
    grad_w_o = jnp.einsum(
        "td,te->de", mixed_heads, attended_low, preferred_element_type=jnp.float32
    )
    grad_mixed = jnp.einsum(
        "te,de->td", attended_low, weights[0][3], preferred_element_type=jnp.float32
    ).astype(jnp.bfloat16)
    triple_grad = jnp.stack(
        attend_back(triple[0], triple[1], triple[2], grad_mixed, log_total, segments, positions)
    )
    grad_w_qkv = jnp.einsum("td,jte->jde", normed, triple_grad, preferred_element_type=jnp.float32)
    agate_low = grad_agate.astype(jnp.bfloat16)
    grad_w_agate = jnp.einsum("td,te->de", normed, agate_low, preferred_element_type=jnp.float32)
    grad_normed = jnp.einsum(
        "jte,jde->td", triple_grad, weights[0][:3], preferred_element_type=jnp.float32
    )
    grad_normed = grad_normed + jnp.einsum(
        "te,de->td", agate_low, weights[1][0], preferred_element_type=jnp.float32
    )
    grad_gain_one = jnp.sum(grad_normed * unit_one, 0)
    grad_shift_one = jnp.sum(grad_normed, 0)
    grad_inputs = grad_inputs + normalize_back(grad_normed, unit_one, scale_one, vectors[0])
    input_grad = grad_inputs.astype(jnp.bfloat16)
    grad_attn = jnp.concatenate([grad_w_qkv, grad_w_o[None]], 0)
    grad_gates = jnp.stack([grad_w_agate, grad_w_fgate])
    grad_vectors = jnp.stack(
        [
            grad_gain_one,
            grad_shift_one,
            grad_gain_two,
            grad_shift_two,
            jnp.sum(grad_agate, 0),
            jnp.sum(grad_fgate, 0),
            jnp.sum(grad_branch, 0),
        ]
    )
    grad_bias = jnp.sum(grad_hidden, 0)
    packed = pack((grad_attn, grad_gates, grad_w_in, grad_w_out, grad_vectors, grad_bias), count)
    reduced = reduce_chunk(jnp.take(packed, order, axis=0), groups)
    owned = unpack(reduced[None], 1)
    local_squares = sum((jnp.sum(element * element) for element in owned))
    grad_norm = jnp.sqrt(sum_all(local_squares, groups))
    factor = jnp.minimum(1.0, clip_norm / (grad_norm + 1e-06))
    states = (
        (attn_weight, attn_m, attn_v),
        (gate_weight, gate_m, gate_v),
        (in_weight, in_m, in_v),
        (out_weight, out_m, out_v),
        (norm_params, norm_m, norm_v),
        (in_bias, bias_m, bias_v),
    )
    step_rates = (learn_rate, learn_rate, learn_rate, learn_rate, vector_rate, vector_rate)
    updated = [
        adam_update(state[0], state[1], state[2], gradient, factor, step_rate)
        for state, gradient, step_rate in zip(states, owned, step_rates)
    ]
    return (
        layer_out,
        input_grad,
        grad_norm,
        updated[0][0],
        updated[0][1],
        updated[0][2],
        updated[1][0],
        updated[1][1],
        updated[1][2],
        updated[2][0],
        updated[2][1],
        updated[2][2],
        updated[3][0],
        updated[3][1],
        updated[3][2],
        updated[4][0],
        updated[4][1],
        updated[4][2],
        updated[5][0],
        updated[5][1],
        updated[5][2],
    )


def solution(mesh):
    return jax.shard_map(
        functools.partial(body, bit_groups(mesh.shape)),
        mesh=mesh,
        in_specs=(
            P(("dp", "inner"), None),
            P(("dp", "inner")),
            P(("dp", "inner")),
            P(("dp", "inner"), None),
            P(None, ("dp", "inner"), None),
            P(None, ("dp", "inner"), None),
            P(None, ("dp", "inner"), None),
            P(None, ("dp", "inner"), None),
            P(None, ("dp", "inner"), None),
            P(None, ("dp", "inner"), None),
            P(("dp", "inner"), None),
            P(("dp", "inner"), None),
            P(("dp", "inner"), None),
            P(("dp", "inner"), None),
            P(("dp", "inner"), None),
            P(("dp", "inner"), None),
            P(None, ("dp", "inner")),
            P(None, ("dp", "inner")),
            P(None, ("dp", "inner")),
            P(("dp", "inner")),
            P(("dp", "inner")),
            P(("dp", "inner")),
        ),
        out_specs=(
            P(("dp", "inner"), None),
            P(("dp", "inner"), None),
            P(),
            P(None, ("dp", "inner"), None),
            P(None, ("dp", "inner"), None),
            P(None, ("dp", "inner"), None),
            P(None, ("dp", "inner"), None),
            P(None, ("dp", "inner"), None),
            P(None, ("dp", "inner"), None),
            P(("dp", "inner"), None),
            P(("dp", "inner"), None),
            P(("dp", "inner"), None),
            P(("dp", "inner"), None),
            P(("dp", "inner"), None),
            P(("dp", "inner"), None),
            P(None, ("dp", "inner")),
            P(None, ("dp", "inner")),
            P(None, ("dp", "inner")),
            P(("dp", "inner")),
            P(("dp", "inner")),
            P(("dp", "inner")),
        ),
        check_vma=False,
    )
```

```python
import functools
import jax
import jax.numpy as jnp
from jax import lax
from jax.experimental import pallas as pl
from jax.experimental.pallas import tpu as pltpu
from jax.sharding import PartitionSpec as P

AXES = ("dp", "inner")
HEADS = 8
HEAD = 64
STEP = 10
LOG2E = 1.4426950408889634
BLOCK = 256


norm_eps = 1e-05
first_decay = 0.9
second_decay = 0.999
adam_eps = 1e-08
learn_rate = 0.05
vector_rate = 0.8
weight_decay = 0.1
clip_norm = 1.0
masked_score = -1e30


def normalize_parts(values, gain_row, bias_row):
    centred = values - jnp.mean(values, -1, keepdims=True)
    spread = jnp.mean(centred * centred, -1, keepdims=True)
    scale_row = lax.rsqrt(spread + norm_eps)
    unit_rows = centred * scale_row
    return (unit_rows * gain_row + bias_row, unit_rows, scale_row)


def normalize_back(grad_rows, unit_rows, scale_row, gain_row):
    grad_unit = grad_rows * gain_row
    return scale_row * (
        grad_unit
        - jnp.mean(grad_unit, -1, keepdims=True)
        - unit_rows * jnp.mean(grad_unit * unit_rows, -1, keepdims=True)
    )


def bit_groups(sizes):
    dp_bits = sizes["dp"].bit_length() - 1
    inner_bits = sizes["inner"].bit_length() - 1
    y_bits = dp_bits // 2
    plane_bits = (inner_bits - 1) + y_bits
    return (1, plane_bits, dp_bits - y_bits)


def swap_with(array, offset, count):
    return lax.ppermute(array, AXES, [(source, source ^ offset) for source in range(count)])


def stage_bits(groups):
    return ((0, groups[0]), (groups[0], groups[1]), (groups[0] + groups[1], groups[2]))


def gather_z(shard, groups):
    count = 2 ** sum(groups)
    first_bit, bits = stage_bits(groups)[2]
    return jnp.stack([shard] + [swap_with(shard, offset << first_bit, count) for offset in range(1, 2**bits)])


def gather_plane(column, groups):
    count = 2 ** sum(groups)
    first_bit, bits = stage_bits(groups)[1]
    return [swap_with(column, offset << first_bit, count) for offset in range(1, 2**bits)]


def gather_core(column, planes, groups):
    return swap_with(jnp.concatenate([column] + planes), 1, 2 ** sum(groups))


def offsets_of(groups):
    (_, _), (plane_bit, plane_bits), (z_bit, z_bits) = stage_bits(groups)
    table = [
        [(plane << plane_bit) | (z << z_bit) for z in range(2**z_bits)] for plane in range(2**plane_bits)
    ]
    return table + [[offset | 1 for row in table for offset in row]]


def any_spec():
    return pl.BlockSpec(memory_space=pl.ANY)


def place_kernel(offsets, layout, own_ref, *refs):
    parts = refs[: len(offsets)]
    outs = refs[len(offsets) : len(offsets) + len(layout)]
    sems = refs[-1]
    own = own_ref[0]
    for part, row in zip(parts, offsets):
        for entry, offset in enumerate(row):
            owner = own ^ offset
            for index, (first, pieces) in enumerate(layout):
                pltpu.make_async_copy(
                    part.at[entry, first : first + pieces], outs[index].at[:, owner], sems.at[index]
                ).start()
    for index in range(len(layout)):
        pltpu.make_async_copy(outs[index], outs[index], sems.at[index]).wait()


def place(own, parts, layout, groups):
    count = 2 ** sum(groups)
    step, width = parts[0].shape[2:]
    offsets = offsets_of(groups)
    if step % 16:
        order = jnp.argsort(jnp.array([o for row in offsets for o in row]) ^ own)
        full = jnp.moveaxis(jnp.concatenate(parts)[order], 0, 1)
        return [full[first : first + pieces] for first, pieces in layout]
    return pl.pallas_call(
        functools.partial(place_kernel, offsets, layout),
        in_specs=[pl.BlockSpec(memory_space=pltpu.SMEM)] + [any_spec() for _ in parts],
        out_specs=[any_spec() for _ in layout],
        out_shape=[jax.ShapeDtypeStruct((pieces, count, step, width), jnp.bfloat16) for _, pieces in layout],
        scratch_shapes=[pltpu.SemaphoreType.DMA((len(layout),))],
        name="place",
    )(own[None].astype(jnp.int32), *parts)


def split_kernel(offsets, layout, own_ref, *refs):
    ins = refs[: len(layout)]
    kept, sent, sems = refs[len(layout) :]
    own = own_ref[0]
    for entry, offset in enumerate(offsets):
        for side, target in enumerate((kept, sent)):
            owner = own ^ (offset | side)
            for index, (first, pieces) in enumerate(layout):
                pltpu.make_async_copy(
                    ins[index].at[:, owner], target.at[entry, first : first + pieces], sems.at[side]
                ).start()
    pltpu.make_async_copy(kept, kept, sems.at[0]).wait()
    pltpu.make_async_copy(sent, sent, sems.at[1]).wait()


def split(own, grads, groups):
    step, width = grads[0].shape[2:]
    layout = []
    first = 0
    for grad in grads:
        layout.append((first, grad.shape[0]))
        first += grad.shape[0]
    offsets = [offset for row in offsets_of(groups)[:-1] for offset in row]
    if step % 16:
        full = jnp.moveaxis(jnp.concatenate(grads), 1, 0)
        order = jnp.array(offsets) ^ own
        return full[order], full[order ^ 1]
    shape = jax.ShapeDtypeStruct((len(offsets), first, step, width), jnp.bfloat16)
    return pl.pallas_call(
        functools.partial(split_kernel, offsets, layout),
        in_specs=[pl.BlockSpec(memory_space=pltpu.SMEM)] + [any_spec() for _ in grads],
        out_specs=[any_spec(), any_spec()],
        out_shape=[shape, shape],
        scratch_shapes=[pltpu.SemaphoreType.DMA((2,))],
        name="split",
    )(own[None].astype(jnp.int32), *grads)


def reduce_plane(kept, received, groups):
    count = 2 ** sum(groups)
    _, (first_bit, bits), (_, z_bits) = stage_bits(groups)
    shape = (2**bits, 2**z_bits) + kept.shape[1:]
    kept = kept.reshape(shape)
    received = received.reshape(shape)
    total = lambda offset: kept[offset].astype(jnp.float32) + received[offset].astype(jnp.float32)
    arrived = [
        swap_with(total(offset).astype(jnp.bfloat16), offset << first_bit, count) for offset in range(1, 2**bits)
    ]
    return total(0), arrived


def reduce_z(own_part, arrived, groups):
    count = 2 ** sum(groups)
    first_bit, bits = stage_bits(groups)[2]
    total = lambda z: own_part[z] + sum(part[z].astype(jnp.float32) for part in arrived)
    return total(0), [
        swap_with(total(z).astype(jnp.bfloat16), z << first_bit, count) for z in range(1, 2**bits)
    ]


def reduce_end(own_part, arrived):
    return own_part + sum(part.astype(jnp.float32) for part in arrived)


def sum_all(value, groups):
    for bit in range(sum(groups)):
        value = value + swap_with(value, 1 << bit, 2 ** sum(groups))
    return value


def tie(*values):
    return lax.optimization_barrier(values)


def small_rows(vec, bias, count, width):
    step = vec.shape[1] // count
    rows = jnp.concatenate(
        [vec.reshape(7, count, step).transpose(1, 0, 2).reshape(count, 7 * step), bias.reshape(count, 4 * step)], 1
    ).astype(jnp.bfloat16)
    return jnp.pad(rows, ((0, 0), (0, width - rows.shape[1])))


def small_back(rows, step):
    count = rows.shape[0]
    vec = rows[:, : 7 * step].reshape(count, 7, step).transpose(1, 0, 2).reshape(7, count * step)
    return vec, rows[:, 7 * step : 11 * step].reshape(-1)


def mat(a,b,dims):
    return lax.dot_general(a,b,(dims,((),())),preferred_element_type=jnp.float32)

def fill_bias(bias_ref, seg_col, pos_col, seg_row, pos_row):
    rows=bias_ref.shape[0]
    step=min(BLOCK,rows)
    for first in range(0,rows,step):
        sc=seg_col[first:first+step,:]; pc=pos_col[first:first+step,:]
        sr=seg_row[:,first:]; pr=pos_row[:,first:]
        allowed=(sc==sr)&(pc<=pr)
        bias_ref[first:first+step,first:]=jnp.where(allowed,0.0,masked_score)

def head_lanes(shape, which):
    lane=lax.broadcasted_iota(jnp.int32,shape,1)
    return (lane//HEAD)==which

def attn_fwd_kernel(segc,posc,segr,posr,q_ref,k_ref,v_ref,o_ref,lse_ref,bias_ref):
    @pl.when(pl.program_id(0)==0)
    def _():
        fill_bias(bias_ref,segc,posc,segr,posr)
    rows=q_ref.shape[0]; step=min(BLOCK,rows)
    pair=q_ref.shape[1]//HEAD
    const=HEAD**-0.5*LOG2E
    for first in range(0,rows,step):
        keys=first+step
        q=q_ref[first:keys,:]
        mixed=None
        for which in range(pair):
            own=head_lanes(q.shape,which)
            qh=jnp.where(own,q,jnp.zeros_like(q))
            s=mat(k_ref[:keys,:],qh,((1,),(1,)))*const+bias_ref[:keys,first:keys]
            m=jnp.max(s,0,keepdims=True)
            w=jnp.exp2(s-m)
            total=jnp.sum(w,0,keepdims=True)
            p=(w*(1.0/total)).astype(jnp.bfloat16)
            o=mat(p,v_ref[:keys,:],((0,),(0,)))
            mixed=o if mixed is None else jnp.where(own,o,mixed)
            lse_ref[0,which:which+1,first:keys]=m+jnp.log2(total)
        o_ref[first:keys,:]=mixed.astype(jnp.bfloat16)

def attn_bwd_kernel(segc,posc,segr,posr,q_ref,k_ref,v_ref,do_ref,lse_ref,dq_ref,dk_ref,dv_ref,bias_ref,dk_acc,dv_acc):
    @pl.when(pl.program_id(0)==0)
    def _():
        fill_bias(bias_ref,segc,posc,segr,posr)
    rows=q_ref.shape[0]; step=min(BLOCK,rows)
    pair=q_ref.shape[1]//HEAD
    const=HEAD**-0.5*LOG2E
    scale=HEAD**-0.5
    dk_acc[...]=jnp.zeros_like(dk_acc); dv_acc[...]=jnp.zeros_like(dv_acc)
    for first in range(0,rows,step):
        keys=first+step
        q=q_ref[first:keys,:]; do=do_ref[first:keys,:]
        dq=None
        for which in range(pair):
            own=head_lanes(q.shape,which)
            qh=jnp.where(own,q,jnp.zeros_like(q))
            doh=jnp.where(own,do,jnp.zeros_like(do))
            s=mat(k_ref[:keys,:],qh,((1,),(1,)))
            p=jnp.exp2(s*const+(bias_ref[:keys,first:keys]-lse_ref[0,which:which+1,first:keys]))
            dp=mat(v_ref[:keys,:],doh,((1,),(1,)))
            inner=jnp.sum(p*dp,0,keepdims=True)
            ds=(p*(dp-inner)).astype(jnp.bfloat16)
            dv_acc[:keys,:]+=mat(p.astype(jnp.bfloat16),doh,((1,),(0,)))
            dk_acc[:keys,:]+=mat(ds,qh,((1,),(0,)))
            d=mat(ds,k_ref[:keys,:],((0,),(0,)))
            dq=d if dq is None else jnp.where(own,d,dq)
        dq_ref[first:keys,:]=(dq*scale).astype(jnp.bfloat16)
    dk_ref[...]=(dk_acc[...]*scale).astype(jnp.bfloat16)
    dv_ref[...]=dv_acc[...].astype(jnp.bfloat16)

def const_map(*_): return (0,0)

def seg_args(segments,positions):
    return (segments[:,None],positions[:,None],segments[None],positions[None])

def attend(q,k,v,segments,positions):
    rows,width=q.shape
    pairs=width//128
    blk=pl.BlockSpec((rows,128),lambda j:(0,j))
    col=pl.BlockSpec((rows,1),const_map); row=pl.BlockSpec((1,rows),const_map)
    return pl.pallas_call(attn_fwd_kernel,grid=(pairs,),
        in_specs=[col,col,row,row,blk,blk,blk],
        out_specs=[blk,pl.BlockSpec((1,2,rows),lambda j:(j,0,0))],
        out_shape=[jax.ShapeDtypeStruct((rows,width),jnp.bfloat16),jax.ShapeDtypeStruct((pairs,2,rows),jnp.float32)],
        scratch_shapes=[pltpu.VMEM((rows,rows),jnp.float32)],
        name="attn_fwd",
    )(*seg_args(segments,positions),q,k,v)

def attend_back(q,k,v,do,lse,segments,positions,base,pairs):
    rows=q.shape[0]
    blk=pl.BlockSpec((rows,128),lambda j:(0,j+base))
    oblk=pl.BlockSpec((rows,128),lambda j:(0,j))
    col=pl.BlockSpec((rows,1),const_map); row=pl.BlockSpec((1,rows),const_map)
    out=jax.ShapeDtypeStruct((rows,128*pairs),jnp.bfloat16)
    return pl.pallas_call(attn_bwd_kernel,grid=(pairs,),
        in_specs=[col,col,row,row,blk,blk,blk,blk,pl.BlockSpec((1,2,rows),lambda j:(j+base,0,0))],
        out_specs=[oblk,oblk,oblk],
        out_shape=[out,out,out],
        scratch_shapes=[pltpu.VMEM((rows,rows),jnp.float32),pltpu.VMEM((rows,128),jnp.float32),pltpu.VMEM((rows,128),jnp.float32)],
        name="attn_bwd",
    )(*seg_args(segments,positions),q,k,v,do,lse)


def adam_update(weight, first_moment, second_moment, gradient, factor, step_rate):
    clipped = gradient * factor
    first_new = first_decay * first_moment + (1.0 - first_decay) * clipped
    second_new = second_decay * second_moment + (1.0 - second_decay) * clipped * clipped
    corrected = first_new / (1.0 - first_decay**STEP)
    spread = second_new / (1.0 - second_decay**STEP)
    weight_new = weight - step_rate * (
        corrected / (jnp.sqrt(spread) + adam_eps) + weight_decay * weight
    )
    return (weight_new, first_new, second_new)


def body(
    groups,
    tokens,
    segments,
    positions,
    cotangent,
    attn_weight,
    attn_m,
    attn_v,
    gate_weight,
    gate_m,
    gate_v,
    in_weight,
    in_m,
    in_v,
    out_weight,
    out_m,
    out_v,
    norm_params,
    norm_m,
    norm_v,
    in_bias,
    bias_m,
    bias_v,
):
    count = 2 ** sum(groups)
    own = lax.axis_index(AXES)
    width = 512
    step = attn_weight.shape[1]
    low = lambda value: value.astype(jnp.bfloat16)
    dot = functools.partial(jnp.einsum, preferred_element_type=jnp.float32)
    columns = lambda value: [value[:, width * j : width * (j + 1)] for j in range(4)]
    small = jnp.pad(small_rows(norm_params, in_bias, 1, width), ((0, step - 1), (0, 0)))
    first_shard = jnp.stack(
        [low(attn_weight[0]), low(attn_weight[1]), low(attn_weight[2]), low(gate_weight[0]), low(attn_weight[3]), small]
    )
    second_shard = jnp.concatenate(
        [
            jnp.stack([low(gate_weight[1])] + columns(low(in_weight))),
            low(out_weight).reshape(4, step, width),
        ]
    )
    z_first = gather_z(first_shard, groups)
    z_first, second_shard = tie(z_first, second_shard)
    plane_first = gather_plane(z_first, groups)
    z_second = gather_z(second_shard, groups)
    z_second, *plane_first = tie(z_second, *plane_first)
    core_first = gather_core(z_first, plane_first, groups)
    plane_second = gather_plane(z_second, groups)
    w_four, w_o, small_all = place(
        own, [z_first] + plane_first + [core_first], [(0, 4), (4, 1), (5, 1)], groups
    )
    w_four = w_four.reshape(4, count * step, width)
    w_o = w_o.reshape(count * step, width)
    vectors, bias = small_back(small_all[0, :, 0].astype(jnp.float32), step)
    inputs = tokens.astype(jnp.float32)
    normed_full, unit_one, scale_one = normalize_parts(inputs, vectors[0], vectors[1])
    normed = low(normed_full)
    queries, keys, values = [low(dot("td,de->te", normed, w_four[j])) for j in range(3)]
    mixed_heads, log_total = attend(queries, keys, values, segments, positions)
    mixed_heads, *plane_second = tie(mixed_heads, *plane_second)
    core_second = gather_core(z_second, plane_second, groups)
    attended = dot("td,de->te", mixed_heads, w_o)
    attn_gate = jax.nn.sigmoid(dot("td,de->te", normed, w_four[3]) + vectors[4])
    middle = attn_gate * attended + (1.0 - attn_gate) * inputs
    normed_two_full, unit_two, scale_two = normalize_parts(middle, vectors[2], vectors[3])
    normed_two = low(normed_two_full)
    w_f, w_in, w_out = place(
        own, [z_second] + plane_second + [core_second], [(0, 1), (1, 4), (5, 4)], groups
    )
    w_f = w_f.reshape(count * step, width)
    w_in = jnp.concatenate(list(w_in.reshape(4, count * step, width)), 1)
    w_out = w_out.transpose(1, 0, 2, 3).reshape(4 * count * step, width)
    hidden = dot("td,df->tf", normed_two, w_in) + bias
    active = low(jnp.maximum(hidden, 0.0))
    branch = dot("tf,fd->td", active, w_out) + vectors[6]
    ffn_gate = jax.nn.sigmoid(dot("td,de->te", normed_two, w_f) + vectors[5])
    layer_out = low(ffn_gate * branch + (1.0 - ffn_gate) * middle)
    grad_out = cotangent.astype(jnp.float32)
    grad_branch = grad_out * ffn_gate
    grad_fgate = grad_out * (branch - middle) * ffn_gate * (1.0 - ffn_gate)
    grad_middle = grad_out * (1.0 - ffn_gate)
    branch_low = low(grad_branch)
    grad_w_out = low(dot("tf,td->fd", active, branch_low))
    grad_active = dot("td,fd->tf", branch_low, w_out)
    grad_hidden = jnp.where(hidden > 0.0, grad_active, 0.0)
    hidden_low = low(grad_hidden)
    grad_w_in = low(dot("td,tf->df", normed_two, hidden_low))
    fgate_low = low(grad_fgate)
    grad_w_f = low(dot("td,te->de", normed_two, fgate_low))
    grad_normed_two = dot("tf,df->td", hidden_low, w_in) + dot("te,de->td", fgate_low, w_f)
    grad_gain_two = jnp.sum(grad_normed_two * unit_two, 0)
    grad_shift_two = jnp.sum(grad_normed_two, 0)
    grad_middle = grad_middle + normalize_back(grad_normed_two, unit_two, scale_two, vectors[2])
    grad_attended = grad_middle * attn_gate
    grad_agate = grad_middle * (attended - inputs) * attn_gate * (1.0 - attn_gate)
    grad_inputs = grad_middle * (1.0 - attn_gate)
    attended_low = low(grad_attended)
    grad_w_o = low(dot("td,te->de", mixed_heads, attended_low))
    grad_mixed = low(dot("te,de->td", attended_low, w_o))
    blocks = lambda value: value.reshape(-1, count, step, width)
    kept_b, sent_b = split(
        own,
        [
            blocks(grad_w_f),
            blocks(jnp.stack(columns(grad_w_in))),
            grad_w_out.reshape(count, 4, step, width).transpose(1, 0, 2, 3),
            blocks(grad_w_o),
        ],
        groups,
    )
    core_b = swap_with(sent_b, 1, count)
    half_one = attend_back(queries, keys, values, grad_mixed, log_total, segments, positions, 0, 2)
    core_b, kept_b, *half_one = tie(core_b, kept_b, *half_one)
    own_b, plane_b = reduce_plane(kept_b, core_b, groups)
    half_two = attend_back(queries, keys, values, grad_mixed, log_total, segments, positions, 2, 2)
    triple_grad = [jnp.concatenate([one, two], 1) for one, two in zip(half_one, half_two)]
    agate_low = low(grad_agate)
    back_four = triple_grad + [agate_low]
    grad_normed = sum(dot("te,de->td", back_four[j], w_four[j]) for j in range(4))
    grad_w_four = jnp.stack([low(dot("td,te->de", normed, back_four[j])) for j in range(4)])
    grad_gain_one = jnp.sum(grad_normed * unit_one, 0)
    grad_shift_one = jnp.sum(grad_normed, 0)
    grad_inputs = grad_inputs + normalize_back(grad_normed, unit_one, scale_one, vectors[0])
    input_grad = low(grad_inputs)
    grad_vectors = jnp.stack(
        [
            grad_gain_one,
            grad_shift_one,
            grad_gain_two,
            grad_shift_two,
            jnp.sum(grad_agate, 0),
            jnp.sum(grad_fgate, 0),
            jnp.sum(grad_branch, 0),
        ]
    )
    grad_bias = jnp.sum(grad_hidden, 0)
    grad_small = jnp.pad(small_rows(grad_vectors, grad_bias, count, width)[:, None], ((0, 0), (0, step - 1), (0, 0)))
    kept_a, sent_a = split(own, [blocks(grad_w_four), grad_small[None]], groups)
    kept_a, sent_a, *plane_b = tie(kept_a, sent_a, *plane_b)
    core_a = swap_with(sent_a, 1, count)
    own_b, z_b = reduce_z(own_b, plane_b, groups)
    own_a, plane_a = reduce_plane(kept_a, core_a, groups)
    own_a, z_a = reduce_z(own_a, plane_a, groups)
    total_b = reduce_end(own_b, z_b)
    total_a = reduce_end(own_a, z_a)
    own_small = total_a[4, :1]
    own_vec, own_bias = small_back(own_small, step)
    owned = (
        jnp.concatenate([total_a[:3], total_b[9:]]),
        jnp.stack([total_a[3], total_b[0]]),
        jnp.concatenate(list(total_b[1:5]), 1),
        total_b[5:9].reshape(4 * step, width),
        own_vec,
        own_bias,
    )
    local_squares = jnp.sum(total_b * total_b) + jnp.sum(total_a[:4] * total_a[:4]) + jnp.sum(own_small * own_small)
    grad_norm = jnp.sqrt(sum_all(local_squares, groups))
    factor = jnp.minimum(1.0, clip_norm / (grad_norm + 1e-06))
    states = (
        (attn_weight, attn_m, attn_v),
        (gate_weight, gate_m, gate_v),
        (in_weight, in_m, in_v),
        (out_weight, out_m, out_v),
        (norm_params, norm_m, norm_v),
        (in_bias, bias_m, bias_v),
    )
    step_rates = (learn_rate, learn_rate, learn_rate, learn_rate, vector_rate, vector_rate)
    updated = [
        adam_update(state[0], state[1], state[2], gradient, factor, step_rate)
        for state, gradient, step_rate in zip(states, owned, step_rates)
    ]
    return (
        layer_out,
        input_grad,
        grad_norm,
        updated[0][0],
        updated[0][1],
        updated[0][2],
        updated[1][0],
        updated[1][1],
        updated[1][2],
        updated[2][0],
        updated[2][1],
        updated[2][2],
        updated[3][0],
        updated[3][1],
        updated[3][2],
        updated[4][0],
        updated[4][1],
        updated[4][2],
        updated[5][0],
        updated[5][1],
        updated[5][2],
    )


def solution(mesh):
    return jax.shard_map(
        functools.partial(body, bit_groups(mesh.shape)),
        mesh=mesh,
        in_specs=(
            P(("dp", "inner"), None),
            P(("dp", "inner")),
            P(("dp", "inner")),
            P(("dp", "inner"), None),
            P(None, ("dp", "inner"), None),
            P(None, ("dp", "inner"), None),
            P(None, ("dp", "inner"), None),
            P(None, ("dp", "inner"), None),
            P(None, ("dp", "inner"), None),
            P(None, ("dp", "inner"), None),
            P(("dp", "inner"), None),
            P(("dp", "inner"), None),
            P(("dp", "inner"), None),
            P(("dp", "inner"), None),
            P(("dp", "inner"), None),
            P(("dp", "inner"), None),
            P(None, ("dp", "inner")),
            P(None, ("dp", "inner")),
            P(None, ("dp", "inner")),
            P(("dp", "inner")),
            P(("dp", "inner")),
            P(("dp", "inner")),
        ),
        out_specs=(
            P(("dp", "inner"), None),
            P(("dp", "inner"), None),
            P(),
            P(None, ("dp", "inner"), None),
            P(None, ("dp", "inner"), None),
            P(None, ("dp", "inner"), None),
            P(None, ("dp", "inner"), None),
            P(None, ("dp", "inner"), None),
            P(None, ("dp", "inner"), None),
            P(("dp", "inner"), None),
            P(("dp", "inner"), None),
            P(("dp", "inner"), None),
            P(("dp", "inner"), None),
            P(("dp", "inner"), None),
            P(("dp", "inner"), None),
            P(None, ("dp", "inner")),
            P(None, ("dp", "inner")),
            P(None, ("dp", "inner")),
            P(("dp", "inner")),
            P(("dp", "inner")),
            P(("dp", "inner")),
        ),
        check_vma=False,
    )
```

```python
import functools
import jax
import jax.numpy as jnp
from jax import lax
from jax.experimental import pallas as pl
from jax.experimental.pallas import tpu as pltpu
from jax.sharding import PartitionSpec as P

AXES = ("dp", "inner")
HEADS = 8
HEAD = 64
STEP = 10
LOG2E = 1.4426950408889634
BLOCK = 256


norm_eps = 1e-05
first_decay = 0.9
second_decay = 0.999
adam_eps = 1e-08
learn_rate = 0.05
vector_rate = 0.8
weight_decay = 0.1
clip_norm = 1.0
masked_score = -1e30


def normalize_parts(values, gain_row, bias_row):
    centred = values - jnp.mean(values, -1, keepdims=True)
    spread = jnp.mean(centred * centred, -1, keepdims=True)
    scale_row = lax.rsqrt(spread + norm_eps)
    unit_rows = centred * scale_row
    return (unit_rows * gain_row + bias_row, unit_rows, scale_row)


def normalize_back(grad_rows, unit_rows, scale_row, gain_row):
    grad_unit = grad_rows * gain_row
    return scale_row * (
        grad_unit
        - jnp.mean(grad_unit, -1, keepdims=True)
        - unit_rows * jnp.mean(grad_unit * unit_rows, -1, keepdims=True)
    )


def bit_groups(sizes):
    dp_bits = sizes["dp"].bit_length() - 1
    inner_bits = sizes["inner"].bit_length() - 1
    y_bits = dp_bits // 2
    plane_bits = (inner_bits - 1) + y_bits
    return (1, plane_bits, dp_bits - y_bits)


def swap_with(array, offset, count):
    return lax.ppermute(array, AXES, [(source, source ^ offset) for source in range(count)])


def stage_bits(groups):
    return ((0, groups[0]), (groups[0], groups[1]), (groups[0] + groups[1], groups[2]))


def gather_z(shard, groups):
    count = 2 ** sum(groups)
    first_bit, bits = stage_bits(groups)[2]
    return jnp.stack([shard] + [swap_with(shard, offset << first_bit, count) for offset in range(1, 2**bits)])


def gather_plane(column, groups):
    count = 2 ** sum(groups)
    first_bit, bits = stage_bits(groups)[1]
    return [swap_with(column, offset << first_bit, count) for offset in range(1, 2**bits)]


def gather_core(column, planes, groups):
    return swap_with(jnp.concatenate([column] + planes), 1, 2 ** sum(groups))


def offsets_of(groups):
    (_, _), (plane_bit, plane_bits), (z_bit, z_bits) = stage_bits(groups)
    table = [
        [(plane << plane_bit) | (z << z_bit) for z in range(2**z_bits)] for plane in range(2**plane_bits)
    ]
    return table + [[offset | 1 for row in table for offset in row]]


def vmem_spec():
    return pl.BlockSpec(memory_space=pltpu.VMEM)


def smem_spec():
    return pl.BlockSpec(memory_space=pltpu.SMEM)


def matrix_shape(kind, pieces, count, step, width):
    if kind == "stack":
        return (pieces, count, step, width)
    if kind == "rows":
        return (count, pieces, step, width)
    return (count, step, pieces * width)


def place_kernel(offsets, layout, own_ref, *refs):
    parts = refs[: len(offsets)]
    outs = refs[len(offsets) :]
    own = own_ref[0]
    total = None
    for part, row in zip(parts, offsets):
        for entry, offset in enumerate(row):
            owner = own ^ offset
            for index, (kind, first, pieces) in enumerate(layout):
                width = part.shape[3]
                if kind == "sum":
                    block = part[entry, first].astype(jnp.float32)
                    total = block if total is None else total + block
                elif kind == "stack":
                    for piece in range(pieces):
                        outs[index][piece, owner] = part[entry, first + piece]
                elif kind == "rows":
                    for piece in range(pieces):
                        outs[index][owner, piece] = part[entry, first + piece]
                else:
                    for piece in range(pieces):
                        outs[index][owner, :, piece * width : (piece + 1) * width] = part[entry, first + piece]
    for index, (kind, _, _) in enumerate(layout):
        if kind == "sum":
            outs[index][...] = total


def place(own, parts, layout, groups):
    count = 2 ** sum(groups)
    step, width = parts[0].shape[2:]
    offsets = offsets_of(groups)
    if step % 16:
        order = jnp.argsort(jnp.array([o for row in offsets for o in row]) ^ own)
        full = jnp.concatenate(parts)[order]
        result = []
        for kind, first, pieces in layout:
            chosen = full[:, first : first + pieces]
            if kind == "sum":
                result.append(jnp.sum(chosen.astype(jnp.float32), 0).reshape(pieces * step, width))
            elif kind == "stack":
                result.append(jnp.moveaxis(chosen, 0, 1))
            elif kind == "rows":
                result.append(chosen)
            else:
                result.append(jnp.moveaxis(chosen, 1, 2).reshape(count, step, pieces * width))
        return result
    shapes = [
        jax.ShapeDtypeStruct((step, width), jnp.float32)
        if kind == "sum"
        else jax.ShapeDtypeStruct(matrix_shape(kind, pieces, count, step, width), jnp.bfloat16)
        for kind, _, pieces in layout
    ]
    return pl.pallas_call(
        functools.partial(place_kernel, offsets, layout),
        in_specs=[smem_spec()] + [vmem_spec() for _ in parts],
        out_specs=[vmem_spec() for _ in layout],
        out_shape=shapes,
        name="place",
    )(own[None].astype(jnp.int32), *parts)


def split_kernel(offsets, layout, own_ref, *refs):
    ins = refs[: len(layout)]
    kept, sent = refs[len(layout) :]
    own = own_ref[0]
    for entry, offset in enumerate(offsets):
        for side, target in enumerate((kept, sent)):
            owner = own ^ (offset | side)
            for index, (kind, first, pieces) in enumerate(layout):
                width = target.shape[3]
                for piece in range(pieces):
                    if kind == "sum":
                        block = ins[index][...]
                    elif kind == "stack":
                        block = ins[index][piece, owner]
                    elif kind == "rows":
                        block = ins[index][owner, piece]
                    else:
                        block = ins[index][owner, :, piece * width : (piece + 1) * width]
                    target[entry, first + piece] = block


def split(own, grads, layout, groups):
    count = 2 ** sum(groups)
    width = 512
    total = sum(pieces for _, _, pieces in layout)
    step = grads[0].shape[-2]
    offsets = [offset for row in offsets_of(groups)[:-1] for offset in row]
    if step % 16:
        pieces_of = []
        for grad, (kind, _, pieces) in zip(grads, layout):
            if kind == "sum":
                grad = jnp.broadcast_to(grad.reshape(1, pieces, step, width), (count, pieces, step, width))
            elif kind == "stack":
                grad = jnp.moveaxis(grad, 1, 0)
            elif kind == "columns":
                grad = jnp.moveaxis(grad.reshape(count, step, pieces, width), 2, 1)
            pieces_of.append(grad)
        full = jnp.concatenate(pieces_of, 1)
        order = jnp.array(offsets) ^ own
        return full[order], full[order ^ 1]
    shape = jax.ShapeDtypeStruct((len(offsets), total, step, width), jnp.bfloat16)
    return pl.pallas_call(
        functools.partial(split_kernel, offsets, layout),
        in_specs=[smem_spec()] + [vmem_spec() for _ in grads],
        out_specs=[vmem_spec(), vmem_spec()],
        out_shape=[shape, shape],
        name="split",
    )(own[None].astype(jnp.int32), *grads)


def reduce_plane(kept, received, groups):
    count = 2 ** sum(groups)
    _, (first_bit, bits), (_, z_bits) = stage_bits(groups)
    shape = (2**bits, 2**z_bits) + kept.shape[1:]
    kept = kept.reshape(shape)
    received = received.reshape(shape)
    total = lambda offset: kept[offset].astype(jnp.float32) + received[offset].astype(jnp.float32)
    arrived = [
        swap_with(total(offset).astype(jnp.bfloat16), offset << first_bit, count) for offset in range(1, 2**bits)
    ]
    return total(0), arrived


def reduce_z(own_part, arrived, groups):
    count = 2 ** sum(groups)
    first_bit, bits = stage_bits(groups)[2]
    total = lambda z: own_part[z] + sum(part[z].astype(jnp.float32) for part in arrived)
    return total(0), [
        swap_with(total(z).astype(jnp.bfloat16), z << first_bit, count) for z in range(1, 2**bits)
    ]


def reduce_end(own_part, arrived):
    return own_part + sum(part.astype(jnp.float32) for part in arrived)


def sum_all(value, groups):
    for bit in range(sum(groups)):
        value = value + swap_with(value, 1 << bit, 2 ** sum(groups))
    return value


def tie(*values):
    return lax.optimization_barrier(values)


def small_shard(vec, bias, own, count, width):
    step = vec.shape[1]
    lane = lax.broadcasted_iota(jnp.int32, (7, width), 1)
    rows = jnp.where(lane // step == own, jnp.tile(vec, (1, count)), 0.0)
    place_of = lax.broadcasted_iota(jnp.int32, (4, width), 0) * width + lax.broadcasted_iota(
        jnp.int32, (4, width), 1
    )
    tiled = jnp.tile(bias, width // bias.shape[0])[None]
    bias_rows = jnp.where(place_of // bias.shape[0] == own, tiled, 0.0)
    return jnp.concatenate([rows, bias_rows])


def pad_rows(rows, step):
    pieces = -(-rows.shape[0] // step)
    rows = jnp.pad(rows.astype(jnp.bfloat16), ((0, pieces * step - rows.shape[0]), (0, 0)))
    return rows.reshape(pieces, step, rows.shape[1])


def mat(a,b,dims):
    return lax.dot_general(a,b,(dims,((),())),preferred_element_type=jnp.float32)

def fill_bias(bias_ref, seg_col, pos_col, seg_row, pos_row):
    rows=bias_ref.shape[0]
    step=min(BLOCK,rows)
    for first in range(0,rows,step):
        sc=seg_col[first:first+step,:]; pc=pos_col[first:first+step,:]
        sr=seg_row[:,first:]; pr=pos_row[:,first:]
        allowed=(sc==sr)&(pc<=pr)
        bias_ref[first:first+step,first:]=jnp.where(allowed,0.0,masked_score)

def head_lanes(shape, which):
    lane=lax.broadcasted_iota(jnp.int32,shape,1)
    return (lane//HEAD)==which

def attn_fwd_kernel(segc,posc,segr,posr,q_ref,k_ref,v_ref,o_ref,lse_ref,bias_ref):
    @pl.when(pl.program_id(0)==0)
    def _():
        fill_bias(bias_ref,segc,posc,segr,posr)
    rows=q_ref.shape[0]; step=min(BLOCK,rows)
    pair=q_ref.shape[1]//HEAD
    const=HEAD**-0.5*LOG2E
    for first in range(0,rows,step):
        keys=first+step
        q=q_ref[first:keys,:]
        mixed=None
        for which in range(pair):
            own=head_lanes(q.shape,which)
            qh=jnp.where(own,q,jnp.zeros_like(q))
            s=mat(k_ref[:keys,:],qh,((1,),(1,)))*const+bias_ref[:keys,first:keys]
            m=jnp.max(s,0,keepdims=True)
            w=jnp.exp2(s-m)
            total=jnp.sum(w,0,keepdims=True)
            p=(w*(1.0/total)).astype(jnp.bfloat16)
            o=mat(p,v_ref[:keys,:],((0,),(0,)))
            mixed=o if mixed is None else jnp.where(own,o,mixed)
            lse_ref[0,which:which+1,first:keys]=m+jnp.log2(total)
        o_ref[first:keys,:]=mixed.astype(jnp.bfloat16)

def attn_bwd_kernel(segc,posc,segr,posr,q_ref,k_ref,v_ref,do_ref,lse_ref,dq_ref,dk_ref,dv_ref,bias_ref,dk_acc,dv_acc):
    @pl.when(pl.program_id(0)==0)
    def _():
        fill_bias(bias_ref,segc,posc,segr,posr)
    rows=q_ref.shape[0]; step=min(BLOCK,rows)
    pair=q_ref.shape[1]//HEAD
    const=HEAD**-0.5*LOG2E
    scale=HEAD**-0.5
    dk_acc[...]=jnp.zeros_like(dk_acc); dv_acc[...]=jnp.zeros_like(dv_acc)
    for first in range(0,rows,step):
        keys=first+step
        q=q_ref[first:keys,:]; do=do_ref[first:keys,:]
        dq=None
        for which in range(pair):
            own=head_lanes(q.shape,which)
            qh=jnp.where(own,q,jnp.zeros_like(q))
            doh=jnp.where(own,do,jnp.zeros_like(do))
            s=mat(k_ref[:keys,:],qh,((1,),(1,)))
            p=jnp.exp2(s*const+(bias_ref[:keys,first:keys]-lse_ref[0,which:which+1,first:keys]))
            dp=mat(v_ref[:keys,:],doh,((1,),(1,)))
            inner=jnp.sum(p*dp,0,keepdims=True)
            ds=(p*(dp-inner)).astype(jnp.bfloat16)
            dv_acc[:keys,:]+=mat(p.astype(jnp.bfloat16),doh,((1,),(0,)))
            dk_acc[:keys,:]+=mat(ds,qh,((1,),(0,)))
            d=mat(ds,k_ref[:keys,:],((0,),(0,)))
            dq=d if dq is None else jnp.where(own,d,dq)
        dq_ref[first:keys,:]=(dq*scale).astype(jnp.bfloat16)
    dk_ref[...]=(dk_acc[...]*scale).astype(jnp.bfloat16)
    dv_ref[...]=dv_acc[...].astype(jnp.bfloat16)

def const_map(*_): return (0,0)

def seg_args(segments,positions):
    return (segments[:,None],positions[:,None],segments[None],positions[None])

def attend(q,k,v,segments,positions):
    rows,width=q.shape
    pairs=width//128
    blk=pl.BlockSpec((rows,128),lambda j:(0,j))
    col=pl.BlockSpec((rows,1),const_map); row=pl.BlockSpec((1,rows),const_map)
    return pl.pallas_call(attn_fwd_kernel,grid=(pairs,),
        in_specs=[col,col,row,row,blk,blk,blk],
        out_specs=[blk,pl.BlockSpec((1,2,rows),lambda j:(j,0,0))],
        out_shape=[jax.ShapeDtypeStruct((rows,width),jnp.bfloat16),jax.ShapeDtypeStruct((pairs,2,rows),jnp.float32)],
        scratch_shapes=[pltpu.VMEM((rows,rows),jnp.float32)],
        name="attn_fwd",
    )(*seg_args(segments,positions),q,k,v)

def attend_back(q,k,v,do,lse,segments,positions,base,pairs):
    rows=q.shape[0]
    blk=pl.BlockSpec((rows,128),lambda j:(0,j+base))
    oblk=pl.BlockSpec((rows,128),lambda j:(0,j))
    col=pl.BlockSpec((rows,1),const_map); row=pl.BlockSpec((1,rows),const_map)
    out=jax.ShapeDtypeStruct((rows,128*pairs),jnp.bfloat16)
    return pl.pallas_call(attn_bwd_kernel,grid=(pairs,),
        in_specs=[col,col,row,row,blk,blk,blk,blk,pl.BlockSpec((1,2,rows),lambda j:(j+base,0,0))],
        out_specs=[oblk,oblk,oblk],
        out_shape=[out,out,out],
        scratch_shapes=[pltpu.VMEM((rows,rows),jnp.float32),pltpu.VMEM((rows,128),jnp.float32),pltpu.VMEM((rows,128),jnp.float32)],
        name="attn_bwd",
    )(*seg_args(segments,positions),q,k,v,do,lse)


def adam_update(weight, first_moment, second_moment, gradient, factor, step_rate):
    clipped = gradient * factor
    first_new = first_decay * first_moment + (1.0 - first_decay) * clipped
    second_new = second_decay * second_moment + (1.0 - second_decay) * clipped * clipped
    corrected = first_new / (1.0 - first_decay**STEP)
    spread = second_new / (1.0 - second_decay**STEP)
    weight_new = weight - step_rate * (
        corrected / (jnp.sqrt(spread) + adam_eps) + weight_decay * weight
    )
    return (weight_new, first_new, second_new)


def body(
    groups,
    tokens,
    segments,
    positions,
    cotangent,
    attn_weight,
    attn_m,
    attn_v,
    gate_weight,
    gate_m,
    gate_v,
    in_weight,
    in_m,
    in_v,
    out_weight,
    out_m,
    out_v,
    norm_params,
    norm_m,
    norm_v,
    in_bias,
    bias_m,
    bias_v,
):
    count = 2 ** sum(groups)
    own = lax.axis_index(AXES)
    width = 512
    step = attn_weight.shape[1]
    low = lambda value: value.astype(jnp.bfloat16)
    dot = functools.partial(jnp.einsum, preferred_element_type=jnp.float32)
    columns = lambda value: [value[:, width * j : width * (j + 1)] for j in range(4)]
    small = pad_rows(small_shard(norm_params, in_bias, own, count, width), step)
    extra = small.shape[0]
    first_shard = jnp.concatenate(
        [low(attn_weight[:3]), low(gate_weight[:1]), low(attn_weight[3:]), small]
    )
    second_shard = jnp.concatenate(
        [
            jnp.stack([low(gate_weight[1])] + columns(low(in_weight))),
            low(out_weight).reshape(4, step, width),
        ]
    )
    z_first = gather_z(first_shard, groups)
    z_first, second_shard = tie(z_first, second_shard)
    plane_first = gather_plane(z_first, groups)
    z_second = gather_z(second_shard, groups)
    z_second, *plane_first = tie(z_second, *plane_first)
    core_first = gather_core(z_first, plane_first, groups)
    plane_second = gather_plane(z_second, groups)
    w_four, w_o, vectors = place(
        own,
        [z_first] + plane_first + [core_first],
        [("stack", 0, 4), ("stack", 4, 1), ("sum", 5, extra)],
        groups,
    )
    w_four = w_four.reshape(4, count * step, width)
    w_o = w_o.reshape(count * step, width)
    bias = vectors[7:11].reshape(-1)
    inputs = tokens.astype(jnp.float32)
    normed_full, unit_one, scale_one = normalize_parts(inputs, vectors[0], vectors[1])
    normed = low(normed_full)
    queries, keys, values = [low(dot("td,de->te", normed, w_four[j])) for j in range(3)]
    mixed_heads, log_total = attend(queries, keys, values, segments, positions)
    mixed_heads, *plane_second = tie(mixed_heads, *plane_second)
    core_second = gather_core(z_second, plane_second, groups)
    attended = dot("td,de->te", mixed_heads, w_o)
    attn_gate = jax.nn.sigmoid(dot("td,de->te", normed, w_four[3]) + vectors[4])
    middle = attn_gate * attended + (1.0 - attn_gate) * inputs
    normed_two_full, unit_two, scale_two = normalize_parts(middle, vectors[2], vectors[3])
    normed_two = low(normed_two_full)
    w_f, w_in, w_out = place(
        own,
        [z_second] + plane_second + [core_second],
        [("stack", 0, 1), ("columns", 1, 4), ("rows", 5, 4)],
        groups,
    )
    w_f = w_f.reshape(count * step, width)
    w_in = w_in.reshape(count * step, 4 * width)
    w_out = w_out.reshape(4 * count * step, width)
    hidden = dot("td,df->tf", normed_two, w_in) + bias
    active = low(jnp.maximum(hidden, 0.0))
    branch = dot("tf,fd->td", active, w_out) + vectors[6]
    ffn_gate = jax.nn.sigmoid(dot("td,de->te", normed_two, w_f) + vectors[5])
    layer_out = low(ffn_gate * branch + (1.0 - ffn_gate) * middle)
    grad_out = cotangent.astype(jnp.float32)
    grad_branch = grad_out * ffn_gate
    grad_fgate = grad_out * (branch - middle) * ffn_gate * (1.0 - ffn_gate)
    grad_middle = grad_out * (1.0 - ffn_gate)
    branch_low = low(grad_branch)
    grad_w_out = low(dot("tf,td->fd", active, branch_low))
    grad_active = dot("td,fd->tf", branch_low, w_out)
    grad_hidden = jnp.where(hidden > 0.0, grad_active, 0.0)
    hidden_low = low(grad_hidden)
    grad_w_in = low(dot("td,tf->df", normed_two, hidden_low))
    fgate_low = low(grad_fgate)
    grad_w_f = low(dot("td,te->de", normed_two, fgate_low))
    grad_normed_two = dot("tf,df->td", hidden_low, w_in) + dot("te,de->td", fgate_low, w_f)
    grad_gain_two = jnp.sum(grad_normed_two * unit_two, 0)
    grad_shift_two = jnp.sum(grad_normed_two, 0)
    grad_middle = grad_middle + normalize_back(grad_normed_two, unit_two, scale_two, vectors[2])
    grad_attended = grad_middle * attn_gate
    grad_agate = grad_middle * (attended - inputs) * attn_gate * (1.0 - attn_gate)
    grad_inputs = grad_middle * (1.0 - attn_gate)
    attended_low = low(grad_attended)
    grad_w_o = low(dot("td,te->de", mixed_heads, attended_low))
    grad_mixed = low(dot("te,de->td", attended_low, w_o))
    blocks = lambda value: value.reshape(1, count, step, width)
    kept_b, sent_b = split(
        own,
        [
            blocks(grad_w_f),
            grad_w_in.reshape(count, step, 4 * width),
            grad_w_out.reshape(count, 4, step, width),
            blocks(grad_w_o),
        ],
        [("stack", 0, 1), ("columns", 1, 4), ("rows", 5, 4), ("stack", 9, 1)],
        groups,
    )
    core_b = swap_with(sent_b, 1, count)
    half_one = attend_back(queries, keys, values, grad_mixed, log_total, segments, positions, 0, 2)
    core_b, kept_b, *half_one = tie(core_b, kept_b, *half_one)
    own_b, plane_b = reduce_plane(kept_b, core_b, groups)
    own_b, log_total = tie(own_b, log_total)
    half_two = attend_back(queries, keys, values, grad_mixed, log_total, segments, positions, 2, 2)
    triple_grad = [jnp.concatenate([one, two], 1) for one, two in zip(half_one, half_two)]
    agate_low = low(grad_agate)
    back_four = triple_grad + [agate_low]
    grad_normed = sum(dot("te,de->td", back_four[j], w_four[j]) for j in range(4))
    grad_w_four = [low(dot("td,te->de", normed, back_four[j])) for j in range(4)]
    grad_gain_one = jnp.sum(grad_normed * unit_one, 0)
    grad_shift_one = jnp.sum(grad_normed, 0)
    grad_inputs = grad_inputs + normalize_back(grad_normed, unit_one, scale_one, vectors[0])
    input_grad = low(grad_inputs)
    grad_vectors = jnp.stack(
        [
            grad_gain_one,
            grad_shift_one,
            grad_gain_two,
            grad_shift_two,
            jnp.sum(grad_agate, 0),
            jnp.sum(grad_fgate, 0),
            jnp.sum(grad_branch, 0),
        ]
    )
    grad_bias = jnp.sum(grad_hidden, 0)
    grad_small = pad_rows(jnp.concatenate([grad_vectors, grad_bias.reshape(4, width)]), step)
    kept_a, sent_a = split(
        own,
        [blocks(grad) for grad in grad_w_four] + [grad_small.reshape(-1, width) if extra == 1 else grad_small],
        [("stack", j, 1) for j in range(4)] + [("sum", 4, extra)],
        groups,
    )
    kept_a, sent_a, *plane_b = tie(kept_a, sent_a, *plane_b)
    core_a = swap_with(sent_a, 1, count)
    own_b, z_b = reduce_z(own_b, plane_b, groups)
    own_a, plane_a = reduce_plane(kept_a, core_a, groups)
    own_a, z_a = reduce_z(own_a, plane_a, groups)
    total_b = reduce_end(own_b, z_b)
    total_a = reduce_end(own_a, z_a)
    own_small = total_a[4:].reshape(extra * step, width)
    own_vec = lax.dynamic_slice(own_small[:7], (0, own * step), (7, step))
    own_bias = lax.dynamic_slice(own_small[7:11].reshape(-1), (own * 4 * step,), (4 * step,))
    owned = (
        jnp.concatenate([total_a[:3], total_b[9:]]),
        jnp.stack([total_a[3], total_b[0]]),
        jnp.concatenate(list(total_b[1:5]), 1),
        total_b[5:9].reshape(4 * step, width),
        own_vec,
        own_bias,
    )
    local_squares = jnp.sum(total_b * total_b) + jnp.sum(total_a[:4] * total_a[:4]) + jnp.sum(own_vec * own_vec) + jnp.sum(own_bias * own_bias)
    grad_norm = jnp.sqrt(sum_all(local_squares, groups))
    factor = jnp.minimum(1.0, clip_norm / (grad_norm + 1e-06))
    states = (
        (attn_weight, attn_m, attn_v),
        (gate_weight, gate_m, gate_v),
        (in_weight, in_m, in_v),
        (out_weight, out_m, out_v),
        (norm_params, norm_m, norm_v),
        (in_bias, bias_m, bias_v),
    )
    step_rates = (learn_rate, learn_rate, learn_rate, learn_rate, vector_rate, vector_rate)
    updated = [
        adam_update(state[0], state[1], state[2], gradient, factor, step_rate)
        for state, gradient, step_rate in zip(states, owned, step_rates)
    ]
    return (
        layer_out,
        input_grad,
        grad_norm,
        updated[0][0],
        updated[0][1],
        updated[0][2],
        updated[1][0],
        updated[1][1],
        updated[1][2],
        updated[2][0],
        updated[2][1],
        updated[2][2],
        updated[3][0],
        updated[3][1],
        updated[3][2],
        updated[4][0],
        updated[4][1],
        updated[4][2],
        updated[5][0],
        updated[5][1],
        updated[5][2],
    )


def solution(mesh):
    return jax.shard_map(
        functools.partial(body, bit_groups(mesh.shape)),
        mesh=mesh,
        in_specs=(
            P(("dp", "inner"), None),
            P(("dp", "inner")),
            P(("dp", "inner")),
            P(("dp", "inner"), None),
            P(None, ("dp", "inner"), None),
            P(None, ("dp", "inner"), None),
            P(None, ("dp", "inner"), None),
            P(None, ("dp", "inner"), None),
            P(None, ("dp", "inner"), None),
            P(None, ("dp", "inner"), None),
            P(("dp", "inner"), None),
            P(("dp", "inner"), None),
            P(("dp", "inner"), None),
            P(("dp", "inner"), None),
            P(("dp", "inner"), None),
            P(("dp", "inner"), None),
            P(None, ("dp", "inner")),
            P(None, ("dp", "inner")),
            P(None, ("dp", "inner")),
            P(("dp", "inner")),
            P(("dp", "inner")),
            P(("dp", "inner")),
        ),
        out_specs=(
            P(("dp", "inner"), None),
            P(("dp", "inner"), None),
            P(),
            P(None, ("dp", "inner"), None),
            P(None, ("dp", "inner"), None),
            P(None, ("dp", "inner"), None),
            P(None, ("dp", "inner"), None),
            P(None, ("dp", "inner"), None),
            P(None, ("dp", "inner"), None),
            P(("dp", "inner"), None),
            P(("dp", "inner"), None),
            P(("dp", "inner"), None),
            P(("dp", "inner"), None),
            P(("dp", "inner"), None),
            P(("dp", "inner"), None),
            P(None, ("dp", "inner")),
            P(None, ("dp", "inner")),
            P(None, ("dp", "inner")),
            P(("dp", "inner")),
            P(("dp", "inner")),
            P(("dp", "inner")),
        ),
        check_vma=False,
    )
```

```python
import functools
import jax
import jax.numpy as jnp
from jax import lax
from jax.experimental import pallas as pl
from jax.experimental.pallas import tpu as pltpu
from jax.sharding import PartitionSpec as P

AXES = ("dp", "inner")
HEADS = 8
HEAD = 64
STEP = 10
LOG2E = 1.4426950408889634
BLOCK = 256


norm_eps = 1e-05
first_decay = 0.9
second_decay = 0.999
adam_eps = 1e-08
learn_rate = 0.05
vector_rate = 0.8
weight_decay = 0.1
clip_norm = 1.0
masked_score = -1e30


def normalize_parts(values, gain_row, bias_row):
    centred = values - jnp.mean(values, -1, keepdims=True)
    spread = jnp.mean(centred * centred, -1, keepdims=True)
    scale_row = lax.rsqrt(spread + norm_eps)
    unit_rows = centred * scale_row
    return (unit_rows * gain_row + bias_row, unit_rows, scale_row)


def normalize_back(grad_rows, unit_rows, scale_row, gain_row):
    grad_unit = grad_rows * gain_row
    return scale_row * (
        grad_unit
        - jnp.mean(grad_unit, -1, keepdims=True)
        - unit_rows * jnp.mean(grad_unit * unit_rows, -1, keepdims=True)
    )


def bit_groups(sizes):
    dp_bits = sizes["dp"].bit_length() - 1
    inner_bits = sizes["inner"].bit_length() - 1
    y_bits = dp_bits // 2
    plane_bits = (inner_bits - 1) + y_bits
    return (1, plane_bits, dp_bits - y_bits)


def swap_with(array, offset, count):
    return lax.ppermute(array, AXES, [(source, source ^ offset) for source in range(count)])


def stage_bits(groups):
    return ((0, groups[0]), (groups[0], groups[1]), (groups[0] + groups[1], groups[2]))


def gather_z(shard, groups):
    count = 2 ** sum(groups)
    first_bit, bits = stage_bits(groups)[2]
    return jnp.stack([shard] + [swap_with(shard, offset << first_bit, count) for offset in range(1, 2**bits)])


def gather_plane(column, groups):
    count = 2 ** sum(groups)
    first_bit, bits = stage_bits(groups)[1]
    return [swap_with(column, offset << first_bit, count) for offset in range(1, 2**bits)]


def gather_core(column, planes, groups):
    return swap_with(jnp.concatenate([column] + planes), 1, 2 ** sum(groups))


def offsets_of(groups):
    (_, _), (plane_bit, plane_bits), (z_bit, z_bits) = stage_bits(groups)
    table = [
        [(plane << plane_bit) | (z << z_bit) for z in range(2**z_bits)] for plane in range(2**plane_bits)
    ]
    return table + [[offset | 1 for row in table for offset in row]]


def plane_orders(groups):
    _, (first_bit, bits), _ = stage_bits(groups)
    order = list(range(first_bit, first_bit + bits))
    return order, order[bits // 2 :] + order[: bits // 2]


def z_offsets(groups):
    _, _, (first_bit, bits) = stage_bits(groups)
    return [z << first_bit for z in range(2**bits)]


def send_halves(arrays, orders, position, groups):
    count = 2 ** sum(groups)
    return [swap_with(array, 1 << order[position], count) for array, order in zip(arrays, orders)]


def join_halves(arrays, received, tables, orders, position):
    arrays = [jnp.concatenate(pair) for pair in zip(arrays, received)]
    tables = [
        table + [offset | (1 << order[position]) for offset in table] for table, order in zip(tables, orders)
    ]
    return arrays, tables


def vmem_spec():
    return pl.BlockSpec(memory_space=pltpu.VMEM)


def smem_spec():
    return pl.BlockSpec(memory_space=pltpu.SMEM)


def matrix_shape(kind, pieces, count, step, width):
    if kind == "stack":
        return (pieces, count, step, width)
    if kind == "rows":
        return (count, pieces, step, width)
    return (count, step, pieces * width)


def place_kernel(tables, layout, own_ref, *refs):
    parts = refs[: len(tables)]
    outs = refs[len(tables) :]
    own = own_ref[0]
    total = None
    where_to = [
        (index, kind, piece) for index, (kind, _, pieces) in enumerate(layout) for piece in range(pieces)
    ]
    for part, (row, first) in zip(parts, tables):
        width = part.shape[3]
        for entry, offset in enumerate(row):
            owner = own ^ offset
            for source in range(part.shape[1]):
                index, kind, piece = where_to[first + source]
                block = part[entry, source]
                if kind == "sum":
                    block = block.astype(jnp.float32)
                    total = block if total is None else total + block
                elif kind == "stack":
                    outs[index][piece, owner] = block
                elif kind == "rows":
                    outs[index][owner, piece] = block
                else:
                    outs[index][owner, :, piece * width : (piece + 1) * width] = block
    for index, (kind, _, _) in enumerate(layout):
        if kind == "sum":
            outs[index][...] = total


def place(own, parts, tables, layout, groups):
    count = 2 ** sum(groups)
    step, width = parts[0].shape[2:]
    if step % 16:
        firsts = sorted({first for _, first in tables})
        groups_of = []
        for first in firsts:
            chosen = [(part, row) for part, (row, base) in zip(parts, tables) if base == first]
            order = jnp.argsort(jnp.array([o for _, row in chosen for o in row]) ^ own)
            groups_of.append(jnp.concatenate([part for part, _ in chosen])[order])
        full = jnp.concatenate(groups_of, 1)
        result = []
        for kind, first, pieces in layout:
            chosen = full[:, first : first + pieces]
            if kind == "sum":
                result.append(jnp.sum(chosen.astype(jnp.float32), 0).reshape(pieces * step, width))
            elif kind == "stack":
                result.append(jnp.moveaxis(chosen, 0, 1))
            elif kind == "rows":
                result.append(chosen)
            else:
                result.append(jnp.moveaxis(chosen, 1, 2).reshape(count, step, pieces * width))
        return result
    shapes = [
        jax.ShapeDtypeStruct((step, width), jnp.float32)
        if kind == "sum"
        else jax.ShapeDtypeStruct(matrix_shape(kind, pieces, count, step, width), jnp.bfloat16)
        for kind, _, pieces in layout
    ]
    return pl.pallas_call(
        functools.partial(place_kernel, tables, layout),
        in_specs=[smem_spec()] + [vmem_spec() for _ in parts],
        out_specs=[vmem_spec() for _ in layout],
        out_shape=shapes,
        name="place",
    )(own[None].astype(jnp.int32), *parts)


def split_kernel(offsets, layout, own_ref, *refs):
    ins = refs[: len(layout)]
    kept, sent = refs[len(layout) :]
    own = own_ref[0]
    for entry, offset in enumerate(offsets):
        for side, target in enumerate((kept, sent)):
            owner = own ^ (offset | side)
            for index, (kind, first, pieces) in enumerate(layout):
                width = target.shape[3]
                for piece in range(pieces):
                    if kind == "sum":
                        block = ins[index][...]
                    elif kind == "stack":
                        block = ins[index][piece, owner]
                    elif kind == "rows":
                        block = ins[index][owner, piece]
                    else:
                        block = ins[index][owner, :, piece * width : (piece + 1) * width]
                    target[entry, first + piece] = block


def split(own, grads, layout, groups):
    count = 2 ** sum(groups)
    width = 512
    total = sum(pieces for _, _, pieces in layout)
    step = grads[0].shape[-2]
    offsets = [offset for row in offsets_of(groups)[:-1] for offset in row]
    if step % 16:
        pieces_of = []
        for grad, (kind, _, pieces) in zip(grads, layout):
            if kind == "sum":
                grad = jnp.broadcast_to(grad.reshape(1, pieces, step, width), (count, pieces, step, width))
            elif kind == "stack":
                grad = jnp.moveaxis(grad, 1, 0)
            elif kind == "columns":
                grad = jnp.moveaxis(grad.reshape(count, step, pieces, width), 2, 1)
            pieces_of.append(grad)
        full = jnp.concatenate(pieces_of, 1)
        order = jnp.array(offsets) ^ own
        return full[order], full[order ^ 1]
    shape = jax.ShapeDtypeStruct((len(offsets), total, step, width), jnp.bfloat16)
    return pl.pallas_call(
        functools.partial(split_kernel, offsets, layout),
        in_specs=[smem_spec()] + [vmem_spec() for _ in grads],
        out_specs=[vmem_spec(), vmem_spec()],
        out_shape=[shape, shape],
        name="split",
    )(own[None].astype(jnp.int32), *grads)


def plane_sums(kept, received, groups):
    _, (_, bits), (_, z_bits) = stage_bits(groups)
    shape = (2**bits, 2**z_bits) + kept.shape[1:]
    kept = kept.reshape(shape)
    received = received.reshape(shape)
    total = lambda offset: kept[offset].astype(jnp.float32) + received[offset].astype(jnp.float32)
    return total(0), [total(offset).astype(jnp.bfloat16) for offset in range(1, 2**bits)]


def plane_send(parts, groups):
    first_bit = stage_bits(groups)[1][0]
    return [swap_with(part, offset << first_bit, 2 ** sum(groups)) for offset, part in enumerate(parts, 1)]


def reduce_z(own_part, arrived, groups):
    count = 2 ** sum(groups)
    first_bit, bits = stage_bits(groups)[2]
    total = lambda z: own_part[z] + sum(part[z].astype(jnp.float32) for part in arrived)
    return total(0), [
        swap_with(total(z).astype(jnp.bfloat16), z << first_bit, count) for z in range(1, 2**bits)
    ]


def reduce_end(own_part, arrived):
    return own_part + sum(part.astype(jnp.float32) for part in arrived)


def sum_all(value, groups):
    for bit in range(sum(groups)):
        value = value + swap_with(value, 1 << bit, 2 ** sum(groups))
    return value


def tie(*values):
    return lax.optimization_barrier(values)


def small_shard(vec, bias, own, count, width):
    step = vec.shape[1]
    lane = lax.broadcasted_iota(jnp.int32, (7, width), 1)
    rows = jnp.where(lane // step == own, jnp.tile(vec, (1, count)), 0.0)
    place_of = lax.broadcasted_iota(jnp.int32, (4, width), 0) * width + lax.broadcasted_iota(
        jnp.int32, (4, width), 1
    )
    tiled = jnp.tile(bias, width // bias.shape[0])[None]
    bias_rows = jnp.where(place_of // bias.shape[0] == own, tiled, 0.0)
    return jnp.concatenate([rows, bias_rows])


def pad_rows(rows, step):
    pieces = -(-rows.shape[0] // step)
    rows = jnp.pad(rows.astype(jnp.bfloat16), ((0, pieces * step - rows.shape[0]), (0, 0)))
    return rows.reshape(pieces, step, rows.shape[1])


def mat(a,b,dims):
    return lax.dot_general(a,b,(dims,((),())),preferred_element_type=jnp.float32)

def fill_bias(bias_ref, seg_col, pos_col, seg_row, pos_row):
    rows=bias_ref.shape[0]
    step=min(BLOCK,rows)
    for first in range(0,rows,step):
        sc=seg_col[first:first+step,:]; pc=pos_col[first:first+step,:]
        sr=seg_row[:,first:]; pr=pos_row[:,first:]
        allowed=(sc==sr)&(pc<=pr)
        bias_ref[first:first+step,first:]=jnp.where(allowed,0.0,masked_score)

def head_lanes(shape, which):
    lane=lax.broadcasted_iota(jnp.int32,shape,1)
    return (lane//HEAD)==which

def attn_fwd_kernel(segc,posc,segr,posr,q_ref,k_ref,v_ref,o_ref,lse_ref,bias_ref):
    @pl.when(pl.program_id(0)==0)
    def _():
        fill_bias(bias_ref,segc,posc,segr,posr)
    rows=q_ref.shape[0]; step=min(BLOCK,rows)
    pair=q_ref.shape[1]//HEAD
    const=HEAD**-0.5*LOG2E
    for first in range(0,rows,step):
        keys=first+step
        q=q_ref[first:keys,:]
        mixed=None
        for which in range(pair):
            own=head_lanes(q.shape,which)
            qh=jnp.where(own,q,jnp.zeros_like(q))
            s=mat(k_ref[:keys,:],qh,((1,),(1,)))*const+bias_ref[:keys,first:keys]
            m=jnp.max(s,0,keepdims=True)
            w=jnp.exp2(s-m)
            total=jnp.sum(w,0,keepdims=True)
            p=(w*(1.0/total)).astype(jnp.bfloat16)
            o=mat(p,v_ref[:keys,:],((0,),(0,)))
            mixed=o if mixed is None else jnp.where(own,o,mixed)
            lse_ref[0,which:which+1,first:keys]=m+jnp.log2(total)
        o_ref[first:keys,:]=mixed.astype(jnp.bfloat16)

def attn_bwd_kernel(
    offsets, own_ref, segc, posc, segr, posr, q_ref, k_ref, v_ref, do_ref, lse_ref, h_ref, w_ref, *refs
):
    *outs, dh_ref, bias_ref, dk_acc, dv_acc, ht_ref, dw_ref = refs
    rows = q_ref.shape[0]

    @pl.when(pl.program_id(0) == 0)
    def _():
        fill_bias(bias_ref, segc, posc, segr, posr)
        ht_ref[...] = h_ref[...].T
        dh_ref[...] = jnp.zeros_like(dh_ref)

    step = min(BLOCK, rows)
    pair = q_ref.shape[1] // HEAD
    const = HEAD**-0.5 * LOG2E
    scale = HEAD**-0.5
    dk_acc[...] = jnp.zeros_like(dk_acc)
    dv_acc[...] = jnp.zeros_like(dv_acc)
    dq_parts = []
    for first in range(0, rows, step):
        keys = first + step
        q = q_ref[first:keys, :]
        do = do_ref[first:keys, :]
        dq = None
        for which in range(pair):
            own = head_lanes(q.shape, which)
            qh = jnp.where(own, q, jnp.zeros_like(q))
            doh = jnp.where(own, do, jnp.zeros_like(do))
            s = mat(k_ref[:keys, :], qh, ((1,), (1,)))
            p = jnp.exp2(s * const + (bias_ref[:keys, first:keys] - lse_ref[0, which : which + 1, first:keys]))
            dp = mat(v_ref[:keys, :], doh, ((1,), (1,)))
            inner = jnp.sum(p * dp, 0, keepdims=True)
            ds = (p * (dp - inner)).astype(jnp.bfloat16)
            dv_acc[:keys, :] += mat(p.astype(jnp.bfloat16), doh, ((1,), (0,)))
            dk_acc[:keys, :] += mat(ds, qh, ((1,), (0,)))
            d = mat(ds, k_ref[:keys, :], ((0,), (0,)))
            dq = d if dq is None else jnp.where(own, d, dq)
        dq_parts.append((dq * scale).astype(jnp.bfloat16))
    grads = jnp.concatenate(
        [
            jnp.concatenate(dq_parts, 0),
            (dk_acc[...] * scale).astype(jnp.bfloat16),
            dv_acc[...].astype(jnp.bfloat16),
        ],
        1,
    )
    weights = jnp.concatenate([w_ref[0], w_ref[1], w_ref[2]], 1)
    dh_ref[...] += mat(grads, weights, ((1,), (1,)))
    dw = mat(ht_ref[...], grads, ((1,), (0,))).astype(jnp.bfloat16)
    lanes = q_ref.shape[1]
    if offsets is None:
        for j in range(3):
            outs[0][j] = dw[:, j * lanes : (j + 1) * lanes]
    else:
        dw_ref[...] = dw.reshape(dw_ref.shape)
        for entry, offset in enumerate(offsets):
            for side in range(2):
                owner = own_ref[0] ^ (offset | side)
                for j in range(3):
                    outs[side][entry, j] = dw_ref[owner, :, j * lanes : (j + 1) * lanes]


def const_map(*_): return (0,0)

def seg_args(segments,positions):
    return (segments[:,None],positions[:,None],segments[None],positions[None])

def attend(q,k,v,segments,positions):
    rows,width=q.shape
    pairs=width//128
    blk=pl.BlockSpec((rows,128),lambda j:(0,j))
    col=pl.BlockSpec((rows,1),const_map); row=pl.BlockSpec((1,rows),const_map)
    return pl.pallas_call(attn_fwd_kernel,grid=(pairs,),
        in_specs=[col,col,row,row,blk,blk,blk],
        out_specs=[blk,pl.BlockSpec((1,2,rows),lambda j:(j,0,0))],
        out_shape=[jax.ShapeDtypeStruct((rows,width),jnp.bfloat16),jax.ShapeDtypeStruct((pairs,2,rows),jnp.float32)],
        scratch_shapes=[pltpu.VMEM((rows,rows),jnp.float32)],
        name="attn_fwd",
    )(*seg_args(segments,positions),q,k,v)

def attend_back(own, q, k, v, do, lse, segments, positions, normed, w_qkv, groups):
    rows, width = q.shape
    lanes = 2 * HEAD
    count = 2 ** sum(groups)
    inputs = w_qkv.shape[1]
    step = inputs // count
    blk = pl.BlockSpec((rows, lanes), lambda j: (0, j))
    col = pl.BlockSpec((rows, 1), const_map)
    row = pl.BlockSpec((1, rows), const_map)
    offsets = None
    if step % 16 == 0:
        offsets = [offset for table in offsets_of(groups)[:-1] for offset in table]
        shape = (len(offsets), 3, step, width)
        out_specs = [pl.BlockSpec(shape[:3] + (lanes,), lambda j: (0, 0, 0, j)) for _ in range(2)]
        out_shape = [jax.ShapeDtypeStruct(shape, jnp.bfloat16) for _ in range(2)]
        dw_scratch = pltpu.VMEM((count, step, 3 * lanes), jnp.bfloat16)
    else:
        out_specs = [pl.BlockSpec((3, inputs, lanes), lambda j: (0, 0, j))]
        out_shape = [jax.ShapeDtypeStruct((3, inputs, width), jnp.bfloat16)]
        dw_scratch = pltpu.VMEM((16, lanes), jnp.bfloat16)
    *grads, dh = pl.pallas_call(
        functools.partial(attn_bwd_kernel, offsets),
        grid=(width // lanes,),
        in_specs=[smem_spec(), col, col, row, row, blk, blk, blk, blk]
        + [
            pl.BlockSpec((1, 2, rows), lambda j: (j, 0, 0)),
            pl.BlockSpec((rows, inputs), const_map),
            pl.BlockSpec((3, inputs, lanes), lambda j: (0, 0, j)),
        ],
        out_specs=out_specs + [pl.BlockSpec((rows, inputs), const_map)],
        out_shape=out_shape + [jax.ShapeDtypeStruct((rows, inputs), jnp.float32)],
        scratch_shapes=[
            pltpu.VMEM((rows, rows), jnp.float32),
            pltpu.VMEM((rows, lanes), jnp.float32),
            pltpu.VMEM((rows, lanes), jnp.float32),
            pltpu.VMEM((inputs, rows), jnp.bfloat16),
            dw_scratch,
        ],
        name="attn_bwd",
    )(own[None].astype(jnp.int32), *seg_args(segments, positions), q, k, v, do, lse, normed, w_qkv)
    if offsets is None:
        grads = split(own, [grads[0].reshape(3, count, step, width)], [("stack", 0, 3)], groups)
    return grads[0], grads[1], dh


def adam_update(weight, first_moment, second_moment, gradient, factor, step_rate):
    clipped = gradient * factor
    first_new = first_decay * first_moment + (1.0 - first_decay) * clipped
    second_new = second_decay * second_moment + (1.0 - second_decay) * clipped * clipped
    corrected = first_new / (1.0 - first_decay**STEP)
    spread = second_new / (1.0 - second_decay**STEP)
    weight_new = weight - step_rate * (
        corrected / (jnp.sqrt(spread) + adam_eps) + weight_decay * weight
    )
    return (weight_new, first_new, second_new)


def body(
    groups,
    tokens,
    segments,
    positions,
    cotangent,
    attn_weight,
    attn_m,
    attn_v,
    gate_weight,
    gate_m,
    gate_v,
    in_weight,
    in_m,
    in_v,
    out_weight,
    out_m,
    out_v,
    norm_params,
    norm_m,
    norm_v,
    in_bias,
    bias_m,
    bias_v,
):
    count = 2 ** sum(groups)
    own = lax.axis_index(AXES)
    width = 512
    step = attn_weight.shape[1]
    low = lambda value: value.astype(jnp.bfloat16)
    dot = functools.partial(jnp.einsum, preferred_element_type=jnp.float32)
    columns = lambda value: [value[:, width * j : width * (j + 1)] for j in range(4)]
    small = pad_rows(small_shard(norm_params, in_bias, own, count, width), step)
    extra = small.shape[0]
    first_shard = jnp.concatenate([low(attn_weight[:3]), small])
    second_shard = jnp.concatenate(
        [
            low(attn_weight[3:]),
            low(gate_weight),
            jnp.stack(columns(low(in_weight))),
            low(out_weight).reshape(4, step, width),
        ]
    )
    cut = 6
    orders = plane_orders(groups)
    plane_steps = range(len(orders[0]))
    z_first = gather_z(first_shard, groups)
    z_first, second_shard = tie(z_first, second_shard)
    plane_first = gather_plane(z_first, groups)
    z_second = gather_z(second_shard, groups)
    halves = [z_second[:, :cut], z_second[:, cut:]]
    tied = tie(*halves, z_first, *plane_first)
    halves, z_first, plane_first = tied[:2], tied[2], list(tied[3:])
    core_first = gather_core(z_first, plane_first, groups)
    received = send_halves(halves, orders, 0, groups)
    w_qkv, vectors = place(
        own,
        [z_first] + plane_first + [core_first],
        [(row, 0) for row in offsets_of(groups)],
        [("stack", 0, 3), ("sum", 3, extra)],
        groups,
    )
    w_qkv = w_qkv.reshape(3, count * step, width)
    bias = vectors[7:11].reshape(-1)
    inputs = tokens.astype(jnp.float32)
    normed_full, unit_one, scale_one = normalize_parts(inputs, vectors[0], vectors[1])
    normed = low(normed_full)
    queries, keys, values = [low(dot("td,de->te", normed, w_qkv[j])) for j in range(3)]
    queries, keys, values, *received = tie(queries, keys, values, *received)
    tables = [z_offsets(groups)] * 2
    for position in plane_steps[1:]:
        halves, tables = join_halves(halves, received, tables, orders, position - 1)
        received = send_halves(halves, orders, position, groups)
    mixed_heads, log_total = attend(queries, keys, values, segments, positions)
    mixed_heads, *received = tie(mixed_heads, *received)
    second_step, tables = join_halves(halves, received, tables, orders, plane_steps[-1])
    others = [swap_with(half, 1, count) for half in second_step]
    w_o, w_a, w_f, w_in, w_out = place(
        own,
        list(second_step) + others,
        [(tables[0], 0), (tables[1], cut)]
        + [([offset | 1 for offset in table], first) for table, first in zip(tables, (0, cut))],
        [("stack", 0, 1), ("stack", 1, 1), ("stack", 2, 1), ("columns", 3, 4), ("rows", 7, 4)],
        groups,
    )
    w_o = w_o.reshape(count * step, width)
    w_a = w_a.reshape(count * step, width)
    w_f = w_f.reshape(count * step, width)
    w_in = w_in.reshape(count * step, 4 * width)
    w_out = w_out.reshape(4 * count * step, width)
    attended = dot("td,de->te", mixed_heads, w_o)
    attn_gate = jax.nn.sigmoid(dot("td,de->te", normed, w_a) + vectors[4])
    middle = attn_gate * attended + (1.0 - attn_gate) * inputs
    normed_two_full, unit_two, scale_two = normalize_parts(middle, vectors[2], vectors[3])
    normed_two = low(normed_two_full)
    hidden = dot("td,df->tf", normed_two, w_in) + bias
    active = low(jnp.maximum(hidden, 0.0))
    branch = dot("tf,fd->td", active, w_out) + vectors[6]
    ffn_gate = jax.nn.sigmoid(dot("td,de->te", normed_two, w_f) + vectors[5])
    layer_out = low(ffn_gate * branch + (1.0 - ffn_gate) * middle)
    grad_out = cotangent.astype(jnp.float32)
    grad_branch = grad_out * ffn_gate
    grad_fgate = grad_out * (branch - middle) * ffn_gate * (1.0 - ffn_gate)
    grad_middle = grad_out * (1.0 - ffn_gate)
    branch_low = low(grad_branch)
    grad_w_out = low(dot("tf,td->fd", active, branch_low))
    grad_active = dot("td,fd->tf", branch_low, w_out)
    grad_hidden = jnp.where(hidden > 0.0, grad_active, 0.0)
    hidden_low = low(grad_hidden)
    grad_w_in = low(dot("td,tf->df", normed_two, hidden_low))
    fgate_low = low(grad_fgate)
    grad_w_f = low(dot("td,te->de", normed_two, fgate_low))
    grad_normed_two = dot("tf,df->td", hidden_low, w_in) + dot("te,de->td", fgate_low, w_f)
    grad_gain_two = jnp.sum(grad_normed_two * unit_two, 0)
    grad_shift_two = jnp.sum(grad_normed_two, 0)
    grad_middle = grad_middle + normalize_back(grad_normed_two, unit_two, scale_two, vectors[2])
    grad_attended = grad_middle * attn_gate
    grad_agate = grad_middle * (attended - inputs) * attn_gate * (1.0 - attn_gate)
    grad_inputs = grad_middle * (1.0 - attn_gate)
    attended_low = low(grad_attended)
    grad_w_o = low(dot("td,te->de", mixed_heads, attended_low))
    grad_mixed = low(dot("te,de->td", attended_low, w_o))
    agate_low = low(grad_agate)
    grad_w_a = low(dot("td,te->de", normed, agate_low))
    blocks = lambda value: value.reshape(1, count, step, width)
    kept_b, sent_b = split(
        own,
        [
            blocks(grad_w_o),
            blocks(grad_w_a),
            blocks(grad_w_f),
            grad_w_in.reshape(count, step, 4 * width),
            grad_w_out.reshape(count, 4, step, width),
        ],
        [("stack", 0, 1), ("stack", 1, 1), ("stack", 2, 1), ("columns", 3, 4), ("rows", 7, 4)],
        groups,
    )
    core_b = swap_with(sent_b, 1, count)
    core_b, kept_b, grad_mixed = tie(core_b, kept_b, grad_mixed)
    own_b, parts_b = plane_sums(kept_b, core_b, groups)
    own_b, log_total, *parts_b = tie(own_b, log_total, *parts_b)
    plane_b = plane_send(parts_b, groups)
    kept_a, sent_a, grad_normed = attend_back(
        own, queries, keys, values, grad_mixed, log_total, segments, positions, normed, w_qkv, groups
    )
    kept_a, sent_a, grad_normed, own_b, *plane_b = tie(kept_a, sent_a, grad_normed, own_b, *plane_b)
    core_a = swap_with(sent_a, 1, count)
    own_b, z_b = reduce_z(own_b, plane_b, groups)
    grad_normed = grad_normed + dot("te,de->td", agate_low, w_a)
    grad_gain_one = jnp.sum(grad_normed * unit_one, 0)
    grad_shift_one = jnp.sum(grad_normed, 0)
    grad_inputs = grad_inputs + normalize_back(grad_normed, unit_one, scale_one, vectors[0])
    input_grad = low(grad_inputs)
    own_a, parts_a = plane_sums(kept_a, core_a, groups)
    plane_a = plane_send(parts_a, groups)
    own_a, z_a = reduce_z(own_a, plane_a, groups)
    total_b = reduce_end(own_b, z_b)
    total_a = reduce_end(own_a, z_a)
    local_squares = jnp.sum(total_b * total_b) + jnp.sum(total_a * total_a)
    payload = jnp.stack(
        [
            grad_gain_one,
            grad_shift_one,
            grad_gain_two,
            grad_shift_two,
            jnp.sum(grad_agate, 0),
            jnp.sum(grad_fgate, 0),
            jnp.sum(grad_branch, 0),
        ]
        + list(jnp.sum(grad_hidden, 0).reshape(4, width))
        + [jnp.full((width,), local_squares)]
    )
    payload = sum_all(payload, groups)
    own_small = payload[:11]
    own_vec = lax.dynamic_slice(own_small[:7], (0, own * step), (7, step))
    own_bias = lax.dynamic_slice(own_small[7:11].reshape(-1), (own * 4 * step,), (4 * step,))
    owned = (
        jnp.concatenate([total_a, total_b[:1]]),
        total_b[1:3],
        jnp.concatenate(list(total_b[3:7]), 1),
        total_b[7:].reshape(4 * step, width),
        own_vec,
        own_bias,
    )
    grad_norm = jnp.sqrt(payload[11, 0] + jnp.sum(own_small * own_small))
    factor = jnp.minimum(1.0, clip_norm / (grad_norm + 1e-06))
    states = (
        (attn_weight, attn_m, attn_v),
        (gate_weight, gate_m, gate_v),
        (in_weight, in_m, in_v),
        (out_weight, out_m, out_v),
        (norm_params, norm_m, norm_v),
        (in_bias, bias_m, bias_v),
    )
    step_rates = (learn_rate, learn_rate, learn_rate, learn_rate, vector_rate, vector_rate)
    updated = [
        adam_update(state[0], state[1], state[2], gradient, factor, step_rate)
        for state, gradient, step_rate in zip(states, owned, step_rates)
    ]
    return (
        layer_out,
        input_grad,
        grad_norm,
        updated[0][0],
        updated[0][1],
        updated[0][2],
        updated[1][0],
        updated[1][1],
        updated[1][2],
        updated[2][0],
        updated[2][1],
        updated[2][2],
        updated[3][0],
        updated[3][1],
        updated[3][2],
        updated[4][0],
        updated[4][1],
        updated[4][2],
        updated[5][0],
        updated[5][1],
        updated[5][2],
    )


def solution(mesh):
    return jax.shard_map(
        functools.partial(body, bit_groups(mesh.shape)),
        mesh=mesh,
        in_specs=(
            P(("dp", "inner"), None),
            P(("dp", "inner")),
            P(("dp", "inner")),
            P(("dp", "inner"), None),
            P(None, ("dp", "inner"), None),
            P(None, ("dp", "inner"), None),
            P(None, ("dp", "inner"), None),
            P(None, ("dp", "inner"), None),
            P(None, ("dp", "inner"), None),
            P(None, ("dp", "inner"), None),
            P(("dp", "inner"), None),
            P(("dp", "inner"), None),
            P(("dp", "inner"), None),
            P(("dp", "inner"), None),
            P(("dp", "inner"), None),
            P(("dp", "inner"), None),
            P(None, ("dp", "inner")),
            P(None, ("dp", "inner")),
            P(None, ("dp", "inner")),
            P(("dp", "inner")),
            P(("dp", "inner")),
            P(("dp", "inner")),
        ),
        out_specs=(
            P(("dp", "inner"), None),
            P(("dp", "inner"), None),
            P(),
            P(None, ("dp", "inner"), None),
            P(None, ("dp", "inner"), None),
            P(None, ("dp", "inner"), None),
            P(None, ("dp", "inner"), None),
            P(None, ("dp", "inner"), None),
            P(None, ("dp", "inner"), None),
            P(("dp", "inner"), None),
            P(("dp", "inner"), None),
            P(("dp", "inner"), None),
            P(("dp", "inner"), None),
            P(("dp", "inner"), None),
            P(("dp", "inner"), None),
            P(None, ("dp", "inner")),
            P(None, ("dp", "inner")),
            P(None, ("dp", "inner")),
            P(("dp", "inner")),
            P(("dp", "inner")),
            P(("dp", "inner")),
        ),
        check_vma=False,
    )
```

```python
import functools
import jax
import jax.numpy as jnp
from jax import lax
from jax.experimental import pallas as pl
from jax.experimental.pallas import tpu as pltpu
from jax.sharding import PartitionSpec as P

AXES = ("dp", "inner")
HEADS = 8
HEAD = 64
STEP = 10
LOG2E = 1.4426950408889634
BLOCK = 256


norm_eps = 1e-05
first_decay = 0.9
second_decay = 0.999
adam_eps = 1e-08
learn_rate = 0.05
vector_rate = 0.8
weight_decay = 0.1
clip_norm = 1.0
masked_score = -1e30


def normalize_parts(values, gain_row, bias_row):
    centred = values - jnp.mean(values, -1, keepdims=True)
    spread = jnp.mean(centred * centred, -1, keepdims=True)
    scale_row = lax.rsqrt(spread + norm_eps)
    unit_rows = centred * scale_row
    return (unit_rows * gain_row + bias_row, unit_rows, scale_row)


def normalize_back(grad_rows, unit_rows, scale_row, gain_row):
    grad_unit = grad_rows * gain_row
    return scale_row * (
        grad_unit
        - jnp.mean(grad_unit, -1, keepdims=True)
        - unit_rows * jnp.mean(grad_unit * unit_rows, -1, keepdims=True)
    )


def bit_groups(sizes):
    dp_bits = sizes["dp"].bit_length() - 1
    inner_bits = sizes["inner"].bit_length() - 1
    y_bits = dp_bits // 2
    plane_bits = (inner_bits - 1) + y_bits
    return (1, plane_bits, dp_bits - y_bits)


def swap_with(array, offset, count):
    return lax.ppermute(array, AXES, [(source, source ^ offset) for source in range(count)])


def stage_bits(groups):
    return ((0, groups[0]), (groups[0], groups[1]), (groups[0] + groups[1], groups[2]))


def gather_z(shard, groups):
    count = 2 ** sum(groups)
    first_bit, bits = stage_bits(groups)[2]
    return jnp.stack([shard] + [swap_with(shard, offset << first_bit, count) for offset in range(1, 2**bits)])


def gather_plane(column, groups):
    count = 2 ** sum(groups)
    first_bit, bits = stage_bits(groups)[1]
    return [swap_with(column, offset << first_bit, count) for offset in range(1, 2**bits)]


def gather_core(column, planes, groups):
    return swap_with(jnp.concatenate([column] + planes), 1, 2 ** sum(groups))


def offsets_of(groups):
    (_, _), (plane_bit, plane_bits), (z_bit, z_bits) = stage_bits(groups)
    table = [
        [(plane << plane_bit) | (z << z_bit) for z in range(2**z_bits)] for plane in range(2**plane_bits)
    ]
    return table + [[offset | 1 for row in table for offset in row]]


def plane_orders(groups):
    _, (first_bit, bits), _ = stage_bits(groups)
    order = list(range(first_bit, first_bit + bits))
    return order, order[bits // 2 :] + order[: bits // 2]


def z_offsets(groups):
    _, _, (first_bit, bits) = stage_bits(groups)
    return [z << first_bit for z in range(2**bits)]


def send_halves(arrays, orders, position, groups):
    count = 2 ** sum(groups)
    return [swap_with(array, 1 << order[position], count) for array, order in zip(arrays, orders)]


def join_halves(arrays, received, tables, orders, position):
    arrays = [jnp.concatenate(pair) for pair in zip(arrays, received)]
    tables = [
        table + [offset | (1 << order[position]) for offset in table] for table, order in zip(tables, orders)
    ]
    return arrays, tables


def vmem_spec():
    return pl.BlockSpec(memory_space=pltpu.VMEM)


def smem_spec():
    return pl.BlockSpec(memory_space=pltpu.SMEM)


def matrix_shape(kind, pieces, count, step, width):
    if kind == "stack":
        return (pieces, count, step, width)
    if kind == "rows":
        return (count, pieces, step, width)
    return (count, step, pieces * width)


def place_kernel(tables, layout, own_ref, *refs):
    parts = refs[: len(tables)]
    outs = refs[len(tables) :]
    own = own_ref[0]
    total = None
    where_to = [
        (index, kind, piece) for index, (kind, _, pieces) in enumerate(layout) for piece in range(pieces)
    ]
    for part, (row, first) in zip(parts, tables):
        width = part.shape[3]
        for entry, offset in enumerate(row):
            owner = own ^ offset
            for source in range(part.shape[1]):
                index, kind, piece = where_to[first + source]
                block = part[entry, source]
                if kind == "sum":
                    block = block.astype(jnp.float32)
                    total = block if total is None else total + block
                elif kind == "stack":
                    outs[index][piece, owner] = block
                elif kind == "rows":
                    outs[index][owner, piece] = block
                else:
                    outs[index][owner, :, piece * width : (piece + 1) * width] = block
    for index, (kind, _, _) in enumerate(layout):
        if kind == "sum":
            outs[index][...] = total


def place(own, parts, tables, layout, groups):
    count = 2 ** sum(groups)
    step, width = parts[0].shape[2:]
    if step % 16:
        firsts = sorted({first for _, first in tables})
        groups_of = []
        for first in firsts:
            chosen = [(part, row) for part, (row, base) in zip(parts, tables) if base == first]
            order = jnp.argsort(jnp.array([o for _, row in chosen for o in row]) ^ own)
            groups_of.append(jnp.concatenate([part for part, _ in chosen])[order])
        full = jnp.concatenate(groups_of, 1)
        result = []
        for kind, first, pieces in layout:
            chosen = full[:, first : first + pieces]
            if kind == "sum":
                result.append(jnp.sum(chosen.astype(jnp.float32), 0).reshape(pieces * step, width))
            elif kind == "stack":
                result.append(jnp.moveaxis(chosen, 0, 1))
            elif kind == "rows":
                result.append(chosen)
            else:
                result.append(jnp.moveaxis(chosen, 1, 2).reshape(count, step, pieces * width))
        return result
    shapes = [
        jax.ShapeDtypeStruct((step, width), jnp.float32)
        if kind == "sum"
        else jax.ShapeDtypeStruct(matrix_shape(kind, pieces, count, step, width), jnp.bfloat16)
        for kind, _, pieces in layout
    ]
    return pl.pallas_call(
        functools.partial(place_kernel, tables, layout),
        in_specs=[smem_spec()] + [vmem_spec() for _ in parts],
        out_specs=[vmem_spec() for _ in layout],
        out_shape=shapes,
        name="place",
    )(own[None].astype(jnp.int32), *parts)


def split_kernel(offsets, layout, own_ref, *refs):
    ins = refs[: len(layout)]
    kept, sent = refs[len(layout) :]
    own = own_ref[0]
    for entry, offset in enumerate(offsets):
        for side, target in enumerate((kept, sent)):
            owner = own ^ (offset | side)
            for index, (kind, first, pieces) in enumerate(layout):
                width = target.shape[3]
                for piece in range(pieces):
                    if kind == "sum":
                        block = ins[index][...]
                    elif kind == "stack":
                        block = ins[index][piece, owner]
                    elif kind == "rows":
                        block = ins[index][owner, piece]
                    else:
                        block = ins[index][owner, :, piece * width : (piece + 1) * width]
                    target[entry, first + piece] = block


def split(own, grads, layout, groups):
    count = 2 ** sum(groups)
    width = 512
    total = sum(pieces for _, _, pieces in layout)
    step = grads[0].shape[-2]
    offsets = [offset for row in offsets_of(groups)[:-1] for offset in row]
    if step % 16:
        pieces_of = []
        for grad, (kind, _, pieces) in zip(grads, layout):
            if kind == "sum":
                grad = jnp.broadcast_to(grad.reshape(1, pieces, step, width), (count, pieces, step, width))
            elif kind == "stack":
                grad = jnp.moveaxis(grad, 1, 0)
            elif kind == "columns":
                grad = jnp.moveaxis(grad.reshape(count, step, pieces, width), 2, 1)
            pieces_of.append(grad)
        full = jnp.concatenate(pieces_of, 1)
        order = jnp.array(offsets) ^ own
        return full[order], full[order ^ 1]
    shape = jax.ShapeDtypeStruct((len(offsets), total, step, width), jnp.bfloat16)
    return pl.pallas_call(
        functools.partial(split_kernel, offsets, layout),
        in_specs=[smem_spec()] + [vmem_spec() for _ in grads],
        out_specs=[vmem_spec(), vmem_spec()],
        out_shape=[shape, shape],
        name="split",
    )(own[None].astype(jnp.int32), *grads)


def plane_sums(kept, received, groups):
    _, (_, bits), (_, z_bits) = stage_bits(groups)
    shape = (2**bits, 2**z_bits) + kept.shape[1:]
    kept = kept.reshape(shape)
    received = received.reshape(shape)
    total = lambda offset: kept[offset].astype(jnp.float32) + received[offset].astype(jnp.float32)
    return total(0), [total(offset).astype(jnp.bfloat16) for offset in range(1, 2**bits)]


def plane_send(parts, groups):
    first_bit = stage_bits(groups)[1][0]
    return [swap_with(part, offset << first_bit, 2 ** sum(groups)) for offset, part in enumerate(parts, 1)]


def reduce_z(own_part, arrived, groups):
    count = 2 ** sum(groups)
    first_bit, bits = stage_bits(groups)[2]
    total = lambda z: own_part[z] + sum(part[z].astype(jnp.float32) for part in arrived)
    return total(0), [
        swap_with(total(z).astype(jnp.bfloat16), z << first_bit, count) for z in range(1, 2**bits)
    ]


def reduce_end(own_part, arrived):
    return own_part + sum(part.astype(jnp.float32) for part in arrived)


def sum_all(value, groups):
    for bit in range(sum(groups)):
        value = value + swap_with(value, 1 << bit, 2 ** sum(groups))
    return value


def tie(*values):
    return lax.optimization_barrier(values)


def small_shard(vec, bias, own, count, width):
    step = vec.shape[1]
    lane = lax.broadcasted_iota(jnp.int32, (7, width), 1)
    rows = jnp.where(lane // step == own, jnp.tile(vec, (1, count)), 0.0)
    place_of = lax.broadcasted_iota(jnp.int32, (4, width), 0) * width + lax.broadcasted_iota(
        jnp.int32, (4, width), 1
    )
    tiled = jnp.tile(bias, width // bias.shape[0])[None]
    bias_rows = jnp.where(place_of // bias.shape[0] == own, tiled, 0.0)
    return jnp.concatenate([rows, bias_rows])


def pad_rows(rows, step):
    pieces = -(-rows.shape[0] // step)
    rows = jnp.pad(rows.astype(jnp.bfloat16), ((0, pieces * step - rows.shape[0]), (0, 0)))
    return rows.reshape(pieces, step, rows.shape[1])


def mat(a,b,dims):
    return lax.dot_general(a,b,(dims,((),())),preferred_element_type=jnp.float32)

def fill_bias(bias_ref, seg_col, pos_col, seg_row, pos_row):
    rows=bias_ref.shape[0]
    step=min(BLOCK,rows)
    for first in range(0,rows,step):
        sc=seg_col[first:first+step,:]; pc=pos_col[first:first+step,:]
        sr=seg_row[:,first:]; pr=pos_row[:,first:]
        allowed=(sc==sr)&(pc<=pr)
        bias_ref[first:first+step,first:]=jnp.where(allowed,0.0,masked_score)

def head_lanes(shape, which):
    lane=lax.broadcasted_iota(jnp.int32,shape,1)
    return (lane//HEAD)==which

def attn_fwd_kernel(segc,posc,segr,posr,q_ref,k_ref,v_ref,o_ref,lse_ref,bias_ref):
    @pl.when(pl.program_id(0)==0)
    def _():
        fill_bias(bias_ref,segc,posc,segr,posr)
    rows=q_ref.shape[0]; step=min(BLOCK,rows)
    pair=q_ref.shape[1]//HEAD
    const=HEAD**-0.5*LOG2E
    for first in range(0,rows,step):
        keys=first+step
        q=q_ref[first:keys,:]
        mixed=None
        for which in range(pair):
            own=head_lanes(q.shape,which)
            qh=jnp.where(own,q,jnp.zeros_like(q))
            s=mat(k_ref[:keys,:],qh,((1,),(1,)))*const+bias_ref[:keys,first:keys]
            m=jnp.max(s,0,keepdims=True)
            w=jnp.exp2(s-m)
            total=jnp.sum(w,0,keepdims=True)
            p=(w*(1.0/total)).astype(jnp.bfloat16)
            o=mat(p,v_ref[:keys,:],((0,),(0,)))
            mixed=o if mixed is None else jnp.where(own,o,mixed)
            lse_ref[0,which:which+1,first:keys]=m+jnp.log2(total)
        o_ref[first:keys,:]=mixed.astype(jnp.bfloat16)

def attn_bwd_kernel(
    offsets, own_ref, segc, posc, segr, posr, q_ref, k_ref, v_ref, do_ref, lse_ref, h_ref, w_ref, start_ref, *refs
):
    *outs, dh_ref, bias_ref, dk_acc, dv_acc, ht_ref, dw_ref = refs
    rows = q_ref.shape[0]

    @pl.when(pl.program_id(0) == 0)
    def _():
        fill_bias(bias_ref, segc, posc, segr, posr)
        ht_ref[...] = h_ref[...].T
        dh_ref[...] = start_ref[...]

    step = min(BLOCK, rows)
    pair = q_ref.shape[1] // HEAD
    const = HEAD**-0.5 * LOG2E
    scale = HEAD**-0.5
    dk_acc[...] = jnp.zeros_like(dk_acc)
    dv_acc[...] = jnp.zeros_like(dv_acc)
    dq_parts = []
    for first in range(0, rows, step):
        keys = first + step
        q = q_ref[first:keys, :]
        do = do_ref[first:keys, :]
        dq = None
        for which in range(pair):
            own = head_lanes(q.shape, which)
            qh = jnp.where(own, q, jnp.zeros_like(q))
            doh = jnp.where(own, do, jnp.zeros_like(do))
            s = mat(k_ref[:keys, :], qh, ((1,), (1,)))
            p = jnp.exp2(s * const + (bias_ref[:keys, first:keys] - lse_ref[0, which : which + 1, first:keys]))
            dp = mat(v_ref[:keys, :], doh, ((1,), (1,)))
            inner = jnp.sum(p * dp, 0, keepdims=True)
            ds = (p * (dp - inner)).astype(jnp.bfloat16)
            dv_acc[:keys, :] += mat(p.astype(jnp.bfloat16), doh, ((1,), (0,)))
            dk_acc[:keys, :] += mat(ds, qh, ((1,), (0,)))
            d = mat(ds, k_ref[:keys, :], ((0,), (0,)))
            dq = d if dq is None else jnp.where(own, d, dq)
        dq_parts.append((dq * scale).astype(jnp.bfloat16))
    grads = jnp.concatenate(
        [
            jnp.concatenate(dq_parts, 0),
            (dk_acc[...] * scale).astype(jnp.bfloat16),
            dv_acc[...].astype(jnp.bfloat16),
        ],
        1,
    )
    weights = jnp.concatenate([w_ref[0], w_ref[1], w_ref[2]], 1)
    dh_ref[...] += mat(grads, weights, ((1,), (1,)))
    dw = mat(ht_ref[...], grads, ((1,), (0,))).astype(jnp.bfloat16)
    lanes = q_ref.shape[1]
    if offsets is None:
        for j in range(3):
            outs[0][j] = dw[:, j * lanes : (j + 1) * lanes]
    else:
        dw_ref[...] = dw.reshape(dw_ref.shape)
        for entry, offset in enumerate(offsets):
            for side in range(2):
                owner = own_ref[0] ^ (offset | side)
                for j in range(3):
                    outs[side][entry, j] = dw_ref[owner, :, j * lanes : (j + 1) * lanes]


def const_map(*_): return (0,0)

def seg_args(segments,positions):
    return (segments[:,None],positions[:,None],segments[None],positions[None])

def attend(q,k,v,segments,positions):
    rows,width=q.shape
    pairs=width//128
    blk=pl.BlockSpec((rows,128),lambda j:(0,j))
    col=pl.BlockSpec((rows,1),const_map); row=pl.BlockSpec((1,rows),const_map)
    return pl.pallas_call(attn_fwd_kernel,grid=(pairs,),
        in_specs=[col,col,row,row,blk,blk,blk],
        out_specs=[blk,pl.BlockSpec((1,2,rows),lambda j:(j,0,0))],
        out_shape=[jax.ShapeDtypeStruct((rows,width),jnp.bfloat16),jax.ShapeDtypeStruct((pairs,2,rows),jnp.float32)],
        scratch_shapes=[pltpu.VMEM((rows,rows),jnp.float32)],
        name="attn_fwd",
    )(*seg_args(segments,positions),q,k,v)

def attend_back(own, q, k, v, do, lse, segments, positions, normed, w_qkv, start, groups):
    rows, width = q.shape
    lanes = 2 * HEAD
    count = 2 ** sum(groups)
    inputs = w_qkv.shape[1]
    step = inputs // count
    blk = pl.BlockSpec((rows, lanes), lambda j: (0, j))
    col = pl.BlockSpec((rows, 1), const_map)
    row = pl.BlockSpec((1, rows), const_map)
    offsets = None
    if step % 16 == 0:
        offsets = [offset for table in offsets_of(groups)[:-1] for offset in table]
        shape = (len(offsets), 3, step, width)
        out_specs = [pl.BlockSpec(shape[:3] + (lanes,), lambda j: (0, 0, 0, j)) for _ in range(2)]
        out_shape = [jax.ShapeDtypeStruct(shape, jnp.bfloat16) for _ in range(2)]
        dw_scratch = pltpu.VMEM((count, step, 3 * lanes), jnp.bfloat16)
    else:
        out_specs = [pl.BlockSpec((3, inputs, lanes), lambda j: (0, 0, j))]
        out_shape = [jax.ShapeDtypeStruct((3, inputs, width), jnp.bfloat16)]
        dw_scratch = pltpu.VMEM((16, lanes), jnp.bfloat16)
    *grads, dh = pl.pallas_call(
        functools.partial(attn_bwd_kernel, offsets),
        grid=(width // lanes,),
        in_specs=[smem_spec(), col, col, row, row, blk, blk, blk, blk]
        + [
            pl.BlockSpec((1, 2, rows), lambda j: (j, 0, 0)),
            pl.BlockSpec((rows, inputs), const_map),
            pl.BlockSpec((3, inputs, lanes), lambda j: (0, 0, j)),
            pl.BlockSpec((rows, inputs), const_map),
        ],
        out_specs=out_specs + [pl.BlockSpec((rows, inputs), const_map)],
        out_shape=out_shape + [jax.ShapeDtypeStruct((rows, inputs), jnp.float32)],
        scratch_shapes=[
            pltpu.VMEM((rows, rows), jnp.float32),
            pltpu.VMEM((rows, lanes), jnp.float32),
            pltpu.VMEM((rows, lanes), jnp.float32),
            pltpu.VMEM((inputs, rows), jnp.bfloat16),
            dw_scratch,
        ],
        name="attn_bwd",
    )(own[None].astype(jnp.int32), *seg_args(segments, positions), q, k, v, do, lse, normed, w_qkv, start)
    if offsets is None:
        grads = split(own, [grads[0].reshape(3, count, step, width)], [("stack", 0, 3)], groups)
    return grads[0], grads[1], dh


def copy_parts(tables, layout, own, parts, outs):
    where_to = [
        (index, kind, piece) for index, (kind, _, pieces) in enumerate(layout) for piece in range(pieces)
    ]
    for part, (row, first) in zip(parts, tables):
        width = part.shape[3]
        for entry, offset in enumerate(row):
            owner = own ^ offset
            for source in range(part.shape[1]):
                index, kind, piece = where_to[first + source]
                if kind == "stack":
                    outs[index][owner] = part[entry, source]
                elif kind == "rows":
                    outs[index][owner, piece] = part[entry, source]
                else:
                    outs[index][owner, :, piece * width : (piece + 1) * width] = part[entry, source]


def copy_blocks(offsets, layout, own, ins, kept, sent):
    width = kept.shape[3]
    for entry, offset in enumerate(offsets):
        for side, target in enumerate((kept, sent)):
            owner = own ^ (offset | side)
            for index, (kind, first, pieces) in enumerate(layout):
                for piece in range(pieces):
                    if kind == "stack":
                        block = ins[index][owner]
                    elif kind == "rows":
                        block = ins[index][owner, piece]
                    else:
                        block = ins[index][owner, :, piece * width : (piece + 1) * width]
                    target[entry, first + piece] = block


def ffn_kernel(direct, part_count, tables, offsets, layout, own_ref, x_ref, cot_ref, h_ref, o_ref, vec_ref, bias_ref, *refs):
    low = lambda value: value.astype(jnp.bfloat16)
    parts = refs[:part_count]
    out_count = 6 + (2 if direct else 5)
    outs = refs[part_count : part_count + out_count]
    scratch = refs[part_count + out_count :]
    y_ref, do_ref, dh_ref, dx_ref, dvec_ref, dbias_ref = outs[:6]
    r_ref, dz_ref, h2_ref, df_ref, dzf_ref, da_ref, dza_ref = scratch[:7]
    tile = pl.program_id(0)
    if direct:
        weights = targets = scratch[7:]

        @pl.when(tile == 0)
        def _():
            copy_parts(tables, layout, own_ref[0], parts, weights)

    else:
        weights, targets = parts, outs[6:]
    width = x_ref.shape[1]
    size = x_ref.shape[0]
    chunks = r_ref.shape[0]
    load = lambda index: weights[index][...].reshape(-1, weights[index].shape[-1])
    rows = pl.ds(tile * size, size)

    @pl.when(tile == 0)
    def _():
        dvec_ref[...] = jnp.zeros_like(dvec_ref)
        dbias_ref[...] = jnp.zeros_like(dbias_ref)

    forward = ((1,), (0,))
    backward = ((1,), (1,))
    x = x_ref[...].astype(jnp.float32)
    a = mat(o_ref[rows, :], load(0), forward)
    ga = jax.nn.sigmoid(mat(h_ref[rows, :], load(1), forward) + vec_ref[4:5, :])
    x1 = ga * a + (1.0 - ga) * x
    gain = vec_ref[2:3, :]
    h2_full, n2, s2 = normalize_parts(x1, gain, vec_ref[3:4, :])
    h2 = low(h2_full)
    z = mat(h2, load(3), forward) + bias_ref[...]
    r = low(jnp.maximum(z, 0.0))
    f = mat(r, load(4), forward) + vec_ref[6:7, :]
    gf = jax.nn.sigmoid(mat(h2, load(2), forward) + vec_ref[5:6, :])
    y_ref[...] = low(gf * f + (1.0 - gf) * x1)
    dy = cot_ref[...].astype(jnp.float32)
    df = dy * gf
    dzf = dy * (f - x1) * gf * (1.0 - gf)
    dx1 = dy * (1.0 - gf)
    dfb = low(df)
    dzfb = low(dzf)
    dz = jnp.where(z > 0.0, mat(dfb, load(4), backward), 0.0)
    dzb = low(dz)
    dh2 = mat(dzb, load(3), backward) + mat(dzfb, load(2), backward)
    dx1 = dx1 + normalize_back(dh2, n2, s2, gain)
    da = low(dx1 * ga)
    dza = dx1 * (a - x) * ga * (1.0 - ga)
    dzab = low(dza)
    dx_ref[...] = dx1 * (1.0 - ga)
    do_ref[...] = low(mat(da, load(0), backward))
    dh_ref[...] = mat(dzab, load(1), backward)
    total = lambda value: jnp.sum(value, 0, keepdims=True)
    dvec_ref[0:1, :] += total(dh2 * n2)
    dvec_ref[1:2, :] += total(dh2)
    dvec_ref[2:3, :] += total(dza)
    dvec_ref[3:4, :] += total(dzf)
    dvec_ref[4:5, :] += total(df)
    dbias_ref[...] += total(dz)
    for chunk in range(chunks):
        r_ref[chunk, rows, :] = r[:, chunk * width : (chunk + 1) * width]
        dz_ref[chunk, rows, :] = dzb[:, chunk * width : (chunk + 1) * width]
    h2_ref[rows, :] = h2
    df_ref[rows, :] = dfb
    dzf_ref[rows, :] = dzfb
    da_ref[rows, :] = da
    dza_ref[rows, :] = dzab

    @pl.when(tile == pl.num_programs(0) - 1)
    def _():
        across = lambda left, right: low(mat(left, right, forward))
        targets[0][...] = across(o_ref[...].T, da_ref[...]).reshape(targets[0].shape)
        targets[1][...] = across(h_ref[...].T, dza_ref[...]).reshape(targets[1].shape)
        h2_turned = h2_ref[...].T
        targets[2][...] = across(h2_turned, dzf_ref[...]).reshape(targets[2].shape)
        for chunk in range(chunks):
            lanes = slice(chunk * width, (chunk + 1) * width)
            grad_in = across(h2_turned, dz_ref[chunk])
            grad_out = across(r_ref[chunk].T, df_ref[...])
            if direct:
                owners = targets[4].shape[0] // chunks
                targets[3][:, :, lanes] = grad_in.reshape(targets[3].shape[:2] + (width,))
                targets[4][chunk * owners : (chunk + 1) * owners] = grad_out.reshape(
                    (owners,) + targets[4].shape[1:]
                )
            else:
                targets[3][:, lanes] = grad_in
                targets[4][lanes, :] = grad_out
        if direct:
            copy_blocks(offsets, layout, own_ref[0], targets, *outs[6:])


FFN_LAYOUT = [("stack", 0, 1), ("stack", 1, 1), ("stack", 2, 1), ("columns", 3, 4), ("rows", 7, 4)]


def ffn(own, tokens, cotangent, normed, mixed_heads, vectors, bias, parts, tables, groups):
    rows, width = tokens.shape
    count = 2 ** sum(groups)
    step = parts[0].shape[2]
    hidden = bias.shape[0]
    chunks = hidden // width
    tile = min(256, rows)
    direct = step % 16 == 0
    offsets = [offset for row in offsets_of(groups)[:-1] for offset in row]
    matrices = [(width, width)] * 3 + [(width, hidden), (hidden, width)]
    low = jnp.bfloat16
    once = dict(pipeline_mode=pl.Buffered(1))
    block = pl.BlockSpec((tile, width), lambda i: (i, 0))
    whole = lambda shape: pl.BlockSpec(shape, lambda i: (0,) * len(shape), **once)
    scratch = [pltpu.VMEM((chunks, rows, width), low)] * 2 + [pltpu.VMEM((rows, width), low)] * 5
    if direct:
        shape = (len(offsets), 3 + 2 * chunks, step, width)
        grads = [jax.ShapeDtypeStruct(shape, low)] * 2
        scratch += [pltpu.VMEM((count, step, width), low)] * 3
        scratch += [pltpu.VMEM((count, step, hidden), low), pltpu.VMEM((count, chunks, step, width), low)]
    else:
        placed = place(own, parts, tables, FFN_LAYOUT, groups)
        parts = [weight.reshape(shape) for weight, shape in zip(placed, matrices)]
        grads = [jax.ShapeDtypeStruct(shape, low) for shape in matrices]
    full = jax.ShapeDtypeStruct((rows, width), jnp.float32)
    half = jax.ShapeDtypeStruct((rows, width), low)
    small = [jax.ShapeDtypeStruct((8, width), jnp.float32), jax.ShapeDtypeStruct((1, hidden), jnp.float32)]
    result = pl.pallas_call(
        functools.partial(ffn_kernel, direct, len(parts), tables, offsets, FFN_LAYOUT),
        grid=(rows // tile,),
        in_specs=[smem_spec(), block, block, whole((rows, width)), whole((rows, width))]
        + [whole(vectors.shape), whole((1, hidden))]
        + [whole(part.shape) for part in parts],
        out_specs=[block] * 4 + [whole(item.shape) for item in small + grads],
        out_shape=[half, half, full, full] + small + grads,
        scratch_shapes=scratch,
        name="ffn",
    )(own[None].astype(jnp.int32), tokens, cotangent, normed, mixed_heads, vectors, bias[None], *parts)
    if not direct:
        blocks = [grad.reshape(1, count, step, width) for grad in result[6:9]]
        blocks += [result[9].reshape(count, step, hidden), result[10].reshape(count, chunks, step, width)]
        result = list(result[:6]) + list(split(own, blocks, FFN_LAYOUT, groups))
    return result


def adam_update(weight, first_moment, second_moment, gradient, factor, step_rate):
    clipped = gradient * factor
    first_new = first_decay * first_moment + (1.0 - first_decay) * clipped
    second_new = second_decay * second_moment + (1.0 - second_decay) * clipped * clipped
    corrected = first_new / (1.0 - first_decay**STEP)
    spread = second_new / (1.0 - second_decay**STEP)
    weight_new = weight - step_rate * (
        corrected / (jnp.sqrt(spread) + adam_eps) + weight_decay * weight
    )
    return (weight_new, first_new, second_new)


def body(
    groups,
    tokens,
    segments,
    positions,
    cotangent,
    attn_weight,
    attn_m,
    attn_v,
    gate_weight,
    gate_m,
    gate_v,
    in_weight,
    in_m,
    in_v,
    out_weight,
    out_m,
    out_v,
    norm_params,
    norm_m,
    norm_v,
    in_bias,
    bias_m,
    bias_v,
):
    count = 2 ** sum(groups)
    own = lax.axis_index(AXES)
    width = 512
    step = attn_weight.shape[1]
    low = lambda value: value.astype(jnp.bfloat16)
    dot = functools.partial(jnp.einsum, preferred_element_type=jnp.float32)
    columns = lambda value: [value[:, width * j : width * (j + 1)] for j in range(4)]
    small = pad_rows(small_shard(norm_params, in_bias, own, count, width), step)
    extra = small.shape[0]
    first_shard = jnp.concatenate([low(attn_weight[:3]), small])
    second_shard = jnp.concatenate(
        [
            low(attn_weight[3:]),
            low(gate_weight),
            jnp.stack(columns(low(in_weight))),
            low(out_weight).reshape(4, step, width),
        ]
    )
    cut = 6
    orders = plane_orders(groups)
    plane_steps = range(len(orders[0]))
    z_first = gather_z(first_shard, groups)
    z_first, second_shard = tie(z_first, second_shard)
    plane_first = gather_plane(z_first, groups)
    z_second = gather_z(second_shard, groups)
    halves = [z_second[:, :cut], z_second[:, cut:]]
    tied = tie(*halves, z_first, *plane_first)
    halves, z_first, plane_first = tied[:2], tied[2], list(tied[3:])
    core_first = gather_core(z_first, plane_first, groups)
    received = send_halves(halves, orders, 0, groups)
    w_qkv, vectors = place(
        own,
        [z_first] + plane_first + [core_first],
        [(row, 0) for row in offsets_of(groups)],
        [("stack", 0, 3), ("sum", 3, extra)],
        groups,
    )
    w_qkv = w_qkv.reshape(3, count * step, width)
    bias = vectors[7:11].reshape(-1)
    inputs = tokens.astype(jnp.float32)
    normed_full, unit_one, scale_one = normalize_parts(inputs, vectors[0], vectors[1])
    normed = low(normed_full)
    queries, keys, values = [low(dot("td,de->te", normed, w_qkv[j])) for j in range(3)]
    queries, keys, values, *received = tie(queries, keys, values, *received)
    tables = [z_offsets(groups)] * 2
    for position in plane_steps[1:]:
        halves, tables = join_halves(halves, received, tables, orders, position - 1)
        received = send_halves(halves, orders, position, groups)
    mixed_heads, log_total = attend(queries, keys, values, segments, positions)
    mixed_heads, *received = tie(mixed_heads, *received)
    second_step, tables = join_halves(halves, received, tables, orders, plane_steps[-1])
    others = [swap_with(half, 1, count) for half in second_step]
    layer_out, grad_mixed, grad_normed, grad_inputs, sums, grad_bias, kept_b, sent_b = ffn(
        own,
        tokens,
        cotangent,
        normed,
        mixed_heads,
        vectors,
        bias,
        list(second_step) + others,
        [(tables[0], 0), (tables[1], cut)]
        + [([offset | 1 for offset in table], first) for table, first in zip(tables, (0, cut))],
        groups,
    )
    core_b = swap_with(sent_b, 1, count)
    core_b, kept_b, grad_mixed = tie(core_b, kept_b, grad_mixed)
    own_b, parts_b = plane_sums(kept_b, core_b, groups)
    own_b, log_total, *parts_b = tie(own_b, log_total, *parts_b)
    plane_b = plane_send(parts_b, groups)
    kept_a, sent_a, grad_normed = attend_back(
        own, queries, keys, values, grad_mixed, log_total, segments, positions, normed, w_qkv, grad_normed, groups
    )
    kept_a, sent_a, grad_normed, own_b, *plane_b = tie(kept_a, sent_a, grad_normed, own_b, *plane_b)
    core_a = swap_with(sent_a, 1, count)
    own_b, z_b = reduce_z(own_b, plane_b, groups)
    grad_gain_one = jnp.sum(grad_normed * unit_one, 0)
    grad_shift_one = jnp.sum(grad_normed, 0)
    grad_inputs = grad_inputs + normalize_back(grad_normed, unit_one, scale_one, vectors[0])
    input_grad = low(grad_inputs)
    own_a, parts_a = plane_sums(kept_a, core_a, groups)
    plane_a = plane_send(parts_a, groups)
    own_a, z_a = reduce_z(own_a, plane_a, groups)
    total_b = reduce_end(own_b, z_b)
    total_a = reduce_end(own_a, z_a)
    local_squares = jnp.sum(total_b * total_b) + jnp.sum(total_a * total_a)
    payload = jnp.concatenate(
        [
            grad_gain_one[None],
            grad_shift_one[None],
            sums[:5],
            grad_bias.reshape(4, width),
            jnp.full((1, width), local_squares),
        ]
    )
    payload = sum_all(payload, groups)
    own_small = payload[:11]
    own_vec = lax.dynamic_slice(own_small[:7], (0, own * step), (7, step))
    own_bias = lax.dynamic_slice(own_small[7:11].reshape(-1), (own * 4 * step,), (4 * step,))
    owned = (
        jnp.concatenate([total_a, total_b[:1]]),
        total_b[1:3],
        jnp.concatenate(list(total_b[3:7]), 1),
        total_b[7:].reshape(4 * step, width),
        own_vec,
        own_bias,
    )
    grad_norm = jnp.sqrt(payload[11, 0] + jnp.sum(own_small * own_small))
    factor = jnp.minimum(1.0, clip_norm / (grad_norm + 1e-06))
    states = (
        (attn_weight, attn_m, attn_v),
        (gate_weight, gate_m, gate_v),
        (in_weight, in_m, in_v),
        (out_weight, out_m, out_v),
        (norm_params, norm_m, norm_v),
        (in_bias, bias_m, bias_v),
    )
    step_rates = (learn_rate, learn_rate, learn_rate, learn_rate, vector_rate, vector_rate)
    updated = [
        adam_update(state[0], state[1], state[2], gradient, factor, step_rate)
        for state, gradient, step_rate in zip(states, owned, step_rates)
    ]
    return (
        layer_out,
        input_grad,
        grad_norm,
        updated[0][0],
        updated[0][1],
        updated[0][2],
        updated[1][0],
        updated[1][1],
        updated[1][2],
        updated[2][0],
        updated[2][1],
        updated[2][2],
        updated[3][0],
        updated[3][1],
        updated[3][2],
        updated[4][0],
        updated[4][1],
        updated[4][2],
        updated[5][0],
        updated[5][1],
        updated[5][2],
    )


def solution(mesh):
    return jax.shard_map(
        functools.partial(body, bit_groups(mesh.shape)),
        mesh=mesh,
        in_specs=(
            P(("dp", "inner"), None),
            P(("dp", "inner")),
            P(("dp", "inner")),
            P(("dp", "inner"), None),
            P(None, ("dp", "inner"), None),
            P(None, ("dp", "inner"), None),
            P(None, ("dp", "inner"), None),
            P(None, ("dp", "inner"), None),
            P(None, ("dp", "inner"), None),
            P(None, ("dp", "inner"), None),
            P(("dp", "inner"), None),
            P(("dp", "inner"), None),
            P(("dp", "inner"), None),
            P(("dp", "inner"), None),
            P(("dp", "inner"), None),
            P(("dp", "inner"), None),
            P(None, ("dp", "inner")),
            P(None, ("dp", "inner")),
            P(None, ("dp", "inner")),
            P(("dp", "inner")),
            P(("dp", "inner")),
            P(("dp", "inner")),
        ),
        out_specs=(
            P(("dp", "inner"), None),
            P(("dp", "inner"), None),
            P(),
            P(None, ("dp", "inner"), None),
            P(None, ("dp", "inner"), None),
            P(None, ("dp", "inner"), None),
            P(None, ("dp", "inner"), None),
            P(None, ("dp", "inner"), None),
            P(None, ("dp", "inner"), None),
            P(("dp", "inner"), None),
            P(("dp", "inner"), None),
            P(("dp", "inner"), None),
            P(("dp", "inner"), None),
            P(("dp", "inner"), None),
            P(("dp", "inner"), None),
            P(None, ("dp", "inner")),
            P(None, ("dp", "inner")),
            P(None, ("dp", "inner")),
            P(("dp", "inner")),
            P(("dp", "inner")),
            P(("dp", "inner")),
        ),
        check_vma=False,
    )
```

```python
import functools
import jax
import jax.numpy as jnp
from jax import lax
from jax.experimental import pallas as pl
from jax.experimental.pallas import tpu as pltpu
from jax.sharding import PartitionSpec as P

AXES = ("dp", "inner")
HEADS = 8
HEAD = 64
STEP = 10
LOG2E = 1.4426950408889634
BLOCK = 256


norm_eps = 1e-05
first_decay = 0.9
second_decay = 0.999
adam_eps = 1e-08
learn_rate = 0.05
vector_rate = 0.8
weight_decay = 0.1
clip_norm = 1.0
masked_score = -1e30


def normalize_parts(values, gain_row, bias_row):
    centred = values - jnp.mean(values, -1, keepdims=True)
    spread = jnp.mean(centred * centred, -1, keepdims=True)
    scale_row = lax.rsqrt(spread + norm_eps)
    unit_rows = centred * scale_row
    return (unit_rows * gain_row + bias_row, unit_rows, scale_row)


def normalize_back(grad_rows, unit_rows, scale_row, gain_row):
    grad_unit = grad_rows * gain_row
    return scale_row * (
        grad_unit
        - jnp.mean(grad_unit, -1, keepdims=True)
        - unit_rows * jnp.mean(grad_unit * unit_rows, -1, keepdims=True)
    )


def bit_groups(sizes):
    dp_bits = sizes["dp"].bit_length() - 1
    inner_bits = sizes["inner"].bit_length() - 1
    y_bits = dp_bits // 2
    plane_bits = (inner_bits - 1) + y_bits
    return (1, plane_bits, dp_bits - y_bits)


def swap_with(array, offset, count):
    return lax.ppermute(array, AXES, [(source, source ^ offset) for source in range(count)])


def stage_bits(groups):
    return ((0, groups[0]), (groups[0], groups[1]), (groups[0] + groups[1], groups[2]))


def gather_z(shard, groups):
    count = 2 ** sum(groups)
    first_bit, bits = stage_bits(groups)[2]
    return jnp.stack([shard] + [swap_with(shard, offset << first_bit, count) for offset in range(1, 2**bits)])


def gather_plane(column, groups):
    count = 2 ** sum(groups)
    first_bit, bits = stage_bits(groups)[1]
    return [swap_with(column, offset << first_bit, count) for offset in range(1, 2**bits)]


def gather_core(column, planes, groups):
    return swap_with(jnp.concatenate([column] + planes), 1, 2 ** sum(groups))


def offsets_of(groups):
    (_, _), (plane_bit, plane_bits), (z_bit, z_bits) = stage_bits(groups)
    table = [
        [(plane << plane_bit) | (z << z_bit) for z in range(2**z_bits)] for plane in range(2**plane_bits)
    ]
    return table + [[offset | 1 for row in table for offset in row]]


def plane_orders(groups):
    _, (first_bit, bits), _ = stage_bits(groups)
    order = list(range(first_bit, first_bit + bits))
    return order, order[bits // 2 :] + order[: bits // 2]


def z_offsets(groups):
    _, _, (first_bit, bits) = stage_bits(groups)
    return [z << first_bit for z in range(2**bits)]


def send_halves(arrays, orders, position, groups):
    count = 2 ** sum(groups)
    return [swap_with(array, 1 << order[position], count) for array, order in zip(arrays, orders)]


def join_halves(arrays, received, tables, orders, position):
    arrays = [jnp.concatenate(pair) for pair in zip(arrays, received)]
    tables = [
        table + [offset | (1 << order[position]) for offset in table] for table, order in zip(tables, orders)
    ]
    return arrays, tables


def vmem_spec():
    return pl.BlockSpec(memory_space=pltpu.VMEM)


def smem_spec():
    return pl.BlockSpec(memory_space=pltpu.SMEM)


def matrix_shape(kind, pieces, count, step, width):
    if kind == "stack":
        return (pieces, count, step, width)
    if kind == "rows":
        return (count, pieces, step, width)
    return (count, step, pieces * width)


def place_kernel(tables, layout, own_ref, *refs):
    parts = refs[: len(tables)]
    outs = refs[len(tables) :]
    own = own_ref[0]
    total = None
    where_to = [
        (index, kind, piece) for index, (kind, _, pieces) in enumerate(layout) for piece in range(pieces)
    ]
    for part, (row, first) in zip(parts, tables):
        width = part.shape[3]
        for entry, offset in enumerate(row):
            owner = own ^ offset
            for source in range(part.shape[1]):
                index, kind, piece = where_to[first + source]
                block = part[entry, source]
                if kind == "sum":
                    block = block.astype(jnp.float32)
                    total = block if total is None else total + block
                elif kind == "stack":
                    outs[index][piece, owner] = block
                elif kind == "rows":
                    outs[index][owner, piece] = block
                else:
                    outs[index][owner, :, piece * width : (piece + 1) * width] = block
    for index, (kind, _, _) in enumerate(layout):
        if kind == "sum":
            outs[index][...] = total


def place(own, parts, tables, layout, groups):
    count = 2 ** sum(groups)
    step, width = parts[0].shape[2:]
    if step % 16:
        firsts = sorted({first for _, first in tables})
        groups_of = []
        for first in firsts:
            chosen = [(part, row) for part, (row, base) in zip(parts, tables) if base == first]
            order = jnp.argsort(jnp.array([o for _, row in chosen for o in row]) ^ own)
            groups_of.append(jnp.concatenate([part for part, _ in chosen])[order])
        full = jnp.concatenate(groups_of, 1)
        result = []
        for kind, first, pieces in layout:
            chosen = full[:, first : first + pieces]
            if kind == "sum":
                result.append(jnp.sum(chosen.astype(jnp.float32), 0).reshape(pieces * step, width))
            elif kind == "stack":
                result.append(jnp.moveaxis(chosen, 0, 1))
            elif kind == "rows":
                result.append(chosen)
            else:
                result.append(jnp.moveaxis(chosen, 1, 2).reshape(count, step, pieces * width))
        return result
    shapes = [
        jax.ShapeDtypeStruct((step, width), jnp.float32)
        if kind == "sum"
        else jax.ShapeDtypeStruct(matrix_shape(kind, pieces, count, step, width), jnp.bfloat16)
        for kind, _, pieces in layout
    ]
    return pl.pallas_call(
        functools.partial(place_kernel, tables, layout),
        in_specs=[smem_spec()] + [vmem_spec() for _ in parts],
        out_specs=[vmem_spec() for _ in layout],
        out_shape=shapes,
        name="place",
    )(own[None].astype(jnp.int32), *parts)


def split_kernel(offsets, layout, own_ref, *refs):
    ins = refs[: len(layout)]
    kept, sent = refs[len(layout) :]
    own = own_ref[0]
    for entry, offset in enumerate(offsets):
        for side, target in enumerate((kept, sent)):
            owner = own ^ (offset | side)
            for index, (kind, first, pieces) in enumerate(layout):
                width = target.shape[3]
                for piece in range(pieces):
                    if kind == "sum":
                        block = ins[index][...]
                    elif kind == "stack":
                        block = ins[index][piece, owner]
                    elif kind == "rows":
                        block = ins[index][owner, piece]
                    else:
                        block = ins[index][owner, :, piece * width : (piece + 1) * width]
                    target[entry, first + piece] = block


def split(own, grads, layout, groups):
    count = 2 ** sum(groups)
    width = 512
    total = sum(pieces for _, _, pieces in layout)
    step = grads[0].shape[-2]
    offsets = [offset for row in offsets_of(groups)[:-1] for offset in row]
    if step % 16:
        pieces_of = []
        for grad, (kind, _, pieces) in zip(grads, layout):
            if kind == "sum":
                grad = jnp.broadcast_to(grad.reshape(1, pieces, step, width), (count, pieces, step, width))
            elif kind == "stack":
                grad = jnp.moveaxis(grad, 1, 0)
            elif kind == "columns":
                grad = jnp.moveaxis(grad.reshape(count, step, pieces, width), 2, 1)
            pieces_of.append(grad)
        full = jnp.concatenate(pieces_of, 1)
        order = jnp.array(offsets) ^ own
        return full[order], full[order ^ 1]
    shape = jax.ShapeDtypeStruct((len(offsets), total, step, width), jnp.bfloat16)
    return pl.pallas_call(
        functools.partial(split_kernel, offsets, layout),
        in_specs=[smem_spec()] + [vmem_spec() for _ in grads],
        out_specs=[vmem_spec(), vmem_spec()],
        out_shape=[shape, shape],
        name="split",
    )(own[None].astype(jnp.int32), *grads)


def plane_sums(kept, received, groups):
    _, (_, bits), (_, z_bits) = stage_bits(groups)
    shape = (2**bits, 2**z_bits) + kept.shape[1:]
    kept = kept.reshape(shape)
    received = received.reshape(shape)
    total = lambda offset: kept[offset].astype(jnp.float32) + received[offset].astype(jnp.float32)
    return total(0), [total(offset).astype(jnp.bfloat16) for offset in range(1, 2**bits)]


def plane_send(parts, groups):
    first_bit = stage_bits(groups)[1][0]
    return [swap_with(part, offset << first_bit, 2 ** sum(groups)) for offset, part in enumerate(parts, 1)]


def reduce_z(own_part, arrived, groups):
    count = 2 ** sum(groups)
    first_bit, bits = stage_bits(groups)[2]
    total = lambda z: own_part[z] + sum(part[z].astype(jnp.float32) for part in arrived)
    return total(0), [
        swap_with(total(z).astype(jnp.bfloat16), z << first_bit, count) for z in range(1, 2**bits)
    ]


def reduce_end(own_part, arrived):
    return own_part + sum(part.astype(jnp.float32) for part in arrived)


def sum_all(value, groups):
    for bit in range(sum(groups)):
        value = value + swap_with(value, 1 << bit, 2 ** sum(groups))
    return value


def tie(*values):
    return lax.optimization_barrier(values)


def small_shard(vec, bias, own, count, width):
    step = vec.shape[1]
    lane = lax.broadcasted_iota(jnp.int32, (7, width), 1)
    rows = jnp.where(lane // step == own, jnp.tile(vec, (1, count)), 0.0)
    place_of = lax.broadcasted_iota(jnp.int32, (4, width), 0) * width + lax.broadcasted_iota(
        jnp.int32, (4, width), 1
    )
    tiled = jnp.tile(bias, width // bias.shape[0])[None]
    bias_rows = jnp.where(place_of // bias.shape[0] == own, tiled, 0.0)
    return jnp.concatenate([rows, bias_rows])


def pad_rows(rows, step):
    pieces = -(-rows.shape[0] // step)
    rows = jnp.pad(rows.astype(jnp.bfloat16), ((0, pieces * step - rows.shape[0]), (0, 0)))
    return rows.reshape(pieces, step, rows.shape[1])


def mat(a,b,dims):
    return lax.dot_general(a,b,(dims,((),())),preferred_element_type=jnp.float32)

def fill_bias(bias_ref, seg_col, pos_col, seg_row, pos_row):
    rows=bias_ref.shape[0]
    step=min(BLOCK,rows)
    for first in range(0,rows,step):
        sc=seg_col[first:first+step,:]; pc=pos_col[first:first+step,:]
        sr=seg_row[:,first:]; pr=pos_row[:,first:]
        allowed=(sc==sr)&(pc<=pr)
        bias_ref[first:first+step,first:]=jnp.where(allowed,0.0,masked_score)

def head_lanes(shape, which):
    lane=lax.broadcasted_iota(jnp.int32,shape,1)
    return (lane//HEAD)==which

def attn_fwd_kernel(segc,posc,segr,posr,q_ref,k_ref,v_ref,o_ref,lse_ref,bias_ref):
    @pl.when(pl.program_id(0)==0)
    def _():
        fill_bias(bias_ref,segc,posc,segr,posr)
    rows=q_ref.shape[0]; step=min(BLOCK,rows)
    pair=q_ref.shape[1]//HEAD
    const=HEAD**-0.5*LOG2E
    for first in range(0,rows,step):
        keys=first+step
        q=q_ref[first:keys,:]
        mixed=None
        for which in range(pair):
            own=head_lanes(q.shape,which)
            qh=jnp.where(own,q,jnp.zeros_like(q))
            s=mat(k_ref[:keys,:],qh,((1,),(1,)))*const+bias_ref[:keys,first:keys]
            m=jnp.max(s,0,keepdims=True)
            w=jnp.exp2(s-m)
            total=jnp.sum(w,0,keepdims=True)
            p=(w*(1.0/total)).astype(jnp.bfloat16)
            o=mat(p,v_ref[:keys,:],((0,),(0,)))
            mixed=o if mixed is None else jnp.where(own,o,mixed)
            lse_ref[0,which:which+1,first:keys]=m+jnp.log2(total)
        o_ref[first:keys,:]=mixed.astype(jnp.bfloat16)

def attn_bwd_kernel(
    offsets, own_ref, segc, posc, segr, posr, q_ref, k_ref, v_ref, do_ref, lse_ref, h_ref, w_ref, start_ref, *refs
):
    *outs, dh_ref, bias_ref, dk_acc, dv_acc, ht_ref, dw_ref = refs
    rows = q_ref.shape[0]

    @pl.when(pl.program_id(0) == 0)
    def _():
        fill_bias(bias_ref, segc, posc, segr, posr)
        ht_ref[...] = h_ref[...].T
        dh_ref[...] = start_ref[...]

    step = min(BLOCK, rows)
    pair = q_ref.shape[1] // HEAD
    const = HEAD**-0.5 * LOG2E
    scale = HEAD**-0.5
    dk_acc[...] = jnp.zeros_like(dk_acc)
    dv_acc[...] = jnp.zeros_like(dv_acc)
    dq_parts = []
    for first in range(0, rows, step):
        keys = first + step
        q = q_ref[first:keys, :]
        do = do_ref[first:keys, :]
        dq = None
        for which in range(pair):
            own = head_lanes(q.shape, which)
            qh = jnp.where(own, q, jnp.zeros_like(q))
            doh = jnp.where(own, do, jnp.zeros_like(do))
            s = mat(k_ref[:keys, :], qh, ((1,), (1,)))
            p = jnp.exp2(s * const + (bias_ref[:keys, first:keys] - lse_ref[0, which : which + 1, first:keys]))
            dp = mat(v_ref[:keys, :], doh, ((1,), (1,)))
            inner = jnp.sum(p * dp, 0, keepdims=True)
            ds = (p * (dp - inner)).astype(jnp.bfloat16)
            dv_acc[:keys, :] += mat(p.astype(jnp.bfloat16), doh, ((1,), (0,)))
            dk_acc[:keys, :] += mat(ds, qh, ((1,), (0,)))
            d = mat(ds, k_ref[:keys, :], ((0,), (0,)))
            dq = d if dq is None else jnp.where(own, d, dq)
        dq_parts.append((dq * scale).astype(jnp.bfloat16))
    grads = jnp.concatenate(
        [
            jnp.concatenate(dq_parts, 0),
            (dk_acc[...] * scale).astype(jnp.bfloat16),
            dv_acc[...].astype(jnp.bfloat16),
        ],
        1,
    )
    weights = jnp.concatenate([w_ref[0], w_ref[1], w_ref[2]], 1)
    dh_ref[...] += mat(grads, weights, ((1,), (1,)))
    dw = mat(ht_ref[...], grads, ((1,), (0,))).astype(jnp.bfloat16)
    lanes = q_ref.shape[1]
    if offsets is None:
        for j in range(3):
            outs[0][j] = dw[:, j * lanes : (j + 1) * lanes]
    else:
        dw_ref[...] = dw.reshape(dw_ref.shape)
        for entry, offset in enumerate(offsets):
            for side in range(2):
                owner = own_ref[0] ^ (offset | side)
                for j in range(3):
                    outs[side][entry, j] = dw_ref[owner, :, j * lanes : (j + 1) * lanes]


def const_map(*_): return (0,0)

def seg_args(segments,positions):
    return (segments[:,None],positions[:,None],segments[None],positions[None])

def attend(q,k,v,segments,positions):
    rows,width=q.shape
    pairs=width//128
    blk=pl.BlockSpec((rows,128),lambda j:(0,j))
    col=pl.BlockSpec((rows,1),const_map); row=pl.BlockSpec((1,rows),const_map)
    return pl.pallas_call(attn_fwd_kernel,grid=(pairs,),
        in_specs=[col,col,row,row,blk,blk,blk],
        out_specs=[blk,pl.BlockSpec((1,2,rows),lambda j:(j,0,0))],
        out_shape=[jax.ShapeDtypeStruct((rows,width),jnp.bfloat16),jax.ShapeDtypeStruct((pairs,2,rows),jnp.float32)],
        scratch_shapes=[pltpu.VMEM((rows,rows),jnp.float32)],
        name="attn_fwd",
    )(*seg_args(segments,positions),q,k,v)

def attend_back(own, q, k, v, do, lse, segments, positions, normed, w_qkv, start, groups):
    rows, width = q.shape
    lanes = 2 * HEAD
    count = 2 ** sum(groups)
    inputs = w_qkv.shape[1]
    step = inputs // count
    blk = pl.BlockSpec((rows, lanes), lambda j: (0, j))
    col = pl.BlockSpec((rows, 1), const_map)
    row = pl.BlockSpec((1, rows), const_map)
    offsets = None
    if step % 16 == 0:
        offsets = [offset for table in offsets_of(groups)[:-1] for offset in table]
        shape = (len(offsets), 3, step, width)
        out_specs = [pl.BlockSpec(shape[:3] + (lanes,), lambda j: (0, 0, 0, j)) for _ in range(2)]
        out_shape = [jax.ShapeDtypeStruct(shape, jnp.bfloat16) for _ in range(2)]
        dw_scratch = pltpu.VMEM((count, step, 3 * lanes), jnp.bfloat16)
    else:
        out_specs = [pl.BlockSpec((3, inputs, lanes), lambda j: (0, 0, j))]
        out_shape = [jax.ShapeDtypeStruct((3, inputs, width), jnp.bfloat16)]
        dw_scratch = pltpu.VMEM((16, lanes), jnp.bfloat16)
    *grads, dh = pl.pallas_call(
        functools.partial(attn_bwd_kernel, offsets),
        grid=(width // lanes,),
        in_specs=[smem_spec(), col, col, row, row, blk, blk, blk, blk]
        + [
            pl.BlockSpec((1, 2, rows), lambda j: (j, 0, 0)),
            pl.BlockSpec((rows, inputs), const_map),
            pl.BlockSpec((3, inputs, lanes), lambda j: (0, 0, j)),
            pl.BlockSpec((rows, inputs), const_map),
        ],
        out_specs=out_specs + [pl.BlockSpec((rows, inputs), const_map)],
        out_shape=out_shape + [jax.ShapeDtypeStruct((rows, inputs), jnp.float32)],
        scratch_shapes=[
            pltpu.VMEM((rows, rows), jnp.float32),
            pltpu.VMEM((rows, lanes), jnp.float32),
            pltpu.VMEM((rows, lanes), jnp.float32),
            pltpu.VMEM((inputs, rows), jnp.bfloat16),
            dw_scratch,
        ],
        name="attn_bwd",
    )(own[None].astype(jnp.int32), *seg_args(segments, positions), q, k, v, do, lse, normed, w_qkv, start)
    if offsets is None:
        grads = split(own, [grads[0].reshape(3, count, step, width)], [("stack", 0, 3)], groups)
    return grads[0], grads[1], dh


def copy_parts(tables, layout, own, parts, outs):
    where_to = [
        (index, kind, piece) for index, (kind, _, pieces) in enumerate(layout) for piece in range(pieces)
    ]
    for part, (row, first) in zip(parts, tables):
        width = part.shape[3]
        for entry, offset in enumerate(row):
            owner = own ^ offset
            for source in range(part.shape[1]):
                index, kind, piece = where_to[first + source]
                if kind == "stack":
                    outs[index][owner] = part[entry, source]
                elif kind == "rows":
                    outs[index][owner, piece] = part[entry, source]
                else:
                    outs[index][owner, :, piece * width : (piece + 1) * width] = part[entry, source]


def copy_blocks(offsets, layout, own, ins, kept, sent):
    width = kept.shape[3]
    for entry, offset in enumerate(offsets):
        for side, target in enumerate((kept, sent)):
            owner = own ^ (offset | side)
            for index, (kind, first, pieces) in enumerate(layout):
                for piece in range(pieces):
                    if kind == "stack":
                        block = ins[index][owner]
                    elif kind == "rows":
                        block = ins[index][owner, piece]
                    else:
                        block = ins[index][owner, :, piece * width : (piece + 1) * width]
                    target[entry, first + piece] = block


def ffn_kernel(direct, part_count, tables, offsets, layout, own_ref, x_ref, cot_ref, h_ref, o_ref, vec_ref, bias_ref, *refs):
    low = lambda value: value.astype(jnp.bfloat16)
    parts = refs[:part_count]
    out_count = 6 + (2 if direct else 5)
    outs = refs[part_count : part_count + out_count]
    scratch = refs[part_count + out_count :]
    y_ref, do_ref, dh_ref, dx_ref, dvec_ref, dbias_ref = outs[:6]
    r_ref, dz_ref, h2_ref, df_ref, dzf_ref, da_ref, dza_ref = scratch[:7]
    tile = pl.program_id(0)
    if direct:
        weights = targets = scratch[7:]

        @pl.when(tile == 0)
        def _():
            copy_parts(tables, layout, own_ref[0], parts, weights)

    else:
        weights, targets = parts, outs[6:]
    width = x_ref.shape[1]
    size = x_ref.shape[0]
    chunks = r_ref.shape[0]
    load = lambda index: weights[index][...].reshape(-1, weights[index].shape[-1])
    rows = pl.ds(tile * size, size)

    @pl.when(tile == 0)
    def _():
        dvec_ref[...] = jnp.zeros_like(dvec_ref)
        dbias_ref[...] = jnp.zeros_like(dbias_ref)

    forward = ((1,), (0,))
    backward = ((1,), (1,))
    x = x_ref[...].astype(jnp.float32)
    a = mat(o_ref[rows, :], load(0), forward)
    ga = jax.nn.sigmoid(mat(h_ref[rows, :], load(1), forward) + vec_ref[4:5, :])
    x1 = ga * a + (1.0 - ga) * x
    gain = vec_ref[2:3, :]
    h2_full, n2, s2 = normalize_parts(x1, gain, vec_ref[3:4, :])
    h2 = low(h2_full)
    z = mat(h2, load(3), forward) + bias_ref[...]
    r = low(jnp.maximum(z, 0.0))
    f = mat(r, load(4), forward) + vec_ref[6:7, :]
    gf = jax.nn.sigmoid(mat(h2, load(2), forward) + vec_ref[5:6, :])
    y_ref[...] = low(gf * f + (1.0 - gf) * x1)
    dy = cot_ref[...].astype(jnp.float32)
    df = dy * gf
    dzf = dy * (f - x1) * gf * (1.0 - gf)
    dx1 = dy * (1.0 - gf)
    dfb = low(df)
    dzfb = low(dzf)
    dz = jnp.where(z > 0.0, mat(dfb, load(4), backward), 0.0)
    dzb = low(dz)
    dh2 = mat(dzb, load(3), backward) + mat(dzfb, load(2), backward)
    dx1 = dx1 + normalize_back(dh2, n2, s2, gain)
    da = low(dx1 * ga)
    dza = dx1 * (a - x) * ga * (1.0 - ga)
    dzab = low(dza)
    dx_ref[...] = dx1 * (1.0 - ga)
    do_ref[...] = low(mat(da, load(0), backward))
    dh_ref[...] = mat(dzab, load(1), backward)
    total = lambda value: jnp.sum(value, 0, keepdims=True)
    dvec_ref[0:1, :] += total(dh2 * n2)
    dvec_ref[1:2, :] += total(dh2)
    dvec_ref[2:3, :] += total(dza)
    dvec_ref[3:4, :] += total(dzf)
    dvec_ref[4:5, :] += total(df)
    dbias_ref[...] += total(dz)
    for chunk in range(chunks):
        r_ref[chunk, rows, :] = r[:, chunk * width : (chunk + 1) * width]
        dz_ref[chunk, rows, :] = dzb[:, chunk * width : (chunk + 1) * width]
    h2_ref[rows, :] = h2
    df_ref[rows, :] = dfb
    dzf_ref[rows, :] = dzfb
    da_ref[rows, :] = da
    dza_ref[rows, :] = dzab

    @pl.when(tile == pl.num_programs(0) - 1)
    def _():
        across = lambda left, right: low(mat(left, right, forward))
        targets[0][...] = across(o_ref[...].T, da_ref[...]).reshape(targets[0].shape)
        targets[1][...] = across(h_ref[...].T, dza_ref[...]).reshape(targets[1].shape)
        h2_turned = h2_ref[...].T
        targets[2][...] = across(h2_turned, dzf_ref[...]).reshape(targets[2].shape)
        for chunk in range(chunks):
            lanes = slice(chunk * width, (chunk + 1) * width)
            grad_in = across(h2_turned, dz_ref[chunk])
            grad_out = across(r_ref[chunk].T, df_ref[...])
            if direct:
                owners = targets[4].shape[0] // chunks
                targets[3][:, :, lanes] = grad_in.reshape(targets[3].shape[:2] + (width,))
                targets[4][chunk * owners : (chunk + 1) * owners] = grad_out.reshape(
                    (owners,) + targets[4].shape[1:]
                )
            else:
                targets[3][:, lanes] = grad_in
                targets[4][lanes, :] = grad_out
        if direct:
            copy_blocks(offsets, layout, own_ref[0], targets, *outs[6:])


FFN_LAYOUT = [("stack", 0, 1), ("stack", 1, 1), ("stack", 2, 1), ("columns", 3, 4), ("rows", 7, 4)]


def ffn(own, tokens, cotangent, normed, mixed_heads, vectors, bias, parts, tables, groups):
    rows, width = tokens.shape
    count = 2 ** sum(groups)
    step = parts[0].shape[2]
    hidden = bias.shape[0]
    chunks = hidden // width
    tile = min(256, rows)
    direct = step % 16 == 0
    offsets = [offset for row in offsets_of(groups)[:-1] for offset in row]
    matrices = [(width, width)] * 3 + [(width, hidden), (hidden, width)]
    low = jnp.bfloat16
    once = dict(pipeline_mode=pl.Buffered(1))
    block = pl.BlockSpec((tile, width), lambda i: (i, 0))
    whole = lambda shape: pl.BlockSpec(shape, lambda i: (0,) * len(shape), **once)
    scratch = [pltpu.VMEM((chunks, rows, width), low)] * 2 + [pltpu.VMEM((rows, width), low)] * 5
    if direct:
        shape = (len(offsets), 3 + 2 * chunks, step, width)
        grads = [jax.ShapeDtypeStruct(shape, low)] * 2
        scratch += [pltpu.VMEM((count, step, width), low)] * 3
        scratch += [pltpu.VMEM((count, step, hidden), low), pltpu.VMEM((count, chunks, step, width), low)]
    else:
        placed = place(own, parts, tables, FFN_LAYOUT, groups)
        parts = [weight.reshape(shape) for weight, shape in zip(placed, matrices)]
        grads = [jax.ShapeDtypeStruct(shape, low) for shape in matrices]
    full = jax.ShapeDtypeStruct((rows, width), jnp.float32)
    half = jax.ShapeDtypeStruct((rows, width), low)
    small = [jax.ShapeDtypeStruct((8, width), jnp.float32), jax.ShapeDtypeStruct((1, hidden), jnp.float32)]
    result = pl.pallas_call(
        functools.partial(ffn_kernel, direct, len(parts), tables, offsets, FFN_LAYOUT),
        grid=(rows // tile,),
        in_specs=[smem_spec(), block, block, whole((rows, width)), whole((rows, width))]
        + [whole(vectors.shape), whole((1, hidden))]
        + [whole(part.shape) for part in parts],
        out_specs=[block] * 4 + [whole(item.shape) for item in small + grads],
        out_shape=[half, half, full, full] + small + grads,
        scratch_shapes=scratch,
        name="ffn",
    )(own[None].astype(jnp.int32), tokens, cotangent, normed, mixed_heads, vectors, bias[None], *parts)
    if not direct:
        blocks = [grad.reshape(1, count, step, width) for grad in result[6:9]]
        blocks += [result[9].reshape(count, step, hidden), result[10].reshape(count, chunks, step, width)]
        result = list(result[:6]) + list(split(own, blocks, FFN_LAYOUT, groups))
    return result


def adam_update(weight, first_moment, second_moment, gradient, factor, step_rate):
    clipped = gradient * factor
    first_new = first_decay * first_moment + (1.0 - first_decay) * clipped
    second_new = second_decay * second_moment + (1.0 - second_decay) * clipped * clipped
    corrected = first_new / (1.0 - first_decay**STEP)
    spread = second_new / (1.0 - second_decay**STEP)
    weight_new = weight - step_rate * (
        corrected / (jnp.sqrt(spread) + adam_eps) + weight_decay * weight
    )
    return (weight_new, first_new, second_new)


def own_lanes(rows, first, lanes):
    width = rows.shape[1]
    return pltpu.roll(rows, (width - first) % width, 1)[:, :lanes]


def update_kernel(own_ref, payload_ref, a_ref, b_ref, *refs):
    states = [refs[3 * index : 3 * index + 3] for index in range(6)]
    norm_ref = refs[18]
    news = [refs[19 + 3 * index : 22 + 3 * index] for index in range(6)]
    squares = payload_ref[:11, :] * payload_ref[:11, :]
    total = jnp.sum(jnp.sum(squares, 1, keepdims=True), 0, keepdims=True)
    norm = jnp.sqrt(total + payload_ref[11:12, 0:1])
    norm_ref[...] = norm
    factor = jnp.minimum(1.0, clip_norm / (norm + 1e-06))

    def update(index, where, gradient):
        rate = vector_rate if index > 3 else learn_rate
        values = adam_update(*[ref[where] for ref in states[index]], gradient, factor, rate)
        for ref, value in zip(news[index], values):
            ref[where] = value

    width = a_ref.shape[2]
    for piece in range(3):
        update(0, piece, a_ref[piece])
    update(0, 3, b_ref[0])
    for piece in range(2):
        update(1, piece, b_ref[1 + piece])
    chunks = (b_ref.shape[0] - 3) // 2
    step = b_ref.shape[1]
    for chunk in range(chunks):
        update(2, (slice(None), slice(chunk * width, (chunk + 1) * width)), b_ref[3 + chunk])
        update(3, slice(chunk * step, (chunk + 1) * step), b_ref[3 + chunks + chunk])
    own = own_ref[0]
    vec_lanes = states[4][0].shape[1]
    update(4, Ellipsis, own_lanes(payload_ref[0:8, :], own * vec_lanes, vec_lanes)[:7])
    bias_lanes = states[5][0].shape[1]
    first = own * bias_lanes
    line = lax.broadcasted_iota(jnp.int32, (5, width), 0)
    picked = jnp.sum(jnp.where(line == first // width, payload_ref[7:12, :], 0.0), 0, keepdims=True)
    picked = own_lanes(jnp.broadcast_to(picked, (8, width)), first % width, bias_lanes)
    update(5, Ellipsis, picked[0:1])


def update_all(own, payload, total_a, total_b, states):
    flat = [value for state in states for value in state]
    shapes = [jax.ShapeDtypeStruct(value.shape, jnp.float32) for value in flat]
    norm, *news = pl.pallas_call(
        update_kernel,
        in_specs=[smem_spec()] + [vmem_spec() for _ in range(3 + len(flat))],
        out_specs=[vmem_spec() for _ in range(1 + len(flat))],
        out_shape=[jax.ShapeDtypeStruct((1, 1), jnp.float32)] + shapes,
        name="update",
    )(own[None].astype(jnp.int32), payload, total_a, total_b, *flat)
    return norm[0, 0], [news[3 * index : 3 * index + 3] for index in range(len(states))]


def body(
    groups,
    tokens,
    segments,
    positions,
    cotangent,
    attn_weight,
    attn_m,
    attn_v,
    gate_weight,
    gate_m,
    gate_v,
    in_weight,
    in_m,
    in_v,
    out_weight,
    out_m,
    out_v,
    norm_params,
    norm_m,
    norm_v,
    in_bias,
    bias_m,
    bias_v,
):
    count = 2 ** sum(groups)
    own = lax.axis_index(AXES)
    width = 512
    step = attn_weight.shape[1]
    low = lambda value: value.astype(jnp.bfloat16)
    dot = functools.partial(jnp.einsum, preferred_element_type=jnp.float32)
    columns = lambda value: [value[:, width * j : width * (j + 1)] for j in range(4)]
    small = pad_rows(small_shard(norm_params, in_bias, own, count, width), step)
    extra = small.shape[0]
    first_shard = jnp.concatenate([low(attn_weight[:3]), small])
    second_shard = jnp.concatenate(
        [
            low(attn_weight[3:]),
            low(gate_weight),
            jnp.stack(columns(low(in_weight))),
            low(out_weight).reshape(4, step, width),
        ]
    )
    cut = 6
    orders = plane_orders(groups)
    plane_steps = range(len(orders[0]))
    z_first = gather_z(first_shard, groups)
    z_first, second_shard = tie(z_first, second_shard)
    plane_first = gather_plane(z_first, groups)
    z_second = gather_z(second_shard, groups)
    halves = [z_second[:, :cut], z_second[:, cut:]]
    tied = tie(*halves, z_first, *plane_first)
    halves, z_first, plane_first = tied[:2], tied[2], list(tied[3:])
    core_first = gather_core(z_first, plane_first, groups)
    received = send_halves(halves, orders, 0, groups)
    w_qkv, vectors = place(
        own,
        [z_first] + plane_first + [core_first],
        [(row, 0) for row in offsets_of(groups)],
        [("stack", 0, 3), ("sum", 3, extra)],
        groups,
    )
    w_qkv = w_qkv.reshape(3, count * step, width)
    bias = vectors[7:11].reshape(-1)
    inputs = tokens.astype(jnp.float32)
    normed_full, unit_one, scale_one = normalize_parts(inputs, vectors[0], vectors[1])
    normed = low(normed_full)
    queries, keys, values = [low(dot("td,de->te", normed, w_qkv[j])) for j in range(3)]
    queries, keys, values, *received = tie(queries, keys, values, *received)
    tables = [z_offsets(groups)] * 2
    for position in plane_steps[1:]:
        halves, tables = join_halves(halves, received, tables, orders, position - 1)
        received = send_halves(halves, orders, position, groups)
    mixed_heads, log_total = attend(queries, keys, values, segments, positions)
    mixed_heads, *received = tie(mixed_heads, *received)
    second_step, tables = join_halves(halves, received, tables, orders, plane_steps[-1])
    others = [swap_with(half, 1, count) for half in second_step]
    layer_out, grad_mixed, grad_normed, grad_inputs, sums, grad_bias, kept_b, sent_b = ffn(
        own,
        tokens,
        cotangent,
        normed,
        mixed_heads,
        vectors,
        bias,
        list(second_step) + others,
        [(tables[0], 0), (tables[1], cut)]
        + [([offset | 1 for offset in table], first) for table, first in zip(tables, (0, cut))],
        groups,
    )
    core_b = swap_with(sent_b, 1, count)
    core_b, kept_b, grad_mixed = tie(core_b, kept_b, grad_mixed)
    own_b, parts_b = plane_sums(kept_b, core_b, groups)
    own_b, log_total, *parts_b = tie(own_b, log_total, *parts_b)
    plane_b = plane_send(parts_b, groups)
    kept_a, sent_a, grad_normed = attend_back(
        own, queries, keys, values, grad_mixed, log_total, segments, positions, normed, w_qkv, grad_normed, groups
    )
    kept_a, sent_a, grad_normed, own_b, *plane_b = tie(kept_a, sent_a, grad_normed, own_b, *plane_b)
    core_a = swap_with(sent_a, 1, count)
    own_b, z_b = reduce_z(own_b, plane_b, groups)
    own_a, parts_a = plane_sums(kept_a, core_a, groups)
    grad_normed, own_a, *parts_a = tie(grad_normed, own_a, *parts_a)
    grad_gain_one = jnp.sum(grad_normed * unit_one, 0)
    grad_shift_one = jnp.sum(grad_normed, 0)
    grad_inputs = grad_inputs + normalize_back(grad_normed, unit_one, scale_one, vectors[0])
    input_grad = low(grad_inputs)
    plane_a = plane_send(parts_a, groups)
    input_grad, grad_gain_one, grad_shift_one, *arrived = tie(
        input_grad, grad_gain_one, grad_shift_one, *z_b, *plane_a
    )
    z_b, plane_a = arrived[: len(z_b)], arrived[len(z_b) :]
    own_a, z_a = reduce_z(own_a, plane_a, groups)
    total_b = reduce_end(own_b, z_b)
    total_a = reduce_end(own_a, z_a)
    local_squares = jnp.sum(total_b * total_b) + jnp.sum(total_a * total_a)
    payload = jnp.concatenate(
        [
            grad_gain_one[None],
            grad_shift_one[None],
            sums[:5],
            grad_bias.reshape(4, width),
            jnp.full((1, width), local_squares),
        ]
    )
    payload = sum_all(payload, groups)
    states = (
        (attn_weight, attn_m, attn_v),
        (gate_weight, gate_m, gate_v),
        (in_weight, in_m, in_v),
        (out_weight, out_m, out_v),
        (norm_params, norm_m, norm_v),
        (in_bias[None], bias_m[None], bias_v[None]),
    )
    grad_norm, updated = update_all(own, payload, total_a, total_b, states)
    return (
        layer_out,
        input_grad,
        grad_norm,
        updated[0][0],
        updated[0][1],
        updated[0][2],
        updated[1][0],
        updated[1][1],
        updated[1][2],
        updated[2][0],
        updated[2][1],
        updated[2][2],
        updated[3][0],
        updated[3][1],
        updated[3][2],
        updated[4][0],
        updated[4][1],
        updated[4][2],
        updated[5][0][0],
        updated[5][1][0],
        updated[5][2][0],
    )


def solution(mesh):
    return jax.shard_map(
        functools.partial(body, bit_groups(mesh.shape)),
        mesh=mesh,
        in_specs=(
            P(("dp", "inner"), None),
            P(("dp", "inner")),
            P(("dp", "inner")),
            P(("dp", "inner"), None),
            P(None, ("dp", "inner"), None),
            P(None, ("dp", "inner"), None),
            P(None, ("dp", "inner"), None),
            P(None, ("dp", "inner"), None),
            P(None, ("dp", "inner"), None),
            P(None, ("dp", "inner"), None),
            P(("dp", "inner"), None),
            P(("dp", "inner"), None),
            P(("dp", "inner"), None),
            P(("dp", "inner"), None),
            P(("dp", "inner"), None),
            P(("dp", "inner"), None),
            P(None, ("dp", "inner")),
            P(None, ("dp", "inner")),
            P(None, ("dp", "inner")),
            P(("dp", "inner")),
            P(("dp", "inner")),
            P(("dp", "inner")),
        ),
        out_specs=(
            P(("dp", "inner"), None),
            P(("dp", "inner"), None),
            P(),
            P(None, ("dp", "inner"), None),
            P(None, ("dp", "inner"), None),
            P(None, ("dp", "inner"), None),
            P(None, ("dp", "inner"), None),
            P(None, ("dp", "inner"), None),
            P(None, ("dp", "inner"), None),
            P(("dp", "inner"), None),
            P(("dp", "inner"), None),
            P(("dp", "inner"), None),
            P(("dp", "inner"), None),
            P(("dp", "inner"), None),
            P(("dp", "inner"), None),
            P(None, ("dp", "inner")),
            P(None, ("dp", "inner")),
            P(None, ("dp", "inner")),
            P(("dp", "inner")),
            P(("dp", "inner")),
            P(("dp", "inner")),
        ),
        check_vma=False,
    )
```

```python
import functools
import jax
import jax.numpy as jnp
from jax import lax
from jax.experimental import pallas as pl
from jax.experimental.pallas import tpu as pltpu
from jax.sharding import PartitionSpec as P

AXES = ("dp", "inner")
HEADS = 8
HEAD = 64
STEP = 10
LOG2E = 1.4426950408889634
BLOCK = 256


norm_eps = 1e-05
first_decay = 0.9
second_decay = 0.999
adam_eps = 1e-08
learn_rate = 0.05
vector_rate = 0.8
weight_decay = 0.1
clip_norm = 1.0
masked_score = -1e30


def normalize_parts(values, gain_row, bias_row):
    centred = values - jnp.mean(values, -1, keepdims=True)
    spread = jnp.mean(centred * centred, -1, keepdims=True)
    scale_row = lax.rsqrt(spread + norm_eps)
    unit_rows = centred * scale_row
    return (unit_rows * gain_row + bias_row, unit_rows, scale_row)


def normalize_back(grad_rows, unit_rows, scale_row, gain_row):
    grad_unit = grad_rows * gain_row
    return scale_row * (
        grad_unit
        - jnp.mean(grad_unit, -1, keepdims=True)
        - unit_rows * jnp.mean(grad_unit * unit_rows, -1, keepdims=True)
    )


def bit_groups(sizes):
    dp_bits = sizes["dp"].bit_length() - 1
    inner_bits = sizes["inner"].bit_length() - 1
    y_bits = dp_bits // 2
    plane_bits = (inner_bits - 1) + y_bits
    return (1, plane_bits, dp_bits - y_bits)


def swap_with(array, offset, count):
    return lax.ppermute(array, AXES, [(source, source ^ offset) for source in range(count)])


def stage_bits(groups):
    return ((0, groups[0]), (groups[0], groups[1]), (groups[0] + groups[1], groups[2]))


def gather_z(shard, groups):
    count = 2 ** sum(groups)
    first_bit, bits = stage_bits(groups)[2]
    return jnp.stack([shard] + [swap_with(shard, offset << first_bit, count) for offset in range(1, 2**bits)])


def gather_plane(column, groups):
    count = 2 ** sum(groups)
    first_bit, bits = stage_bits(groups)[1]
    return [swap_with(column, offset << first_bit, count) for offset in range(1, 2**bits)]


def gather_core(column, planes, groups):
    return swap_with(jnp.concatenate([column] + planes), 1, 2 ** sum(groups))


def offsets_of(groups):
    (_, _), (plane_bit, plane_bits), (z_bit, z_bits) = stage_bits(groups)
    table = [
        [(plane << plane_bit) | (z << z_bit) for z in range(2**z_bits)] for plane in range(2**plane_bits)
    ]
    return table + [[offset | 1 for row in table for offset in row]]


def vmem_spec():
    return pl.BlockSpec(memory_space=pltpu.VMEM)


def smem_spec():
    return pl.BlockSpec(memory_space=pltpu.SMEM)


def place(own, parts, tables, layout, groups):
    count = 2 ** sum(groups)
    step, width = parts[0].shape[2:]
    firsts = sorted({first for _, first in tables})
    groups_of = []
    for first in firsts:
        chosen = [(part, row) for part, (row, base) in zip(parts, tables) if base == first]
        order = jnp.argsort(jnp.array([o for _, row in chosen for o in row]) ^ own)
        groups_of.append(jnp.concatenate([part for part, _ in chosen])[order])
    full = jnp.concatenate(groups_of, 1)
    result = []
    for kind, first, pieces in layout:
        chosen = full[:, first : first + pieces]
        if kind == "sum":
            result.append(jnp.sum(chosen.astype(jnp.float32), 0).reshape(pieces * step, width))
        elif kind == "stack":
            result.append(jnp.moveaxis(chosen, 0, 1))
        elif kind == "rows":
            result.append(chosen)
        else:
            result.append(jnp.moveaxis(chosen, 1, 2).reshape(count, step, pieces * width))
    return result


def split(own, grads, layout, groups):
    count = 2 ** sum(groups)
    width = 512
    step = grads[0].shape[-2]
    offsets = [offset for row in offsets_of(groups)[:-1] for offset in row]
    pieces_of = []
    for grad, (kind, _, pieces) in zip(grads, layout):
        if kind == "stack":
            grad = jnp.moveaxis(grad, 1, 0)
        elif kind == "columns":
            grad = jnp.moveaxis(grad.reshape(count, step, pieces, width), 2, 1)
        pieces_of.append(grad)
    full = jnp.concatenate(pieces_of, 1)
    order = jnp.array(offsets) ^ own
    return full[order], full[order ^ 1]


def plane_sums(kept, received, groups):
    _, (_, bits), (_, z_bits) = stage_bits(groups)
    shape = (2**bits, 2**z_bits) + kept.shape[1:]
    kept = kept.reshape(shape)
    received = received.reshape(shape)
    total = lambda offset: kept[offset].astype(jnp.float32) + received[offset].astype(jnp.float32)
    return total(0), [total(offset).astype(jnp.bfloat16) for offset in range(1, 2**bits)]


def plane_send(parts, groups):
    first_bit = stage_bits(groups)[1][0]
    return [swap_with(part, offset << first_bit, 2 ** sum(groups)) for offset, part in enumerate(parts, 1)]


def reduce_z(own_part, arrived, groups):
    count = 2 ** sum(groups)
    first_bit, bits = stage_bits(groups)[2]
    total = lambda z: own_part[z] + sum(part[z].astype(jnp.float32) for part in arrived)
    return total(0), [
        swap_with(total(z).astype(jnp.bfloat16), z << first_bit, count) for z in range(1, 2**bits)
    ]


def reduce_end(own_part, arrived):
    return own_part + sum(part.astype(jnp.float32) for part in arrived)


def sum_all(value, groups):
    for bit in range(sum(groups)):
        value = value + swap_with(value, 1 << bit, 2 ** sum(groups))
    return value


def tie(*values):
    return lax.optimization_barrier(values)


def small_shard(vec, bias, own, count, width):
    step = vec.shape[1]
    lane = lax.broadcasted_iota(jnp.int32, (7, width), 1)
    rows = jnp.where(lane // step == own, jnp.tile(vec, (1, count)), 0.0)
    place_of = lax.broadcasted_iota(jnp.int32, (4, width), 0) * width + lax.broadcasted_iota(
        jnp.int32, (4, width), 1
    )
    tiled = jnp.tile(bias, width // bias.shape[0])[None]
    bias_rows = jnp.where(place_of // bias.shape[0] == own, tiled, 0.0)
    return jnp.concatenate([rows, bias_rows])


def pad_rows(rows, step):
    pieces = -(-rows.shape[0] // step)
    rows = jnp.pad(rows.astype(jnp.bfloat16), ((0, pieces * step - rows.shape[0]), (0, 0)))
    return rows.reshape(pieces, step, rows.shape[1])


def mat(a,b,dims):
    return lax.dot_general(a,b,(dims,((),())),preferred_element_type=jnp.float32)

def fill_bias(bias_ref, seg_col, pos_col, seg_row, pos_row):
    rows=bias_ref.shape[0]
    step=min(BLOCK,rows)
    for first in range(0,rows,step):
        sc=seg_col[first:first+step,:]; pc=pos_col[first:first+step,:]
        sr=seg_row[:,first:]; pr=pos_row[:,first:]
        allowed=(sc==sr)&(pc<=pr)
        bias_ref[first:first+step,first:]=jnp.where(allowed,0.0,masked_score)

def head_lanes(shape, which):
    lane=lax.broadcasted_iota(jnp.int32,shape,1)
    return (lane//HEAD)==which

def attn_fwd_kernel(direct, tables, layout, own_ref, segc, posc, segr, posr, x_ref, *refs):
    part_count = len(tables) if direct else 2
    parts = refs[:part_count]
    h_ref, q_ref, k_ref, v_ref, o_ref, lse_ref, *rest = refs[part_count:]
    bias_ref, q_all, k_all, v_all = rest[-4:]
    rows = x_ref.shape[0]
    step = min(BLOCK, rows)
    lanes = q_ref.shape[1]
    pair = lanes // HEAD
    const = HEAD**-0.5 * LOG2E
    low = lambda value: value.astype(jnp.bfloat16)
    weights, vectors = rest[:2] if direct else parts
    tile = pl.program_id(0)

    @pl.when(tile == 0)
    def _():
        if direct:
            copy_parts(tables, layout, own_ref[0], parts, [weights, vectors])
        fill_bias(bias_ref, segc, posc, segr, posr)
        for first in range(0, rows, step):
            x = x_ref[first : first + step, :].astype(jnp.float32)
            h_ref[first : first + step, :] = low(normalize_parts(x, vectors[0:1, :], vectors[1:2, :])[0])
        for j, target in enumerate((q_all, k_all, v_all)):
            whole = low(mat(h_ref[...], weights[j].reshape(-1, weights.shape[-1]), ((1,), (0,))))
            for which in range(target.shape[0]):
                target[which] = whole[:, which * lanes : (which + 1) * lanes]

    q_ref[...] = q_all[tile]
    k_ref[...] = k_all[tile]
    v_ref[...] = v_all[tile]
    for first in range(0, rows, step):
        keys = first + step
        q = q_ref[first:keys, :]
        mixed = None
        for which in range(pair):
            own = head_lanes(q.shape, which)
            qh = jnp.where(own, q, jnp.zeros_like(q))
            s = mat(k_ref[:keys, :], qh, ((1,), (1,))) * const + bias_ref[:keys, first:keys]
            m = jnp.max(s, 0, keepdims=True)
            w = jnp.exp2(s - m)
            total = jnp.sum(w, 0, keepdims=True)
            p = (w * (1.0 / total)).astype(jnp.bfloat16)
            o = mat(p, v_ref[:keys, :], ((0,), (0,)))
            mixed = o if mixed is None else jnp.where(own, o, mixed)
            lse_ref[0, which : which + 1, first:keys] = m + jnp.log2(total)
        o_ref[first:keys, :] = mixed.astype(jnp.bfloat16)


def attn_bwd_kernel(
    offsets, own_ref, segc, posc, segr, posr, q_ref, k_ref, v_ref, do_ref, lse_ref, h_ref, w_ref, start_ref, *refs
):
    *outs, dh_ref, bias_ref, dk_acc, dv_acc, ht_ref, dw_ref = refs
    rows = q_ref.shape[0]

    @pl.when(pl.program_id(0) == 0)
    def _():
        fill_bias(bias_ref, segc, posc, segr, posr)
        ht_ref[...] = h_ref[...].T
        dh_ref[...] = start_ref[...]

    step = min(BLOCK, rows)
    pair = q_ref.shape[1] // HEAD
    const = HEAD**-0.5 * LOG2E
    scale = HEAD**-0.5
    dk_acc[...] = jnp.zeros_like(dk_acc)
    dv_acc[...] = jnp.zeros_like(dv_acc)
    dq_parts = []
    for first in range(0, rows, step):
        keys = first + step
        q = q_ref[first:keys, :]
        do = do_ref[first:keys, :]
        dq = None
        for which in range(pair):
            own = head_lanes(q.shape, which)
            qh = jnp.where(own, q, jnp.zeros_like(q))
            doh = jnp.where(own, do, jnp.zeros_like(do))
            s = mat(k_ref[:keys, :], qh, ((1,), (1,)))
            p = jnp.exp2(s * const + (bias_ref[:keys, first:keys] - lse_ref[0, which : which + 1, first:keys]))
            dp = mat(v_ref[:keys, :], doh, ((1,), (1,)))
            inner = jnp.sum(p * dp, 0, keepdims=True)
            ds = (p * (dp - inner)).astype(jnp.bfloat16)
            dv_acc[:keys, :] += mat(p.astype(jnp.bfloat16), doh, ((1,), (0,)))
            dk_acc[:keys, :] += mat(ds, qh, ((1,), (0,)))
            d = mat(ds, k_ref[:keys, :], ((0,), (0,)))
            dq = d if dq is None else jnp.where(own, d, dq)
        dq_parts.append((dq * scale).astype(jnp.bfloat16))
    grads = jnp.concatenate(
        [
            jnp.concatenate(dq_parts, 0),
            (dk_acc[...] * scale).astype(jnp.bfloat16),
            dv_acc[...].astype(jnp.bfloat16),
        ],
        1,
    )
    weights = jnp.concatenate([w_ref[0], w_ref[1], w_ref[2]], 1)
    dh_ref[...] += mat(grads, weights, ((1,), (1,)))
    dw = mat(ht_ref[...], grads, ((1,), (0,))).astype(jnp.bfloat16)
    lanes = q_ref.shape[1]
    if offsets is None:
        for j in range(3):
            outs[0][j] = dw[:, j * lanes : (j + 1) * lanes]
    else:
        dw_ref[...] = dw.reshape(dw_ref.shape)
        for entry, offset in enumerate(offsets):
            for side in range(2):
                owner = own_ref[0] ^ (offset | side)
                for j in range(3):
                    outs[side][entry, j] = dw_ref[owner, :, j * lanes : (j + 1) * lanes]


def const_map(*_): return (0,0)

def seg_args(segments,positions):
    return (segments[:,None],positions[:,None],segments[None],positions[None])

def attend(own, tokens, segments, positions, parts, tables, layout, groups):
    rows, width = tokens.shape
    count = 2 ** sum(groups)
    step = parts[0].shape[2]
    lanes = 2 * HEAD
    pairs = width // lanes
    low = jnp.bfloat16
    direct = step % 16 == 0
    blk = pl.BlockSpec((rows, lanes), lambda j: (0, j))
    whole = lambda shape: pl.BlockSpec(shape, lambda j: (0,) * len(shape), pipeline_mode=pl.Buffered(1))
    half = jax.ShapeDtypeStruct((rows, width), low)
    out_shape = [half] * 5 + [jax.ShapeDtypeStruct((pairs, 2, rows), jnp.float32)]
    out_specs = [whole((rows, width)), blk, blk, blk, blk, pl.BlockSpec((1, 2, rows), lambda j: (j, 0, 0))]
    if direct:
        extra = [
            jax.ShapeDtypeStruct((3, count, step, width), low),
            jax.ShapeDtypeStruct((step, width), jnp.float32),
        ]
        out_shape += extra
        out_specs += [whole(item.shape) for item in extra]
    else:
        parts = place(own, parts, tables, layout, groups)
    result = pl.pallas_call(
        functools.partial(attn_fwd_kernel, direct, tables, layout),
        grid=(pairs,),
        in_specs=[smem_spec(), whole((rows, 1)), whole((rows, 1)), whole((1, rows)), whole((1, rows))]
        + [whole((rows, width))]
        + [whole(part.shape) for part in parts],
        out_specs=out_specs,
        out_shape=out_shape,
        scratch_shapes=[pltpu.VMEM((rows, rows), jnp.float32)] + [pltpu.VMEM((pairs, rows, lanes), low)] * 3,
        name="attn_fwd",
    )(own[None].astype(jnp.int32), *seg_args(segments, positions), tokens, *parts)
    if not direct:
        result = list(result) + list(parts)
    return result


def attend_back(own, q, k, v, do, lse, segments, positions, normed, w_qkv, start, groups):
    rows, width = q.shape
    lanes = 2 * HEAD
    count = 2 ** sum(groups)
    inputs = w_qkv.shape[1]
    step = inputs // count
    blk = pl.BlockSpec((rows, lanes), lambda j: (0, j))
    col = pl.BlockSpec((rows, 1), const_map)
    row = pl.BlockSpec((1, rows), const_map)
    offsets = None
    if step % 16 == 0:
        offsets = [offset for table in offsets_of(groups)[:-1] for offset in table]
        shape = (len(offsets), 3, step, width)
        out_specs = [pl.BlockSpec(shape[:3] + (lanes,), lambda j: (0, 0, 0, j)) for _ in range(2)]
        out_shape = [jax.ShapeDtypeStruct(shape, jnp.bfloat16) for _ in range(2)]
        dw_scratch = pltpu.VMEM((count, step, 3 * lanes), jnp.bfloat16)
    else:
        out_specs = [pl.BlockSpec((3, inputs, lanes), lambda j: (0, 0, j))]
        out_shape = [jax.ShapeDtypeStruct((3, inputs, width), jnp.bfloat16)]
        dw_scratch = pltpu.VMEM((16, lanes), jnp.bfloat16)
    *grads, dh = pl.pallas_call(
        functools.partial(attn_bwd_kernel, offsets),
        grid=(width // lanes,),
        in_specs=[smem_spec(), col, col, row, row, blk, blk, blk, blk]
        + [
            pl.BlockSpec((1, 2, rows), lambda j: (j, 0, 0)),
            pl.BlockSpec((rows, inputs), const_map),
            pl.BlockSpec((3, inputs, lanes), lambda j: (0, 0, j)),
            pl.BlockSpec((rows, inputs), const_map),
        ],
        out_specs=out_specs + [pl.BlockSpec((rows, inputs), const_map)],
        out_shape=out_shape + [jax.ShapeDtypeStruct((rows, inputs), jnp.float32)],
        scratch_shapes=[
            pltpu.VMEM((rows, rows), jnp.float32),
            pltpu.VMEM((rows, lanes), jnp.float32),
            pltpu.VMEM((rows, lanes), jnp.float32),
            pltpu.VMEM((inputs, rows), jnp.bfloat16),
            dw_scratch,
        ],
        name="attn_bwd",
    )(own[None].astype(jnp.int32), *seg_args(segments, positions), q, k, v, do, lse, normed, w_qkv, start)
    if offsets is None:
        grads = split(own, [grads[0].reshape(3, count, step, width)], [("stack", 0, 3)], groups)
    return grads[0], grads[1], dh


def copy_parts(tables, layout, own, parts, outs):
    where_to = [
        (index, kind, piece) for index, (kind, _, pieces) in enumerate(layout) for piece in range(pieces)
    ]
    total = None
    for part, (row, first) in zip(parts, tables):
        width = part.shape[3]
        for entry, offset in enumerate(row):
            owner = own ^ offset
            for source in range(part.shape[1]):
                index, kind, piece = where_to[first + source]
                block = part[entry, source]
                if kind == "sum":
                    block = block.astype(jnp.float32)
                    total = block if total is None else total + block
                elif kind == "stack":
                    outs[index][piece, owner] = block
                elif kind == "rows":
                    outs[index][owner, piece] = block
                else:
                    outs[index][owner, :, piece * width : (piece + 1) * width] = block
    for index, (kind, _, _) in enumerate(layout):
        if kind == "sum":
            outs[index][...] = total


def copy_blocks(offsets, layout, own, ins, kept, sent):
    width = kept.shape[3]
    for entry, offset in enumerate(offsets):
        for side, target in enumerate((kept, sent)):
            owner = own ^ (offset | side)
            for index, (kind, first, pieces) in enumerate(layout):
                for piece in range(pieces):
                    if kind == "stack":
                        block = ins[index][piece, owner]
                    elif kind == "rows":
                        block = ins[index][owner, piece]
                    else:
                        block = ins[index][owner, :, piece * width : (piece + 1) * width]
                    target[entry, first + piece] = block


def ffn_kernel(direct, part_count, tables, offsets, layout, own_ref, x_ref, cot_ref, h_ref, o_ref, vec_ref, bias_ref, *refs):
    low = lambda value: value.astype(jnp.bfloat16)
    parts = refs[:part_count]
    out_count = 6 + (2 if direct else 5)
    outs = refs[part_count : part_count + out_count]
    scratch = refs[part_count + out_count :]
    y_ref, do_ref, dh_ref, dx_ref, dvec_ref, dbias_ref = outs[:6]
    r_ref, dz_ref, h2_ref, df_ref, dzf_ref, da_ref, dza_ref = scratch[:7]
    tile = pl.program_id(0)
    if direct:
        weights = targets = scratch[7:]

        @pl.when(tile == 0)
        def _():
            copy_parts(tables, layout, own_ref[0], parts, weights)

    else:
        weights, targets = parts, outs[6:]
    width = x_ref.shape[1]
    size = x_ref.shape[0]
    chunks = r_ref.shape[0]
    load = lambda index: weights[index][...].reshape(-1, weights[index].shape[-1])
    rows = pl.ds(tile * size, size)

    @pl.when(tile == 0)
    def _():
        dvec_ref[...] = jnp.zeros_like(dvec_ref)
        dbias_ref[...] = jnp.zeros_like(dbias_ref)

    forward = ((1,), (0,))
    backward = ((1,), (1,))
    x = x_ref[...].astype(jnp.float32)
    a = mat(o_ref[rows, :], load(0), forward)
    ga = jax.nn.sigmoid(mat(h_ref[rows, :], load(1), forward) + vec_ref[4:5, :])
    x1 = ga * a + (1.0 - ga) * x
    gain = vec_ref[2:3, :]
    h2_full, n2, s2 = normalize_parts(x1, gain, vec_ref[3:4, :])
    h2 = low(h2_full)
    z = mat(h2, load(3), forward) + bias_ref[...]
    r = low(jnp.maximum(z, 0.0))
    f = mat(r, load(4), forward) + vec_ref[6:7, :]
    gf = jax.nn.sigmoid(mat(h2, load(2), forward) + vec_ref[5:6, :])
    y_ref[...] = low(gf * f + (1.0 - gf) * x1)
    dy = cot_ref[...].astype(jnp.float32)
    df = dy * gf
    dzf = dy * (f - x1) * gf * (1.0 - gf)
    dx1 = dy * (1.0 - gf)
    dfb = low(df)
    dzfb = low(dzf)
    dz = jnp.where(z > 0.0, mat(dfb, load(4), backward), 0.0)
    dzb = low(dz)
    dh2 = mat(dzb, load(3), backward) + mat(dzfb, load(2), backward)
    dx1 = dx1 + normalize_back(dh2, n2, s2, gain)
    da = low(dx1 * ga)
    dza = dx1 * (a - x) * ga * (1.0 - ga)
    dzab = low(dza)
    dx_ref[...] = dx1 * (1.0 - ga)
    do_ref[...] = low(mat(da, load(0), backward))
    dh_ref[...] = mat(dzab, load(1), backward)
    total = lambda value: jnp.sum(value, 0, keepdims=True)
    dvec_ref[0:1, :] += total(dh2 * n2)
    dvec_ref[1:2, :] += total(dh2)
    dvec_ref[2:3, :] += total(dza)
    dvec_ref[3:4, :] += total(dzf)
    dvec_ref[4:5, :] += total(df)
    dbias_ref[...] += total(dz)
    for chunk in range(chunks):
        r_ref[chunk, rows, :] = r[:, chunk * width : (chunk + 1) * width]
        dz_ref[chunk, rows, :] = dzb[:, chunk * width : (chunk + 1) * width]
    h2_ref[rows, :] = h2
    df_ref[rows, :] = dfb
    dzf_ref[rows, :] = dzfb
    da_ref[rows, :] = da
    dza_ref[rows, :] = dzab

    @pl.when(tile == pl.num_programs(0) - 1)
    def _():
        across = lambda left, right: low(mat(left, right, forward))
        targets[0][...] = across(o_ref[...].T, da_ref[...]).reshape(targets[0].shape)
        targets[1][...] = across(h_ref[...].T, dza_ref[...]).reshape(targets[1].shape)
        h2_turned = h2_ref[...].T
        targets[2][...] = across(h2_turned, dzf_ref[...]).reshape(targets[2].shape)
        for chunk in range(chunks):
            lanes = slice(chunk * width, (chunk + 1) * width)
            grad_in = across(h2_turned, dz_ref[chunk])
            grad_out = across(r_ref[chunk].T, df_ref[...])
            if direct:
                owners = targets[4].shape[0] // chunks
                targets[3][:, :, lanes] = grad_in.reshape(targets[3].shape[:2] + (width,))
                targets[4][chunk * owners : (chunk + 1) * owners] = grad_out.reshape(
                    (owners,) + targets[4].shape[1:]
                )
            else:
                targets[3][:, lanes] = grad_in
                targets[4][lanes, :] = grad_out
        if direct:
            copy_blocks(offsets, layout, own_ref[0], targets, *outs[6:])


FFN_LAYOUT = [("stack", 0, 1), ("stack", 1, 1), ("stack", 2, 1), ("columns", 3, 4), ("rows", 7, 4)]


def ffn(own, tokens, cotangent, normed, mixed_heads, vectors, bias, parts, tables, groups):
    rows, width = tokens.shape
    count = 2 ** sum(groups)
    step = parts[0].shape[2]
    hidden = bias.shape[0]
    chunks = hidden // width
    tile = min(256, rows)
    direct = step % 16 == 0
    offsets = [offset for row in offsets_of(groups)[:-1] for offset in row]
    matrices = [(width, width)] * 3 + [(width, hidden), (hidden, width)]
    low = jnp.bfloat16
    once = dict(pipeline_mode=pl.Buffered(1))
    block = pl.BlockSpec((tile, width), lambda i: (i, 0))
    whole = lambda shape: pl.BlockSpec(shape, lambda i: (0,) * len(shape), **once)
    scratch = [pltpu.VMEM((chunks, rows, width), low)] * 2 + [pltpu.VMEM((rows, width), low)] * 5
    if direct:
        shape = (len(offsets), 3 + 2 * chunks, step, width)
        grads = [jax.ShapeDtypeStruct(shape, low)] * 2
        scratch += [pltpu.VMEM((1, count, step, width), low)] * 3
        scratch += [pltpu.VMEM((count, step, hidden), low), pltpu.VMEM((count, chunks, step, width), low)]
    else:
        placed = place(own, parts, tables, FFN_LAYOUT, groups)
        parts = [weight.reshape(shape) for weight, shape in zip(placed, matrices)]
        grads = [jax.ShapeDtypeStruct(shape, low) for shape in matrices]
    full = jax.ShapeDtypeStruct((rows, width), jnp.float32)
    half = jax.ShapeDtypeStruct((rows, width), low)
    small = [jax.ShapeDtypeStruct((8, width), jnp.float32), jax.ShapeDtypeStruct((1, hidden), jnp.float32)]
    result = pl.pallas_call(
        functools.partial(ffn_kernel, direct, len(parts), tables, offsets, FFN_LAYOUT),
        grid=(rows // tile,),
        in_specs=[smem_spec(), block, block, whole((rows, width)), whole((rows, width))]
        + [whole(vectors.shape), whole((1, hidden))]
        + [whole(part.shape) for part in parts],
        out_specs=[block] * 4 + [whole(item.shape) for item in small + grads],
        out_shape=[half, half, full, full] + small + grads,
        scratch_shapes=scratch,
        name="ffn",
    )(own[None].astype(jnp.int32), tokens, cotangent, normed, mixed_heads, vectors, bias[None], *parts)
    if not direct:
        blocks = [grad.reshape(1, count, step, width) for grad in result[6:9]]
        blocks += [result[9].reshape(count, step, hidden), result[10].reshape(count, chunks, step, width)]
        result = list(result[:6]) + list(split(own, blocks, FFN_LAYOUT, groups))
    return result


def adam_update(weight, first_moment, second_moment, gradient, factor, step_rate):
    clipped = gradient * factor
    first_new = first_decay * first_moment + (1.0 - first_decay) * clipped
    second_new = second_decay * second_moment + (1.0 - second_decay) * clipped * clipped
    corrected = first_new / (1.0 - first_decay**STEP)
    spread = second_new / (1.0 - second_decay**STEP)
    weight_new = weight - step_rate * (
        corrected / (jnp.sqrt(spread) + adam_eps) + weight_decay * weight
    )
    return (weight_new, first_new, second_new)


def own_lanes(rows, first, lanes):
    width = rows.shape[1]
    return pltpu.roll(rows, (width - first) % width, 1)[:, :lanes]


def update_kernel(own_ref, payload_ref, a_ref, b_ref, *refs):
    states = [refs[3 * index : 3 * index + 3] for index in range(6)]
    norm_ref = refs[18]
    news = [refs[19 + 3 * index : 22 + 3 * index] for index in range(6)]
    squares = payload_ref[:11, :] * payload_ref[:11, :]
    total = jnp.sum(jnp.sum(squares, 1, keepdims=True), 0, keepdims=True)
    norm = jnp.sqrt(total + payload_ref[11:12, 0:1])
    norm_ref[...] = norm
    factor = jnp.minimum(1.0, clip_norm / (norm + 1e-06))

    def update(index, where, gradient):
        rate = vector_rate if index > 3 else learn_rate
        values = adam_update(*[ref[where] for ref in states[index]], gradient, factor, rate)
        for ref, value in zip(news[index], values):
            ref[where] = value

    width = a_ref.shape[2]
    for piece in range(3):
        update(0, piece, a_ref[piece])
    update(0, 3, b_ref[0])
    for piece in range(2):
        update(1, piece, b_ref[1 + piece])
    chunks = (b_ref.shape[0] - 3) // 2
    step = b_ref.shape[1]
    for chunk in range(chunks):
        update(2, (slice(None), slice(chunk * width, (chunk + 1) * width)), b_ref[3 + chunk])
        update(3, slice(chunk * step, (chunk + 1) * step), b_ref[3 + chunks + chunk])
    own = own_ref[0]
    vec_lanes = states[4][0].shape[1]
    update(4, Ellipsis, own_lanes(payload_ref[0:8, :], own * vec_lanes, vec_lanes)[:7])
    bias_lanes = states[5][0].shape[1]
    first = own * bias_lanes
    line = lax.broadcasted_iota(jnp.int32, (5, width), 0)
    picked = jnp.sum(jnp.where(line == first // width, payload_ref[7:12, :], 0.0), 0, keepdims=True)
    picked = own_lanes(jnp.broadcast_to(picked, (8, width)), first % width, bias_lanes)
    update(5, Ellipsis, picked[0:1])


def update_all(own, payload, total_a, total_b, states):
    flat = [value for state in states for value in state]
    shapes = [jax.ShapeDtypeStruct(value.shape, jnp.float32) for value in flat]
    norm, *news = pl.pallas_call(
        update_kernel,
        in_specs=[smem_spec()] + [vmem_spec() for _ in range(3 + len(flat))],
        out_specs=[vmem_spec() for _ in range(1 + len(flat))],
        out_shape=[jax.ShapeDtypeStruct((1, 1), jnp.float32)] + shapes,
        name="update",
    )(own[None].astype(jnp.int32), payload, total_a, total_b, *flat)
    return norm[0, 0], [news[3 * index : 3 * index + 3] for index in range(len(states))]


def body(
    groups,
    tokens,
    segments,
    positions,
    cotangent,
    attn_weight,
    attn_m,
    attn_v,
    gate_weight,
    gate_m,
    gate_v,
    in_weight,
    in_m,
    in_v,
    out_weight,
    out_m,
    out_v,
    norm_params,
    norm_m,
    norm_v,
    in_bias,
    bias_m,
    bias_v,
):
    count = 2 ** sum(groups)
    own = lax.axis_index(AXES)
    width = 512
    step = attn_weight.shape[1]
    low = lambda value: value.astype(jnp.bfloat16)
    dot = functools.partial(jnp.einsum, preferred_element_type=jnp.float32)
    columns = lambda value: [value[:, width * j : width * (j + 1)] for j in range(4)]
    small = pad_rows(small_shard(norm_params, in_bias, own, count, width), step)
    extra = small.shape[0]
    first_shard = jnp.concatenate([low(attn_weight[:3]), small])
    second_shard = jnp.concatenate(
        [
            low(attn_weight[3:]),
            low(gate_weight),
            jnp.stack(columns(low(in_weight))),
            low(out_weight).reshape(4, step, width),
        ]
    )
    z_first = gather_z(first_shard, groups)
    z_first, second_shard = tie(z_first, second_shard)
    plane_first = gather_plane(z_first, groups)
    z_second = gather_z(second_shard, groups)
    z_first, z_second, *plane_first = tie(z_first, z_second, *plane_first)
    core_first = gather_core(z_first, plane_first, groups)
    plane_second = gather_plane(z_second, groups)
    relative = offsets_of(groups)
    normed, queries, keys, values, mixed_heads, log_total, w_qkv, vectors = attend(
        own,
        tokens,
        segments,
        positions,
        [z_first] + plane_first + [core_first],
        [(row, 0) for row in relative],
        [("stack", 0, 3), ("sum", 3, extra)],
        groups,
    )
    w_qkv = w_qkv.reshape(3, count * step, width)
    bias = vectors[7:11].reshape(-1)
    inputs = tokens.astype(jnp.float32)
    mean_one = jnp.mean(inputs, -1, keepdims=True)
    scale_one = lax.rsqrt(jnp.mean((inputs - mean_one) * (inputs - mean_one), -1, keepdims=True) + norm_eps)
    core_second = [swap_with(z_second, 1, count)]
    mixed_heads, mean_one, scale_one, core_second[0], *plane_second = tie(
        mixed_heads, mean_one, scale_one, core_second[0], *plane_second
    )
    unit_one = (inputs - mean_one) * scale_one
    core_second += [swap_with(part, 1, count) for part in plane_second]
    layer_out, grad_mixed, grad_normed, grad_inputs, sums, grad_bias, kept_b, sent_b = ffn(
        own,
        tokens,
        cotangent,
        normed,
        mixed_heads,
        vectors,
        bias,
        [z_second] + plane_second + core_second,
        [(row, 0) for row in relative[:-1]] + [([offset | 1 for offset in row], 0) for row in relative[:-1]],
        groups,
    )
    core_b = swap_with(sent_b, 1, count)
    core_b, kept_b, grad_mixed = tie(core_b, kept_b, grad_mixed)
    own_b, parts_b = plane_sums(kept_b, core_b, groups)
    own_b, log_total, *parts_b = tie(own_b, log_total, *parts_b)
    plane_b = plane_send(parts_b, groups)
    kept_a, sent_a, grad_normed = attend_back(
        own, queries, keys, values, grad_mixed, log_total, segments, positions, normed, w_qkv, grad_normed, groups
    )
    kept_a, sent_a, grad_normed, own_b, *plane_b = tie(kept_a, sent_a, grad_normed, own_b, *plane_b)
    core_a = swap_with(sent_a, 1, count)
    own_b, z_b = reduce_z(own_b, plane_b, groups)
    own_a, parts_a = plane_sums(kept_a, core_a, groups)
    grad_normed, own_a, *parts_a = tie(grad_normed, own_a, *parts_a)
    grad_gain_one = jnp.sum(grad_normed * unit_one, 0)
    grad_shift_one = jnp.sum(grad_normed, 0)
    grad_inputs = grad_inputs + normalize_back(grad_normed, unit_one, scale_one, vectors[0])
    input_grad = low(grad_inputs)
    plane_a = plane_send(parts_a, groups)
    input_grad, grad_gain_one, grad_shift_one, *arrived = tie(
        input_grad, grad_gain_one, grad_shift_one, *z_b, *plane_a
    )
    z_b, plane_a = arrived[: len(z_b)], arrived[len(z_b) :]
    own_a, z_a = reduce_z(own_a, plane_a, groups)
    total_b = reduce_end(own_b, z_b)
    total_a = reduce_end(own_a, z_a)
    local_squares = jnp.sum(total_b * total_b) + jnp.sum(total_a * total_a)
    payload = jnp.concatenate(
        [
            grad_gain_one[None],
            grad_shift_one[None],
            sums[:5],
            grad_bias.reshape(4, width),
            jnp.full((1, width), local_squares),
        ]
    )
    payload = sum_all(payload, groups)
    states = (
        (attn_weight, attn_m, attn_v),
        (gate_weight, gate_m, gate_v),
        (in_weight, in_m, in_v),
        (out_weight, out_m, out_v),
        (norm_params, norm_m, norm_v),
        (in_bias[None], bias_m[None], bias_v[None]),
    )
    grad_norm, updated = update_all(own, payload, total_a, total_b, states)
    return (
        layer_out,
        input_grad,
        grad_norm,
        updated[0][0],
        updated[0][1],
        updated[0][2],
        updated[1][0],
        updated[1][1],
        updated[1][2],
        updated[2][0],
        updated[2][1],
        updated[2][2],
        updated[3][0],
        updated[3][1],
        updated[3][2],
        updated[4][0],
        updated[4][1],
        updated[4][2],
        updated[5][0][0],
        updated[5][1][0],
        updated[5][2][0],
    )


def solution(mesh):
    return jax.shard_map(
        functools.partial(body, bit_groups(mesh.shape)),
        mesh=mesh,
        in_specs=(
            P(("dp", "inner"), None),
            P(("dp", "inner")),
            P(("dp", "inner")),
            P(("dp", "inner"), None),
            P(None, ("dp", "inner"), None),
            P(None, ("dp", "inner"), None),
            P(None, ("dp", "inner"), None),
            P(None, ("dp", "inner"), None),
            P(None, ("dp", "inner"), None),
            P(None, ("dp", "inner"), None),
            P(("dp", "inner"), None),
            P(("dp", "inner"), None),
            P(("dp", "inner"), None),
            P(("dp", "inner"), None),
            P(("dp", "inner"), None),
            P(("dp", "inner"), None),
            P(None, ("dp", "inner")),
            P(None, ("dp", "inner")),
            P(None, ("dp", "inner")),
            P(("dp", "inner")),
            P(("dp", "inner")),
            P(("dp", "inner")),
        ),
        out_specs=(
            P(("dp", "inner"), None),
            P(("dp", "inner"), None),
            P(),
            P(None, ("dp", "inner"), None),
            P(None, ("dp", "inner"), None),
            P(None, ("dp", "inner"), None),
            P(None, ("dp", "inner"), None),
            P(None, ("dp", "inner"), None),
            P(None, ("dp", "inner"), None),
            P(("dp", "inner"), None),
            P(("dp", "inner"), None),
            P(("dp", "inner"), None),
            P(("dp", "inner"), None),
            P(("dp", "inner"), None),
            P(("dp", "inner"), None),
            P(None, ("dp", "inner")),
            P(None, ("dp", "inner")),
            P(None, ("dp", "inner")),
            P(("dp", "inner")),
            P(("dp", "inner")),
            P(("dp", "inner")),
        ),
        check_vma=False,
    )
```

```python
import functools
import jax
import jax.numpy as jnp
from jax import lax
from jax.experimental import pallas as pl
from jax.experimental.pallas import tpu as pltpu
from jax.sharding import PartitionSpec as P

AXES = ("dp", "inner")
HEADS = 8
HEAD = 64
STEP = 10
LOG2E = 1.4426950408889634
BLOCK = 256


norm_eps = 1e-05
first_decay = 0.9
second_decay = 0.999
adam_eps = 1e-08
learn_rate = 0.05
vector_rate = 0.8
weight_decay = 0.1
clip_norm = 1.0
masked_score = -1e30


def normalize_parts(values, gain_row, bias_row):
    centred = values - jnp.mean(values, -1, keepdims=True)
    spread = jnp.mean(centred * centred, -1, keepdims=True)
    scale_row = lax.rsqrt(spread + norm_eps)
    unit_rows = centred * scale_row
    return (unit_rows * gain_row + bias_row, unit_rows, scale_row)


def normalize_back(grad_rows, unit_rows, scale_row, gain_row):
    grad_unit = grad_rows * gain_row
    return scale_row * (
        grad_unit
        - jnp.mean(grad_unit, -1, keepdims=True)
        - unit_rows * jnp.mean(grad_unit * unit_rows, -1, keepdims=True)
    )


def bit_groups(sizes):
    dp_bits = sizes["dp"].bit_length() - 1
    inner_bits = sizes["inner"].bit_length() - 1
    y_bits = dp_bits // 2
    plane_bits = (inner_bits - 1) + y_bits
    return (1, plane_bits, dp_bits - y_bits)


def swap_with(array, offset, count):
    return lax.ppermute(array, AXES, [(source, source ^ offset) for source in range(count)])


def stage_bits(groups):
    return ((0, groups[0]), (groups[0], groups[1]), (groups[0] + groups[1], groups[2]))


def gather_z(shard, groups):
    count = 2 ** sum(groups)
    first_bit, bits = stage_bits(groups)[2]
    return jnp.stack([shard] + [swap_with(shard, offset << first_bit, count) for offset in range(1, 2**bits)])


def gather_plane(column, groups):
    count = 2 ** sum(groups)
    first_bit, bits = stage_bits(groups)[1]
    return [swap_with(column, offset << first_bit, count) for offset in range(1, 2**bits)]


def gather_core(column, planes, groups):
    return swap_with(jnp.concatenate([column] + planes), 1, 2 ** sum(groups))


def offsets_of(groups):
    (_, _), (plane_bit, plane_bits), (z_bit, z_bits) = stage_bits(groups)
    table = [
        [(plane << plane_bit) | (z << z_bit) for z in range(2**z_bits)] for plane in range(2**plane_bits)
    ]
    return table + [[offset | 1 for row in table for offset in row]]


def plane_orders(groups):
    _, (first_bit, bits), _ = stage_bits(groups)
    order = list(range(first_bit, first_bit + bits))
    return order, order[bits // 2 :] + order[: bits // 2]


def z_offsets(groups):
    _, _, (first_bit, bits) = stage_bits(groups)
    return [z << first_bit for z in range(2**bits)]


def send_halves(arrays, orders, position, groups):
    count = 2 ** sum(groups)
    return [swap_with(array, 1 << order[position], count) for array, order in zip(arrays, orders)]


def flip_tables(tables, bits):
    return [[offset ^ (1 << bit) for offset in table] for table, bit in zip(tables, bits)]


def vmem_spec():
    return pl.BlockSpec(memory_space=pltpu.VMEM)


def smem_spec():
    return pl.BlockSpec(memory_space=pltpu.SMEM)


def place(own, parts, tables, layout, groups):
    count = 2 ** sum(groups)
    step, width = parts[0].shape[2:]
    firsts = sorted({first for _, first in tables})
    groups_of = []
    for first in firsts:
        chosen = [(part, row) for part, (row, base) in zip(parts, tables) if base == first]
        order = jnp.argsort(jnp.array([o for _, row in chosen for o in row]) ^ own)
        groups_of.append(jnp.concatenate([part for part, _ in chosen])[order])
    full = jnp.concatenate(groups_of, 1)
    result = []
    for kind, first, pieces in layout:
        chosen = full[:, first : first + pieces]
        if kind == "sum":
            result.append(jnp.sum(chosen.astype(jnp.float32), 0).reshape(pieces * step, width))
        elif kind == "stack":
            result.append(jnp.moveaxis(chosen, 0, 1))
        elif kind == "rows":
            result.append(chosen)
        else:
            result.append(jnp.moveaxis(chosen, 1, 2).reshape(count, step, pieces * width))
    return result


def split(own, grads, layout, groups):
    count = 2 ** sum(groups)
    width = 512
    step = grads[0].shape[-2]
    offsets = [offset for row in offsets_of(groups)[:-1] for offset in row]
    pieces_of = []
    for grad, (kind, _, pieces) in zip(grads, layout):
        if kind == "stack":
            grad = jnp.moveaxis(grad, 1, 0)
        elif kind == "columns":
            grad = jnp.moveaxis(grad.reshape(count, step, pieces, width), 2, 1)
        pieces_of.append(grad)
    full = jnp.concatenate(pieces_of, 1)
    order = jnp.array(offsets) ^ own
    return full[order], full[order ^ 1]


def plane_sums(kept, received, groups):
    _, (_, bits), (_, z_bits) = stage_bits(groups)
    shape = (2**bits, 2**z_bits) + kept.shape[1:]
    kept = kept.reshape(shape)
    received = received.reshape(shape)
    total = lambda offset: kept[offset].astype(jnp.float32) + received[offset].astype(jnp.float32)
    return total(0), [total(offset).astype(jnp.bfloat16) for offset in range(1, 2**bits)]


def plane_send(parts, groups):
    first_bit = stage_bits(groups)[1][0]
    return [swap_with(part, offset << first_bit, 2 ** sum(groups)) for offset, part in enumerate(parts, 1)]


def reduce_z(own_part, arrived, groups):
    count = 2 ** sum(groups)
    first_bit, bits = stage_bits(groups)[2]
    total = lambda z: own_part[z] + sum(part[z].astype(jnp.float32) for part in arrived)
    return total(0), [
        swap_with(total(z).astype(jnp.bfloat16), z << first_bit, count) for z in range(1, 2**bits)
    ]


def reduce_end(own_part, arrived):
    return own_part + sum(part.astype(jnp.float32) for part in arrived)


def sum_all(value, groups):
    for bit in range(sum(groups)):
        value = value + swap_with(value, 1 << bit, 2 ** sum(groups))
    return value


def tie(*values):
    return lax.optimization_barrier(values)


def small_shard(vec, bias, own, count, width):
    step = vec.shape[1]
    lane = lax.broadcasted_iota(jnp.int32, (7, width), 1)
    rows = jnp.where(lane // step == own, jnp.tile(vec, (1, count)), 0.0)
    place_of = lax.broadcasted_iota(jnp.int32, (4, width), 0) * width + lax.broadcasted_iota(
        jnp.int32, (4, width), 1
    )
    tiled = jnp.tile(bias, width // bias.shape[0])[None]
    bias_rows = jnp.where(place_of // bias.shape[0] == own, tiled, 0.0)
    return jnp.concatenate([rows, bias_rows])


def pad_rows(rows, step):
    pieces = -(-rows.shape[0] // step)
    rows = jnp.pad(rows.astype(jnp.bfloat16), ((0, pieces * step - rows.shape[0]), (0, 0)))
    return rows.reshape(pieces, step, rows.shape[1])


def mat(a,b,dims):
    return lax.dot_general(a,b,(dims,((),())),preferred_element_type=jnp.float32)

def fill_bias(bias_ref, seg_col, pos_col, seg_row, pos_row):
    rows=bias_ref.shape[0]
    step=min(BLOCK,rows)
    for first in range(0,rows,step):
        sc=seg_col[first:first+step,:]; pc=pos_col[first:first+step,:]
        sr=seg_row[:,first:]; pr=pos_row[:,first:]
        allowed=(sc==sr)&(pc<=pr)
        bias_ref[first:first+step,first:]=jnp.where(allowed,0.0,masked_score)

def head_lanes(shape, which):
    lane=lax.broadcasted_iota(jnp.int32,shape,1)
    return (lane//HEAD)==which

def attn_fwd_kernel(direct, tables, layout, own_ref, segc, posc, segr, posr, x_ref, *refs):
    part_count = len(tables) if direct else 2
    parts = refs[:part_count]
    h_ref, q_ref, k_ref, v_ref, o_ref, lse_ref, *rest = refs[part_count:]
    bias_ref, q_all, k_all, v_all = rest[-4:]
    rows = x_ref.shape[0]
    step = min(BLOCK, rows)
    lanes = q_ref.shape[1]
    pair = lanes // HEAD
    const = HEAD**-0.5 * LOG2E
    low = lambda value: value.astype(jnp.bfloat16)
    weights, vectors = rest[:2] if direct else parts
    tile = pl.program_id(0)

    @pl.when(tile == 0)
    def _():
        if direct:
            copy_parts(tables, layout, own_ref[0], parts, [weights, vectors])
        fill_bias(bias_ref, segc, posc, segr, posr)
        for first in range(0, rows, step):
            x = x_ref[first : first + step, :].astype(jnp.float32)
            h_ref[first : first + step, :] = low(normalize_parts(x, vectors[0:1, :], vectors[1:2, :])[0])
        for j, target in enumerate((q_all, k_all, v_all)):
            whole = low(mat(h_ref[...], weights[j].reshape(-1, weights.shape[-1]), ((1,), (0,))))
            for which in range(target.shape[0]):
                target[which] = whole[:, which * lanes : (which + 1) * lanes]

    q_ref[...] = q_all[tile]
    k_ref[...] = k_all[tile]
    v_ref[...] = v_all[tile]
    for first in range(0, rows, step):
        keys = first + step
        q = q_ref[first:keys, :]
        mixed = None
        for which in range(pair):
            own = head_lanes(q.shape, which)
            qh = jnp.where(own, q, jnp.zeros_like(q))
            s = mat(k_ref[:keys, :], qh, ((1,), (1,))) * const + bias_ref[:keys, first:keys]
            m = jnp.max(s, 0, keepdims=True)
            w = jnp.exp2(s - m)
            total = jnp.sum(w, 0, keepdims=True)
            p = (w * (1.0 / total)).astype(jnp.bfloat16)
            o = mat(p, v_ref[:keys, :], ((0,), (0,)))
            mixed = o if mixed is None else jnp.where(own, o, mixed)
            lse_ref[0, which : which + 1, first:keys] = m + jnp.log2(total)
        o_ref[first:keys, :] = mixed.astype(jnp.bfloat16)


def attn_bwd_kernel(
    offsets, own_ref, segc, posc, segr, posr, q_ref, k_ref, v_ref, do_ref, lse_ref, h_ref, w_ref, start_ref, *refs
):
    *outs, dh_ref, bias_ref, dk_acc, dv_acc, ht_ref, dw_ref = refs
    rows = q_ref.shape[0]

    @pl.when(pl.program_id(0) == 0)
    def _():
        fill_bias(bias_ref, segc, posc, segr, posr)
        ht_ref[...] = h_ref[...].T
        dh_ref[...] = start_ref[...]

    step = min(BLOCK, rows)
    pair = q_ref.shape[1] // HEAD
    const = HEAD**-0.5 * LOG2E
    scale = HEAD**-0.5
    dk_acc[...] = jnp.zeros_like(dk_acc)
    dv_acc[...] = jnp.zeros_like(dv_acc)
    dq_parts = []
    for first in range(0, rows, step):
        keys = first + step
        q = q_ref[first:keys, :]
        do = do_ref[first:keys, :]
        dq = None
        for which in range(pair):
            own = head_lanes(q.shape, which)
            qh = jnp.where(own, q, jnp.zeros_like(q))
            doh = jnp.where(own, do, jnp.zeros_like(do))
            s = mat(k_ref[:keys, :], qh, ((1,), (1,)))
            p = jnp.exp2(s * const + (bias_ref[:keys, first:keys] - lse_ref[0, which : which + 1, first:keys]))
            dp = mat(v_ref[:keys, :], doh, ((1,), (1,)))
            inner = jnp.sum(p * dp, 0, keepdims=True)
            ds = (p * (dp - inner)).astype(jnp.bfloat16)
            dv_acc[:keys, :] += mat(p.astype(jnp.bfloat16), doh, ((1,), (0,)))
            dk_acc[:keys, :] += mat(ds, qh, ((1,), (0,)))
            d = mat(ds, k_ref[:keys, :], ((0,), (0,)))
            dq = d if dq is None else jnp.where(own, d, dq)
        dq_parts.append((dq * scale).astype(jnp.bfloat16))
    grads = jnp.concatenate(
        [
            jnp.concatenate(dq_parts, 0),
            (dk_acc[...] * scale).astype(jnp.bfloat16),
            dv_acc[...].astype(jnp.bfloat16),
        ],
        1,
    )
    weights = jnp.concatenate([w_ref[0], w_ref[1], w_ref[2]], 1)
    dh_ref[...] += mat(grads, weights, ((1,), (1,)))
    dw = mat(ht_ref[...], grads, ((1,), (0,))).astype(jnp.bfloat16)
    lanes = q_ref.shape[1]
    if offsets is None:
        for j in range(3):
            outs[0][j] = dw[:, j * lanes : (j + 1) * lanes]
    else:
        dw_ref[...] = dw.reshape(dw_ref.shape)
        for entry, offset in enumerate(offsets):
            for side in range(2):
                owner = own_ref[0] ^ (offset | side)
                for j in range(3):
                    outs[side][entry, j] = dw_ref[owner, :, j * lanes : (j + 1) * lanes]


def const_map(*_): return (0,0)

def seg_args(segments,positions):
    return (segments[:,None],positions[:,None],segments[None],positions[None])

def attend(own, tokens, marks, parts, tables, layout, groups):
    rows, width = tokens.shape
    count = 2 ** sum(groups)
    step = parts[0].shape[2]
    lanes = 2 * HEAD
    pairs = width // lanes
    low = jnp.bfloat16
    direct = step % 16 == 0
    blk = pl.BlockSpec((rows, lanes), lambda j: (0, j))
    whole = lambda shape: pl.BlockSpec(shape, lambda j: (0,) * len(shape), pipeline_mode=pl.Buffered(1))
    half = jax.ShapeDtypeStruct((rows, width), low)
    out_shape = [half] * 5 + [jax.ShapeDtypeStruct((pairs, 2, rows), jnp.float32)]
    out_specs = [whole((rows, width)), blk, blk, blk, blk, pl.BlockSpec((1, 2, rows), lambda j: (j, 0, 0))]
    if direct:
        extra = [
            jax.ShapeDtypeStruct((3, count, step, width), low),
            jax.ShapeDtypeStruct((step, width), jnp.float32),
        ]
        out_shape += extra
        out_specs += [whole(item.shape) for item in extra]
    else:
        parts = place(own, parts, tables, layout, groups)
    result = pl.pallas_call(
        functools.partial(attn_fwd_kernel, direct, tables, layout),
        grid=(pairs,),
        in_specs=[smem_spec(), whole((rows, 1)), whole((rows, 1)), whole((1, rows)), whole((1, rows))]
        + [whole((rows, width))]
        + [whole(part.shape) for part in parts],
        out_specs=out_specs,
        out_shape=out_shape,
        scratch_shapes=[pltpu.VMEM((rows, rows), jnp.float32)] + [pltpu.VMEM((pairs, rows, lanes), low)] * 3,
        name="attn_fwd",
    )(own[None].astype(jnp.int32), *marks, tokens, *parts)
    if not direct:
        result = list(result) + list(parts)
    return result


def attend_back(own, q, k, v, do, lse, marks, normed, w_qkv, start, groups):
    rows, width = q.shape
    lanes = 2 * HEAD
    count = 2 ** sum(groups)
    inputs = w_qkv.shape[1]
    step = inputs // count
    blk = pl.BlockSpec((rows, lanes), lambda j: (0, j))
    col = pl.BlockSpec((rows, 1), const_map)
    row = pl.BlockSpec((1, rows), const_map)
    offsets = None
    if step % 16 == 0:
        offsets = [offset for table in offsets_of(groups)[:-1] for offset in table]
        shape = (len(offsets), 3, step, width)
        out_specs = [pl.BlockSpec(shape[:3] + (lanes,), lambda j: (0, 0, 0, j)) for _ in range(2)]
        out_shape = [jax.ShapeDtypeStruct(shape, jnp.bfloat16) for _ in range(2)]
        dw_scratch = pltpu.VMEM((count, step, 3 * lanes), jnp.bfloat16)
    else:
        out_specs = [pl.BlockSpec((3, inputs, lanes), lambda j: (0, 0, j))]
        out_shape = [jax.ShapeDtypeStruct((3, inputs, width), jnp.bfloat16)]
        dw_scratch = pltpu.VMEM((16, lanes), jnp.bfloat16)
    *grads, dh = pl.pallas_call(
        functools.partial(attn_bwd_kernel, offsets),
        grid=(width // lanes,),
        in_specs=[smem_spec(), col, col, row, row, blk, blk, blk, blk]
        + [
            pl.BlockSpec((1, 2, rows), lambda j: (j, 0, 0)),
            pl.BlockSpec((rows, inputs), const_map),
            pl.BlockSpec((3, inputs, lanes), lambda j: (0, 0, j)),
            pl.BlockSpec((rows, inputs), const_map),
        ],
        out_specs=out_specs + [pl.BlockSpec((rows, inputs), const_map)],
        out_shape=out_shape + [jax.ShapeDtypeStruct((rows, inputs), jnp.float32)],
        scratch_shapes=[
            pltpu.VMEM((rows, rows), jnp.float32),
            pltpu.VMEM((rows, lanes), jnp.float32),
            pltpu.VMEM((rows, lanes), jnp.float32),
            pltpu.VMEM((inputs, rows), jnp.bfloat16),
            dw_scratch,
        ],
        name="attn_bwd",
    )(own[None].astype(jnp.int32), *marks, q, k, v, do, lse, normed, w_qkv, start)
    if offsets is None:
        grads = split(own, [grads[0].reshape(3, count, step, width)], [("stack", 0, 3)], groups)
    return grads[0], grads[1], dh


def copy_parts(tables, layout, own, parts, outs):
    where_to = [
        (index, kind, piece) for index, (kind, _, pieces) in enumerate(layout) for piece in range(pieces)
    ]
    total = None
    for part, (row, first) in zip(parts, tables):
        width = part.shape[3]
        for entry, offset in enumerate(row):
            owner = own ^ offset
            for source in range(part.shape[1]):
                index, kind, piece = where_to[first + source]
                block = part[entry, source]
                if kind == "sum":
                    block = block.astype(jnp.float32)
                    total = block if total is None else total + block
                elif kind == "stack":
                    outs[index][piece, owner] = block
                elif kind == "rows":
                    outs[index][owner, piece] = block
                else:
                    outs[index][owner, :, piece * width : (piece + 1) * width] = block
    for index, (kind, _, _) in enumerate(layout):
        if kind == "sum":
            outs[index][...] = total


def copy_blocks(offsets, layout, own, ins, kept, sent):
    width = kept.shape[3]
    for entry, offset in enumerate(offsets):
        for side, target in enumerate((kept, sent)):
            owner = own ^ (offset | side)
            for index, (kind, first, pieces) in enumerate(layout):
                for piece in range(pieces):
                    if kind == "stack":
                        block = ins[index][piece, owner]
                    elif kind == "rows":
                        block = ins[index][owner, piece]
                    else:
                        block = ins[index][owner, :, piece * width : (piece + 1) * width]
                    target[entry, first + piece] = block


def ffn_kernel(direct, part_count, tables, offsets, layout, own_ref, x_ref, cot_ref, h_ref, o_ref, vec_ref, bias_ref, *refs):
    low = lambda value: value.astype(jnp.bfloat16)
    parts = refs[:part_count]
    out_count = 6 + (2 if direct else 5)
    outs = refs[part_count : part_count + out_count]
    scratch = refs[part_count + out_count :]
    y_ref, do_ref, dh_ref, dx_ref, dvec_ref, dbias_ref = outs[:6]
    r_ref, dz_ref, h2_ref, df_ref, dzf_ref, da_ref, dza_ref = scratch[:7]
    tile = pl.program_id(0)
    if direct:
        weights = targets = scratch[7:]

        @pl.when(tile == 0)
        def _():
            copy_parts(tables, layout, own_ref[0], parts, weights)

    else:
        weights, targets = parts, outs[6:]
    width = x_ref.shape[1]
    size = x_ref.shape[0]
    chunks = r_ref.shape[0]
    load = lambda index: weights[index][...].reshape(-1, weights[index].shape[-1])
    rows = pl.ds(tile * size, size)

    @pl.when(tile == 0)
    def _():
        dvec_ref[...] = jnp.zeros_like(dvec_ref)
        dbias_ref[...] = jnp.zeros_like(dbias_ref)

    forward = ((1,), (0,))
    backward = ((1,), (1,))
    x = x_ref[...].astype(jnp.float32)
    a = mat(o_ref[rows, :], load(0), forward)
    ga = jax.nn.sigmoid(mat(h_ref[rows, :], load(1), forward) + vec_ref[4:5, :])
    x1 = ga * a + (1.0 - ga) * x
    gain = vec_ref[2:3, :]
    h2_full, n2, s2 = normalize_parts(x1, gain, vec_ref[3:4, :])
    h2 = low(h2_full)
    z = mat(h2, load(3), forward) + bias_ref[...]
    r = low(jnp.maximum(z, 0.0))
    f = mat(r, load(4), forward) + vec_ref[6:7, :]
    gf = jax.nn.sigmoid(mat(h2, load(2), forward) + vec_ref[5:6, :])
    y_ref[...] = low(gf * f + (1.0 - gf) * x1)
    dy = cot_ref[...].astype(jnp.float32)
    df = dy * gf
    dzf = dy * (f - x1) * gf * (1.0 - gf)
    dx1 = dy * (1.0 - gf)
    dfb = low(df)
    dzfb = low(dzf)
    dz = jnp.where(z > 0.0, mat(dfb, load(4), backward), 0.0)
    dzb = low(dz)
    dh2 = mat(dzb, load(3), backward) + mat(dzfb, load(2), backward)
    dx1 = dx1 + normalize_back(dh2, n2, s2, gain)
    da = low(dx1 * ga)
    dza = dx1 * (a - x) * ga * (1.0 - ga)
    dzab = low(dza)
    dx_ref[...] = dx1 * (1.0 - ga)
    do_ref[...] = low(mat(da, load(0), backward))
    dh_ref[...] = mat(dzab, load(1), backward)
    total = lambda value: jnp.sum(value, 0, keepdims=True)
    dvec_ref[0:1, :] += total(dh2 * n2)
    dvec_ref[1:2, :] += total(dh2)
    dvec_ref[2:3, :] += total(dza)
    dvec_ref[3:4, :] += total(dzf)
    dvec_ref[4:5, :] += total(df)
    dbias_ref[...] += total(dz)
    for chunk in range(chunks):
        r_ref[chunk, rows, :] = r[:, chunk * width : (chunk + 1) * width]
        dz_ref[chunk, rows, :] = dzb[:, chunk * width : (chunk + 1) * width]
    h2_ref[rows, :] = h2
    df_ref[rows, :] = dfb
    dzf_ref[rows, :] = dzfb
    da_ref[rows, :] = da
    dza_ref[rows, :] = dzab

    @pl.when(tile == pl.num_programs(0) - 1)
    def _():
        across = lambda left, right: low(mat(left, right, forward))
        targets[0][...] = across(o_ref[...].T, da_ref[...]).reshape(targets[0].shape)
        targets[1][...] = across(h_ref[...].T, dza_ref[...]).reshape(targets[1].shape)
        h2_turned = h2_ref[...].T
        targets[2][...] = across(h2_turned, dzf_ref[...]).reshape(targets[2].shape)
        for chunk in range(chunks):
            lanes = slice(chunk * width, (chunk + 1) * width)
            grad_in = across(h2_turned, dz_ref[chunk])
            grad_out = across(r_ref[chunk].T, df_ref[...])
            if direct:
                owners = targets[4].shape[0] // chunks
                targets[3][:, :, lanes] = grad_in.reshape(targets[3].shape[:2] + (width,))
                targets[4][chunk * owners : (chunk + 1) * owners] = grad_out.reshape(
                    (owners,) + targets[4].shape[1:]
                )
            else:
                targets[3][:, lanes] = grad_in
                targets[4][lanes, :] = grad_out
        if direct:
            copy_blocks(offsets, layout, own_ref[0], targets, *outs[6:])


FFN_LAYOUT = [("stack", 0, 1), ("stack", 1, 1), ("stack", 2, 1), ("columns", 3, 4), ("rows", 7, 4)]


def ffn(own, tokens, cotangent, normed, mixed_heads, vectors, bias, parts, tables, groups):
    rows, width = tokens.shape
    count = 2 ** sum(groups)
    step = parts[0].shape[2]
    hidden = bias.shape[0]
    chunks = hidden // width
    tile = min(256, rows)
    direct = step % 16 == 0
    offsets = [offset for row in offsets_of(groups)[:-1] for offset in row]
    matrices = [(width, width)] * 3 + [(width, hidden), (hidden, width)]
    low = jnp.bfloat16
    once = dict(pipeline_mode=pl.Buffered(1))
    block = pl.BlockSpec((tile, width), lambda i: (i, 0))
    whole = lambda shape: pl.BlockSpec(shape, lambda i: (0,) * len(shape), **once)
    scratch = [pltpu.VMEM((chunks, rows, width), low)] * 2 + [pltpu.VMEM((rows, width), low)] * 5
    if direct:
        shape = (len(offsets), 3 + 2 * chunks, step, width)
        grads = [jax.ShapeDtypeStruct(shape, low)] * 2
        scratch += [pltpu.VMEM((1, count, step, width), low)] * 3
        scratch += [pltpu.VMEM((count, step, hidden), low), pltpu.VMEM((count, chunks, step, width), low)]
    else:
        placed = place(own, parts, tables, FFN_LAYOUT, groups)
        parts = [weight.reshape(shape) for weight, shape in zip(placed, matrices)]
        grads = [jax.ShapeDtypeStruct(shape, low) for shape in matrices]
    full = jax.ShapeDtypeStruct((rows, width), jnp.float32)
    half = jax.ShapeDtypeStruct((rows, width), low)
    small = [jax.ShapeDtypeStruct((8, width), jnp.float32), jax.ShapeDtypeStruct((1, hidden), jnp.float32)]
    result = pl.pallas_call(
        functools.partial(ffn_kernel, direct, len(parts), tables, offsets, FFN_LAYOUT),
        grid=(rows // tile,),
        in_specs=[smem_spec(), block, block, whole((rows, width)), whole((rows, width))]
        + [whole(vectors.shape), whole((1, hidden))]
        + [whole(part.shape) for part in parts],
        out_specs=[block] * 4 + [whole(item.shape) for item in small + grads],
        out_shape=[half, half, full, full] + small + grads,
        scratch_shapes=scratch,
        name="ffn",
    )(own[None].astype(jnp.int32), tokens, cotangent, normed, mixed_heads, vectors, bias[None], *parts)
    if not direct:
        blocks = [grad.reshape(1, count, step, width) for grad in result[6:9]]
        blocks += [result[9].reshape(count, step, hidden), result[10].reshape(count, chunks, step, width)]
        result = list(result[:6]) + list(split(own, blocks, FFN_LAYOUT, groups))
    return result


def adam_update(weight, first_moment, second_moment, gradient, factor, step_rate):
    clipped = gradient * factor
    first_new = first_decay * first_moment + (1.0 - first_decay) * clipped
    second_new = second_decay * second_moment + (1.0 - second_decay) * clipped * clipped
    corrected = first_new / (1.0 - first_decay**STEP)
    spread = second_new / (1.0 - second_decay**STEP)
    weight_new = weight - step_rate * (
        corrected / (jnp.sqrt(spread) + adam_eps) + weight_decay * weight
    )
    return (weight_new, first_new, second_new)


def own_lanes(rows, first, lanes):
    width = rows.shape[1]
    return pltpu.roll(rows, (width - first) % width, 1)[:, :lanes]


def update_kernel(own_ref, payload_ref, a_ref, b_ref, *refs):
    states = [refs[3 * index : 3 * index + 3] for index in range(6)]
    norm_ref = refs[18]
    news = [refs[19 + 3 * index : 22 + 3 * index] for index in range(6)]
    squares = payload_ref[:11, :] * payload_ref[:11, :]
    total = jnp.sum(jnp.sum(squares, 1, keepdims=True), 0, keepdims=True)
    norm = jnp.sqrt(total + payload_ref[11:12, 0:1])
    norm_ref[...] = norm
    factor = jnp.minimum(1.0, clip_norm / (norm + 1e-06))

    def update(index, where, gradient):
        rate = vector_rate if index > 3 else learn_rate
        values = adam_update(*[ref[where] for ref in states[index]], gradient, factor, rate)
        for ref, value in zip(news[index], values):
            ref[where] = value

    width = a_ref.shape[2]
    for piece in range(3):
        update(0, piece, a_ref[piece])
    update(0, 3, b_ref[0])
    for piece in range(2):
        update(1, piece, b_ref[1 + piece])
    chunks = (b_ref.shape[0] - 3) // 2
    step = b_ref.shape[1]
    for chunk in range(chunks):
        update(2, (slice(None), slice(chunk * width, (chunk + 1) * width)), b_ref[3 + chunk])
        update(3, slice(chunk * step, (chunk + 1) * step), b_ref[3 + chunks + chunk])
    own = own_ref[0]
    vec_lanes = states[4][0].shape[1]
    update(4, Ellipsis, own_lanes(payload_ref[0:8, :], own * vec_lanes, vec_lanes)[:7])
    bias_lanes = states[5][0].shape[1]
    first = own * bias_lanes
    line = lax.broadcasted_iota(jnp.int32, (5, width), 0)
    picked = jnp.sum(jnp.where(line == first // width, payload_ref[7:12, :], 0.0), 0, keepdims=True)
    picked = own_lanes(jnp.broadcast_to(picked, (8, width)), first % width, bias_lanes)
    update(5, Ellipsis, picked[0:1])


def update_all(own, payload, total_a, total_b, states):
    flat = [value for state in states for value in state]
    shapes = [jax.ShapeDtypeStruct(value.shape, jnp.float32) for value in flat]
    norm, *news = pl.pallas_call(
        update_kernel,
        in_specs=[smem_spec()] + [vmem_spec() for _ in range(3 + len(flat))],
        out_specs=[vmem_spec() for _ in range(1 + len(flat))],
        out_shape=[jax.ShapeDtypeStruct((1, 1), jnp.float32)] + shapes,
        name="update",
    )(own[None].astype(jnp.int32), payload, total_a, total_b, *flat)
    return norm[0, 0], [news[3 * index : 3 * index + 3] for index in range(len(states))]


def body(
    groups,
    tokens,
    segments,
    positions,
    cotangent,
    attn_weight,
    attn_m,
    attn_v,
    gate_weight,
    gate_m,
    gate_v,
    in_weight,
    in_m,
    in_v,
    out_weight,
    out_m,
    out_v,
    norm_params,
    norm_m,
    norm_v,
    in_bias,
    bias_m,
    bias_v,
):
    count = 2 ** sum(groups)
    own = lax.axis_index(AXES)
    width = 512
    step = attn_weight.shape[1]
    low = lambda value: value.astype(jnp.bfloat16)
    dot = functools.partial(jnp.einsum, preferred_element_type=jnp.float32)
    columns = lambda value: [value[:, width * j : width * (j + 1)] for j in range(4)]
    small = pad_rows(small_shard(norm_params, in_bias, own, count, width), step)
    extra = small.shape[0]
    first_shard = jnp.concatenate([low(attn_weight[:3]), small])
    second_shard = jnp.concatenate(
        [
            low(attn_weight[3:]),
            low(gate_weight),
            jnp.stack(columns(low(in_weight))),
            low(out_weight).reshape(4, step, width),
        ]
    )
    cut = 6
    orders = plane_orders(groups)
    z_first = gather_z(first_shard, groups)
    plane_first = gather_plane(z_first, groups)
    z_second = gather_z(second_shard, groups)
    tied = tie(z_first, z_second[:, :cut], z_second[:, cut:], *plane_first)
    z_first, halves, plane_first = tied[0], tied[1:3], list(tied[3:])
    core_first = gather_core(z_first, plane_first, groups)
    tables = [z_offsets(groups)] * 2
    received = send_halves(halves, orders, 0, groups)
    inputs = tokens.astype(jnp.float32)
    mean_one = jnp.mean(inputs, -1, keepdims=True)
    scale_one = lax.rsqrt(jnp.mean((inputs - mean_one) * (inputs - mean_one), -1, keepdims=True) + norm_eps)
    marks = seg_args(segments, positions)
    core_first, mean_one, scale_one, *tied = tie(core_first, mean_one, scale_one, *marks, *received)
    marks, received = tied[:4], tied[4:]
    last = len(orders[0]) - 1
    for position in range(last):
        tables = [
            table + row
            for table, row in zip(tables, flip_tables(tables, [order[position] for order in orders]))
        ]
        halves = [jnp.concatenate(pair) for pair in zip(halves, received)]
        received = send_halves(halves, orders, position + 1, groups)
    far_tables = flip_tables(tables, [order[last] for order in orders])
    relative = offsets_of(groups)
    normed, queries, keys, values, mixed_heads, log_total, w_qkv, vectors = attend(
        own,
        tokens,
        marks,
        [z_first] + plane_first + [core_first],
        [(row, 0) for row in relative],
        [("stack", 0, 3), ("sum", 3, extra)],
        groups,
    )
    w_qkv = w_qkv.reshape(3, count * step, width)
    bias = vectors[7:11].reshape(-1)
    core_near = [swap_with(half, 1, count) for half in halves]
    mixed_heads, *tied = tie(mixed_heads, *core_near, *received)
    core_near, received = tied[:2], tied[2:]
    core_far = [swap_with(half, 1, count) for half in received]
    unit_one = (inputs - mean_one) * scale_one
    layer_out, grad_mixed, grad_normed, grad_inputs, sums, grad_bias, kept_b, sent_b = ffn(
        own,
        tokens,
        cotangent,
        normed,
        mixed_heads,
        vectors,
        bias,
        list(halves) + list(received) + list(core_near) + core_far,
        [
            ([offset | core for offset in table], first)
            for core in range(2)
            for half_tables in (tables, far_tables)
            for table, first in zip(half_tables, (0, cut))
        ],
        groups,
    )
    core_b = swap_with(sent_b, 1, count)
    core_b, kept_b, grad_mixed = tie(core_b, kept_b, grad_mixed)
    own_b, parts_b = plane_sums(kept_b, core_b, groups)
    own_b, log_total, *parts_b = tie(own_b, log_total, *parts_b)
    plane_b = plane_send(parts_b, groups)
    kept_a, sent_a, grad_normed = attend_back(
        own, queries, keys, values, grad_mixed, log_total, marks, normed, w_qkv, grad_normed, groups
    )
    kept_a, sent_a, grad_normed, own_b, *plane_b = tie(kept_a, sent_a, grad_normed, own_b, *plane_b)
    core_a = swap_with(sent_a, 1, count)
    own_b, z_b = reduce_z(own_b, plane_b, groups)
    own_a, parts_a = plane_sums(kept_a, core_a, groups)
    grad_normed, own_a, *parts_a = tie(grad_normed, own_a, *parts_a)
    grad_gain_one = jnp.sum(grad_normed * unit_one, 0)
    grad_shift_one = jnp.sum(grad_normed, 0)
    grad_inputs = grad_inputs + normalize_back(grad_normed, unit_one, scale_one, vectors[0])
    input_grad = low(grad_inputs)
    plane_a = plane_send(parts_a, groups)
    input_grad, grad_gain_one, grad_shift_one, *arrived = tie(
        input_grad, grad_gain_one, grad_shift_one, *z_b, *plane_a
    )
    z_b, plane_a = arrived[: len(z_b)], arrived[len(z_b) :]
    own_a, z_a = reduce_z(own_a, plane_a, groups)
    total_b = reduce_end(own_b, z_b)
    total_a = reduce_end(own_a, z_a)
    local_squares = jnp.sum(total_b * total_b) + jnp.sum(total_a * total_a)
    payload = jnp.concatenate(
        [
            grad_gain_one[None],
            grad_shift_one[None],
            sums[:5],
            grad_bias.reshape(4, width),
            jnp.full((1, width), local_squares),
        ]
    )
    payload = sum_all(payload, groups)
    states = (
        (attn_weight, attn_m, attn_v),
        (gate_weight, gate_m, gate_v),
        (in_weight, in_m, in_v),
        (out_weight, out_m, out_v),
        (norm_params, norm_m, norm_v),
        (in_bias[None], bias_m[None], bias_v[None]),
    )
    grad_norm, updated = update_all(own, payload, total_a, total_b, states)
    return (
        layer_out,
        input_grad,
        grad_norm,
        updated[0][0],
        updated[0][1],
        updated[0][2],
        updated[1][0],
        updated[1][1],
        updated[1][2],
        updated[2][0],
        updated[2][1],
        updated[2][2],
        updated[3][0],
        updated[3][1],
        updated[3][2],
        updated[4][0],
        updated[4][1],
        updated[4][2],
        updated[5][0][0],
        updated[5][1][0],
        updated[5][2][0],
    )


def solution(mesh):
    return jax.shard_map(
        functools.partial(body, bit_groups(mesh.shape)),
        mesh=mesh,
        in_specs=(
            P(("dp", "inner"), None),
            P(("dp", "inner")),
            P(("dp", "inner")),
            P(("dp", "inner"), None),
            P(None, ("dp", "inner"), None),
            P(None, ("dp", "inner"), None),
            P(None, ("dp", "inner"), None),
            P(None, ("dp", "inner"), None),
            P(None, ("dp", "inner"), None),
            P(None, ("dp", "inner"), None),
            P(("dp", "inner"), None),
            P(("dp", "inner"), None),
            P(("dp", "inner"), None),
            P(("dp", "inner"), None),
            P(("dp", "inner"), None),
            P(("dp", "inner"), None),
            P(None, ("dp", "inner")),
            P(None, ("dp", "inner")),
            P(None, ("dp", "inner")),
            P(("dp", "inner")),
            P(("dp", "inner")),
            P(("dp", "inner")),
        ),
        out_specs=(
            P(("dp", "inner"), None),
            P(("dp", "inner"), None),
            P(),
            P(None, ("dp", "inner"), None),
            P(None, ("dp", "inner"), None),
            P(None, ("dp", "inner"), None),
            P(None, ("dp", "inner"), None),
            P(None, ("dp", "inner"), None),
            P(None, ("dp", "inner"), None),
            P(("dp", "inner"), None),
            P(("dp", "inner"), None),
            P(("dp", "inner"), None),
            P(("dp", "inner"), None),
            P(("dp", "inner"), None),
            P(("dp", "inner"), None),
            P(None, ("dp", "inner")),
            P(None, ("dp", "inner")),
            P(None, ("dp", "inner")),
            P(("dp", "inner")),
            P(("dp", "inner")),
            P(("dp", "inner")),
        ),
        check_vma=False,
    )
```

```python
import functools
import jax
import jax.numpy as jnp
from jax import lax
from jax.experimental import pallas as pl
from jax.experimental.pallas import tpu as pltpu
from jax.sharding import PartitionSpec as P

AXES = ("dp", "inner")
HEADS = 8
HEAD = 64
STEP = 10
LOG2E = 1.4426950408889634
BLOCK = 256


norm_eps = 1e-05
first_decay = 0.9
second_decay = 0.999
adam_eps = 1e-08
learn_rate = 0.05
vector_rate = 0.8
weight_decay = 0.1
clip_norm = 1.0
masked_score = -1e30


def normalize_parts(values, gain_row, bias_row):
    centred = values - jnp.mean(values, -1, keepdims=True)
    spread = jnp.mean(centred * centred, -1, keepdims=True)
    scale_row = lax.rsqrt(spread + norm_eps)
    unit_rows = centred * scale_row
    return (unit_rows * gain_row + bias_row, unit_rows, scale_row)


def normalize_back(grad_rows, unit_rows, scale_row, gain_row):
    grad_unit = grad_rows * gain_row
    return scale_row * (
        grad_unit
        - jnp.mean(grad_unit, -1, keepdims=True)
        - unit_rows * jnp.mean(grad_unit * unit_rows, -1, keepdims=True)
    )


def bit_groups(sizes):
    dp_bits = sizes["dp"].bit_length() - 1
    inner_bits = sizes["inner"].bit_length() - 1
    y_bits = dp_bits // 2
    plane_bits = (inner_bits - 1) + y_bits
    return (1, plane_bits, dp_bits - y_bits)


def swap_with(array, offset, count):
    return lax.ppermute(array, AXES, [(source, source ^ offset) for source in range(count)])


def stage_bits(groups):
    return ((0, groups[0]), (groups[0], groups[1]), (groups[0] + groups[1], groups[2]))


def gather_z(shard, groups):
    count = 2 ** sum(groups)
    first_bit, bits = stage_bits(groups)[2]
    return jnp.stack([shard] + [swap_with(shard, offset << first_bit, count) for offset in range(1, 2**bits)])


def gather_plane(column, groups):
    count = 2 ** sum(groups)
    first_bit, bits = stage_bits(groups)[1]
    return [swap_with(column, offset << first_bit, count) for offset in range(1, 2**bits)]


def gather_core(column, planes, groups):
    return swap_with(jnp.concatenate([column] + planes), 1, 2 ** sum(groups))


def offsets_of(groups):
    (_, _), (plane_bit, plane_bits), (z_bit, z_bits) = stage_bits(groups)
    table = [
        [(plane << plane_bit) | (z << z_bit) for z in range(2**z_bits)] for plane in range(2**plane_bits)
    ]
    return table + [[offset | 1 for row in table for offset in row]]


def plane_orders(groups):
    _, (first_bit, bits), _ = stage_bits(groups)
    order = list(range(first_bit, first_bit + bits))
    return order, order[bits // 2 :] + order[: bits // 2]


def z_offsets(groups):
    _, _, (first_bit, bits) = stage_bits(groups)
    return [z << first_bit for z in range(2**bits)]


def send_halves(arrays, orders, position, groups):
    count = 2 ** sum(groups)
    return [swap_with(array, 1 << order[position], count) for array, order in zip(arrays, orders)]


def flip_tables(tables, bits):
    return [[offset ^ (1 << bit) for offset in table] for table, bit in zip(tables, bits)]


def vmem_spec():
    return pl.BlockSpec(memory_space=pltpu.VMEM)


def smem_spec():
    return pl.BlockSpec(memory_space=pltpu.SMEM)


def place(own, parts, tables, layout, groups):
    count = 2 ** sum(groups)
    step, width = parts[0].shape[2:]
    firsts = sorted({first for _, first in tables})
    groups_of = []
    for first in firsts:
        chosen = [(part, row) for part, (row, base) in zip(parts, tables) if base == first]
        order = jnp.argsort(jnp.array([o for _, row in chosen for o in row]) ^ own)
        groups_of.append(jnp.concatenate([part for part, _ in chosen])[order])
    full = jnp.concatenate(groups_of, 1)
    result = []
    for kind, first, pieces in layout:
        chosen = full[:, first : first + pieces]
        if kind == "sum":
            result.append(jnp.sum(chosen.astype(jnp.float32), 0).reshape(pieces * step, width))
        elif kind == "stack":
            result.append(jnp.moveaxis(chosen, 0, 1))
        elif kind == "rows":
            result.append(chosen)
        else:
            result.append(jnp.moveaxis(chosen, 1, 2).reshape(count, step, pieces * width))
    return result


def split(own, grads, layout, groups):
    count = 2 ** sum(groups)
    width = 512
    step = grads[0].shape[-2]
    offsets = [offset for row in offsets_of(groups)[:-1] for offset in row]
    pieces_of = []
    for grad, (kind, _, pieces) in zip(grads, layout):
        if kind == "stack":
            grad = jnp.moveaxis(grad, 1, 0)
        elif kind == "columns":
            grad = jnp.moveaxis(grad.reshape(count, step, pieces, width), 2, 1)
        pieces_of.append(grad)
    full = jnp.concatenate(pieces_of, 1)
    order = jnp.array(offsets) ^ own
    return full[order], full[order ^ 1]


def plane_sums(kept, received, groups):
    _, (_, bits), (_, z_bits) = stage_bits(groups)
    shape = (2**bits, 2**z_bits) + kept.shape[1:]
    kept = kept.reshape(shape)
    received = received.reshape(shape)
    total = lambda offset: kept[offset].astype(jnp.float32) + received[offset].astype(jnp.float32)
    return total(0), [total(offset).astype(jnp.bfloat16) for offset in range(1, 2**bits)]


def plane_send(parts, groups):
    first_bit = stage_bits(groups)[1][0]
    return [swap_with(part, offset << first_bit, 2 ** sum(groups)) for offset, part in enumerate(parts, 1)]


def reduce_z(own_part, arrived, groups):
    count = 2 ** sum(groups)
    first_bit, bits = stage_bits(groups)[2]
    total = lambda z: own_part[z] + sum(part[z].astype(jnp.float32) for part in arrived)
    return total(0), [
        swap_with(total(z).astype(jnp.bfloat16), z << first_bit, count) for z in range(2**bits - 1, 0, -1)
    ]


def reduce_end(own_part, arrived):
    return own_part + sum(part.astype(jnp.float32) for part in arrived)


def sum_all(value, groups):
    count = 2 ** sum(groups)
    for first_bit, bits in stage_bits(groups):
        values = [value] + [swap_with(value, offset << first_bit, count) for offset in range(1, 2**bits)]
        while len(values) > 1:
            values = [one + two for one, two in zip(values[::2], values[1::2])]
        value = values[0]
    return value


def tie(*values):
    return lax.optimization_barrier(values)


def small_shard(vec, bias, own, count, width):
    step = vec.shape[1]
    lane = lax.broadcasted_iota(jnp.int32, (7, width), 1)
    rows = jnp.where(lane // step == own, jnp.tile(vec, (1, count)), 0.0)
    place_of = lax.broadcasted_iota(jnp.int32, (4, width), 0) * width + lax.broadcasted_iota(
        jnp.int32, (4, width), 1
    )
    tiled = jnp.tile(bias, width // bias.shape[0])[None]
    bias_rows = jnp.where(place_of // bias.shape[0] == own, tiled, 0.0)
    return jnp.concatenate([rows, bias_rows])


def pad_rows(rows, step):
    pieces = -(-rows.shape[0] // step)
    rows = jnp.pad(rows.astype(jnp.bfloat16), ((0, pieces * step - rows.shape[0]), (0, 0)))
    return rows.reshape(pieces, step, rows.shape[1])


def mat(a,b,dims):
    return lax.dot_general(a,b,(dims,((),())),preferred_element_type=jnp.float32)

def fill_bias(bias_ref, seg_row, pos_row):
    rows = bias_ref.shape[0]
    step = min(BLOCK, rows)
    for first in range(0, rows, step):
        seg_keys, pos_keys = [
            jnp.broadcast_to(ref[:, first : first + step], (8, step)).T[:, 0:1] for ref in (seg_row, pos_row)
        ]
        allowed = (seg_keys == seg_row[:, first:]) & (pos_keys <= pos_row[:, first:])
        bias_ref[first : first + step, first:] = jnp.where(allowed, 0.0, masked_score)


def head_lanes(shape, which):
    lane=lax.broadcasted_iota(jnp.int32,shape,1)
    return (lane//HEAD)==which

def attn_fwd_kernel(direct, tables, layout, own_ref, segr, posr, x_ref, *refs):
    part_count = len(tables) if direct else 2
    parts = refs[:part_count]
    h_ref, q_ref, k_ref, v_ref, o_ref, lse_ref, *rest = refs[part_count:]
    bias_ref, q_all, k_all, v_all = rest[-4:]
    rows = x_ref.shape[0]
    step = min(BLOCK, rows)
    lanes = q_ref.shape[1]
    pair = lanes // HEAD
    const = HEAD**-0.5 * LOG2E
    low = lambda value: value.astype(jnp.bfloat16)
    weights, vectors = rest[:2] if direct else parts
    tile = pl.program_id(0)

    @pl.when(tile == 0)
    def _():
        if direct:
            copy_parts(tables, layout, own_ref[0], parts, [weights, vectors])
        fill_bias(bias_ref, segr, posr)
        for first in range(0, rows, step):
            x = x_ref[first : first + step, :].astype(jnp.float32)
            h_ref[first : first + step, :] = low(normalize_parts(x, vectors[0:1, :], vectors[1:2, :])[0])
        for j, target in enumerate((q_all, k_all, v_all)):
            whole = low(mat(h_ref[...], weights[j].reshape(-1, weights.shape[-1]), ((1,), (0,))))
            for which in range(target.shape[0]):
                target[which] = whole[:, which * lanes : (which + 1) * lanes]

    q_ref[...] = q_all[tile]
    k_ref[...] = k_all[tile]
    v_ref[...] = v_all[tile]
    for first in range(0, rows, step):
        keys = first + step
        q = q_ref[first:keys, :]
        mixed = None
        for which in range(pair):
            own = head_lanes(q.shape, which)
            qh = jnp.where(own, q, jnp.zeros_like(q))
            s = mat(k_ref[:keys, :], qh, ((1,), (1,))) * const + bias_ref[:keys, first:keys]
            m = jnp.max(s, 0, keepdims=True)
            w = jnp.exp2(s - m)
            total = jnp.sum(w, 0, keepdims=True)
            p = (w * (1.0 / total)).astype(jnp.bfloat16)
            o = mat(p, v_ref[:keys, :], ((0,), (0,)))
            mixed = o if mixed is None else jnp.where(own, o, mixed)
            lse_ref[0, which : which + 1, first:keys] = m + jnp.log2(total)
        o_ref[first:keys, :] = mixed.astype(jnp.bfloat16)


def attn_bwd_kernel(
    offsets, own_ref, segr, posr, q_ref, k_ref, v_ref, do_ref, lse_ref, h_ref, w_ref, start_ref, *refs
):
    *outs, dh_ref, bias_ref, dk_acc, dv_acc, ht_ref, dw_ref = refs
    rows = q_ref.shape[0]

    @pl.when(pl.program_id(0) == 0)
    def _():
        fill_bias(bias_ref, segr, posr)
        ht_ref[...] = h_ref[...].T
        dh_ref[...] = start_ref[...]

    step = min(BLOCK, rows)
    pair = q_ref.shape[1] // HEAD
    const = HEAD**-0.5 * LOG2E
    scale = HEAD**-0.5
    dk_acc[...] = jnp.zeros_like(dk_acc)
    dv_acc[...] = jnp.zeros_like(dv_acc)
    dq_parts = []
    for first in range(0, rows, step):
        keys = first + step
        q = q_ref[first:keys, :]
        do = do_ref[first:keys, :]
        dq = None
        for which in range(pair):
            own = head_lanes(q.shape, which)
            qh = jnp.where(own, q, jnp.zeros_like(q))
            doh = jnp.where(own, do, jnp.zeros_like(do))
            s = mat(k_ref[:keys, :], qh, ((1,), (1,)))
            p = jnp.exp2(s * const + (bias_ref[:keys, first:keys] - lse_ref[0, which : which + 1, first:keys]))
            dp = mat(v_ref[:keys, :], doh, ((1,), (1,)))
            inner = jnp.sum(p * dp, 0, keepdims=True)
            ds = (p * (dp - inner)).astype(jnp.bfloat16)
            dv_acc[:keys, :] += mat(p.astype(jnp.bfloat16), doh, ((1,), (0,)))
            dk_acc[:keys, :] += mat(ds, qh, ((1,), (0,)))
            d = mat(ds, k_ref[:keys, :], ((0,), (0,)))
            dq = d if dq is None else jnp.where(own, d, dq)
        dq_parts.append((dq * scale).astype(jnp.bfloat16))
    grads = jnp.concatenate(
        [
            jnp.concatenate(dq_parts, 0),
            (dk_acc[...] * scale).astype(jnp.bfloat16),
            dv_acc[...].astype(jnp.bfloat16),
        ],
        1,
    )
    weights = jnp.concatenate([w_ref[0], w_ref[1], w_ref[2]], 1)
    dh_ref[...] += mat(grads, weights, ((1,), (1,)))
    dw = mat(ht_ref[...], grads, ((1,), (0,))).astype(jnp.bfloat16)
    lanes = q_ref.shape[1]
    if offsets is None:
        for j in range(3):
            outs[0][j] = dw[:, j * lanes : (j + 1) * lanes]
    else:
        dw_ref[...] = dw.reshape(dw_ref.shape)
        for entry, offset in enumerate(offsets):
            for side in range(2):
                owner = own_ref[0] ^ (offset | side)
                for j in range(3):
                    outs[side][entry, j] = dw_ref[owner, :, j * lanes : (j + 1) * lanes]


def const_map(*_): return (0,0)

def attend(own, tokens, marks, parts, tables, layout, groups):
    rows, width = tokens.shape
    count = 2 ** sum(groups)
    step = parts[0].shape[2]
    lanes = 2 * HEAD
    pairs = width // lanes
    low = jnp.bfloat16
    direct = step % 16 == 0
    blk = pl.BlockSpec((rows, lanes), lambda j: (0, j))
    whole = lambda shape: pl.BlockSpec(shape, lambda j: (0,) * len(shape), pipeline_mode=pl.Buffered(1))
    half = jax.ShapeDtypeStruct((rows, width), low)
    out_shape = [half] * 5 + [jax.ShapeDtypeStruct((pairs, 2, rows), jnp.float32)]
    out_specs = [whole((rows, width)), blk, blk, blk, blk, pl.BlockSpec((1, 2, rows), lambda j: (j, 0, 0))]
    if direct:
        extra = [
            jax.ShapeDtypeStruct((3, count, step, width), low),
            jax.ShapeDtypeStruct((step, width), jnp.float32),
        ]
        out_shape += extra
        out_specs += [whole(item.shape) for item in extra]
    else:
        parts = place(own, parts, tables, layout, groups)
    result = pl.pallas_call(
        functools.partial(attn_fwd_kernel, direct, tables, layout),
        grid=(pairs,),
        in_specs=[smem_spec(), whole((1, rows)), whole((1, rows))]
        + [whole((rows, width))]
        + [whole(part.shape) for part in parts],
        out_specs=out_specs,
        out_shape=out_shape,
        scratch_shapes=[pltpu.VMEM((rows, rows), jnp.float32)] + [pltpu.VMEM((pairs, rows, lanes), low)] * 3,
        name="attn_fwd",
    )(own[None].astype(jnp.int32), *marks, tokens, *parts)
    if not direct:
        result = list(result) + list(parts)
    return result


def attend_back(own, q, k, v, do, lse, marks, normed, w_qkv, start, groups):
    rows, width = q.shape
    lanes = 2 * HEAD
    count = 2 ** sum(groups)
    inputs = w_qkv.shape[1]
    step = inputs // count
    blk = pl.BlockSpec((rows, lanes), lambda j: (0, j))
    row = pl.BlockSpec((1, rows), const_map)
    offsets = None
    if step % 16 == 0:
        offsets = [offset for table in offsets_of(groups)[:-1] for offset in table]
        shape = (len(offsets), 3, step, width)
        out_specs = [pl.BlockSpec(shape[:3] + (lanes,), lambda j: (0, 0, 0, j)) for _ in range(2)]
        out_shape = [jax.ShapeDtypeStruct(shape, jnp.bfloat16) for _ in range(2)]
        dw_scratch = pltpu.VMEM((count, step, 3 * lanes), jnp.bfloat16)
    else:
        out_specs = [pl.BlockSpec((3, inputs, lanes), lambda j: (0, 0, j))]
        out_shape = [jax.ShapeDtypeStruct((3, inputs, width), jnp.bfloat16)]
        dw_scratch = pltpu.VMEM((16, lanes), jnp.bfloat16)
    *grads, dh = pl.pallas_call(
        functools.partial(attn_bwd_kernel, offsets),
        grid=(width // lanes,),
        in_specs=[smem_spec(), row, row, blk, blk, blk, blk]
        + [
            pl.BlockSpec((1, 2, rows), lambda j: (j, 0, 0)),
            pl.BlockSpec((rows, inputs), const_map),
            pl.BlockSpec((3, inputs, lanes), lambda j: (0, 0, j)),
            pl.BlockSpec((rows, inputs), const_map),
        ],
        out_specs=out_specs + [pl.BlockSpec((rows, inputs), const_map)],
        out_shape=out_shape + [jax.ShapeDtypeStruct((rows, inputs), jnp.float32)],
        scratch_shapes=[
            pltpu.VMEM((rows, rows), jnp.float32),
            pltpu.VMEM((rows, lanes), jnp.float32),
            pltpu.VMEM((rows, lanes), jnp.float32),
            pltpu.VMEM((inputs, rows), jnp.bfloat16),
            dw_scratch,
        ],
        name="attn_bwd",
    )(own[None].astype(jnp.int32), *marks, q, k, v, do, lse, normed, w_qkv, start)
    if offsets is None:
        grads = split(own, [grads[0].reshape(3, count, step, width)], [("stack", 0, 3)], groups)
    return grads[0], grads[1], dh


def copy_parts(tables, layout, own, parts, outs):
    where_to = [
        (index, kind, piece) for index, (kind, _, pieces) in enumerate(layout) for piece in range(pieces)
    ]
    total = None
    for part, (row, first) in zip(parts, tables):
        width = part.shape[3]
        for entry, offset in enumerate(row):
            owner = own ^ offset
            for source in range(part.shape[1]):
                index, kind, piece = where_to[first + source]
                block = part[entry, source]
                if kind == "sum":
                    block = block.astype(jnp.float32)
                    total = block if total is None else total + block
                elif kind == "stack":
                    outs[index][piece, owner] = block
                elif kind == "rows":
                    outs[index][owner, piece] = block
                else:
                    outs[index][owner, :, piece * width : (piece + 1) * width] = block
    for index, (kind, _, _) in enumerate(layout):
        if kind == "sum":
            outs[index][...] = total


def copy_blocks(offsets, layout, own, ins, kept, sent):
    width = kept.shape[3]
    for entry, offset in enumerate(offsets):
        for side, target in enumerate((kept, sent)):
            owner = own ^ (offset | side)
            for index, (kind, first, pieces) in enumerate(layout):
                for piece in range(pieces):
                    if kind == "stack":
                        block = ins[index][piece, owner]
                    elif kind == "rows":
                        block = ins[index][owner, piece]
                    else:
                        block = ins[index][owner, :, piece * width : (piece + 1) * width]
                    target[entry, first + piece] = block


def ffn_kernel(direct, part_count, tables, offsets, layout, own_ref, x_ref, cot_ref, h_ref, o_ref, vec_ref, *refs):
    low = lambda value: value.astype(jnp.bfloat16)
    parts = refs[:part_count]
    out_count = 5 + (2 if direct else 5)
    outs = refs[part_count : part_count + out_count]
    scratch = refs[part_count + out_count :]
    y_ref, do_ref, dh_ref, dx_ref, dvec_ref = outs[:5]
    r_ref, dz_ref, h2_ref, df_ref, dzf_ref, da_ref, dza_ref = scratch[:7]
    tile = pl.program_id(0)
    if direct:
        weights = targets = scratch[7:]

        @pl.when(tile == 0)
        def _():
            copy_parts(tables, layout, own_ref[0], parts, weights)

    else:
        weights, targets = parts, outs[5:]
    width = x_ref.shape[1]
    size = x_ref.shape[0]
    chunks = r_ref.shape[0]
    load = lambda index: weights[index][...].reshape(-1, weights[index].shape[-1])
    rows = pl.ds(tile * size, size)

    @pl.when(tile == 0)
    def _():
        dvec_ref[...] = jnp.zeros_like(dvec_ref)

    forward = ((1,), (0,))
    backward = ((1,), (1,))
    x = x_ref[...].astype(jnp.float32)
    a = mat(o_ref[rows, :], load(0), forward)
    ga = jax.nn.sigmoid(mat(h_ref[rows, :], load(1), forward) + vec_ref[4:5, :])
    x1 = ga * a + (1.0 - ga) * x
    gain = vec_ref[2:3, :]
    h2_full, n2, s2 = normalize_parts(x1, gain, vec_ref[3:4, :])
    h2 = low(h2_full)
    bias = jnp.concatenate([vec_ref[7 + chunk : 8 + chunk, :] for chunk in range(chunks)], 1)
    z = mat(h2, load(3), forward) + bias
    r = low(jnp.maximum(z, 0.0))
    f = mat(r, load(4), forward) + vec_ref[6:7, :]
    gf = jax.nn.sigmoid(mat(h2, load(2), forward) + vec_ref[5:6, :])
    y_ref[...] = low(gf * f + (1.0 - gf) * x1)
    dy = cot_ref[...].astype(jnp.float32)
    df = dy * gf
    dzf = dy * (f - x1) * gf * (1.0 - gf)
    dx1 = dy * (1.0 - gf)
    dfb = low(df)
    dzfb = low(dzf)
    dz = jnp.where(z > 0.0, mat(dfb, load(4), backward), 0.0)
    dzb = low(dz)
    dh2 = mat(dzb, load(3), backward) + mat(dzfb, load(2), backward)
    dx1 = dx1 + normalize_back(dh2, n2, s2, gain)
    da = low(dx1 * ga)
    dza = dx1 * (a - x) * ga * (1.0 - ga)
    dzab = low(dza)
    dx_ref[...] = dx1 * (1.0 - ga)
    do_ref[...] = low(mat(da, load(0), backward))
    dh_ref[...] = mat(dzab, load(1), backward)
    total = lambda value: jnp.sum(value, 0, keepdims=True)
    sums = [total(dh2 * n2), total(dh2), total(dza), total(dzf), total(df)]
    hidden_sums = total(dz)
    sums += [hidden_sums[:, chunk * width : (chunk + 1) * width] for chunk in range(chunks)]
    for index, value in enumerate(sums):
        dvec_ref[2 + index : 3 + index, :] += value
    for chunk in range(chunks):
        r_ref[chunk, rows, :] = r[:, chunk * width : (chunk + 1) * width]
        dz_ref[chunk, rows, :] = dzb[:, chunk * width : (chunk + 1) * width]
    h2_ref[rows, :] = h2
    df_ref[rows, :] = dfb
    dzf_ref[rows, :] = dzfb
    da_ref[rows, :] = da
    dza_ref[rows, :] = dzab

    @pl.when(tile == pl.num_programs(0) - 1)
    def _():
        across = lambda left, right: low(mat(left, right, forward))
        targets[0][...] = across(o_ref[...].T, da_ref[...]).reshape(targets[0].shape)
        targets[1][...] = across(h_ref[...].T, dza_ref[...]).reshape(targets[1].shape)
        h2_turned = h2_ref[...].T
        targets[2][...] = across(h2_turned, dzf_ref[...]).reshape(targets[2].shape)
        for chunk in range(chunks):
            lanes = slice(chunk * width, (chunk + 1) * width)
            grad_in = across(h2_turned, dz_ref[chunk])
            grad_out = across(r_ref[chunk].T, df_ref[...])
            if direct:
                owners = targets[4].shape[0] // chunks
                targets[3][:, :, lanes] = grad_in.reshape(targets[3].shape[:2] + (width,))
                targets[4][chunk * owners : (chunk + 1) * owners] = grad_out.reshape(
                    (owners,) + targets[4].shape[1:]
                )
            else:
                targets[3][:, lanes] = grad_in
                targets[4][lanes, :] = grad_out
        if direct:
            copy_blocks(offsets, layout, own_ref[0], targets, *outs[5:])


FFN_LAYOUT = [("stack", 0, 1), ("stack", 1, 1), ("stack", 2, 1), ("columns", 3, 4), ("rows", 7, 4)]


def ffn(own, tokens, cotangent, normed, mixed_heads, vectors, hidden, parts, tables, groups):
    rows, width = tokens.shape
    count = 2 ** sum(groups)
    step = parts[0].shape[2]
    chunks = hidden // width
    tile = min(256, rows)
    direct = step % 16 == 0
    offsets = [offset for row in offsets_of(groups)[:-1] for offset in row]
    matrices = [(width, width)] * 3 + [(width, hidden), (hidden, width)]
    low = jnp.bfloat16
    once = dict(pipeline_mode=pl.Buffered(1))
    block = pl.BlockSpec((tile, width), lambda i: (i, 0))
    whole = lambda shape: pl.BlockSpec(shape, lambda i: (0,) * len(shape), **once)
    scratch = [pltpu.VMEM((chunks, rows, width), low)] * 2 + [pltpu.VMEM((rows, width), low)] * 5
    if direct:
        shape = (len(offsets), 3 + 2 * chunks, step, width)
        grads = [jax.ShapeDtypeStruct(shape, low)] * 2
        scratch += [pltpu.VMEM((1, count, step, width), low)] * 3
        scratch += [pltpu.VMEM((count, step, hidden), low), pltpu.VMEM((count, chunks, step, width), low)]
    else:
        placed = place(own, parts, tables, FFN_LAYOUT, groups)
        parts = [weight.reshape(shape) for weight, shape in zip(placed, matrices)]
        grads = [jax.ShapeDtypeStruct(shape, low) for shape in matrices]
    full = jax.ShapeDtypeStruct((rows, width), jnp.float32)
    half = jax.ShapeDtypeStruct((rows, width), low)
    small = [jax.ShapeDtypeStruct((12, width), jnp.float32)]
    result = pl.pallas_call(
        functools.partial(ffn_kernel, direct, len(parts), tables, offsets, FFN_LAYOUT),
        grid=(rows // tile,),
        in_specs=[smem_spec(), block, block, whole((rows, width)), whole((rows, width))]
        + [whole(vectors.shape)]
        + [whole(part.shape) for part in parts],
        out_specs=[block] * 4 + [whole(item.shape) for item in small + grads],
        out_shape=[half, half, full, full] + small + grads,
        scratch_shapes=scratch,
        name="ffn",
    )(own[None].astype(jnp.int32), tokens, cotangent, normed, mixed_heads, vectors, *parts)
    if not direct:
        blocks = [grad.reshape(1, count, step, width) for grad in result[5:8]]
        blocks += [result[8].reshape(count, step, hidden), result[9].reshape(count, chunks, step, width)]
        result = list(result[:5]) + list(split(own, blocks, FFN_LAYOUT, groups))
    return result


def adam_update(weight, first_moment, second_moment, gradient, factor, step_rate):
    clipped = gradient * factor
    first_new = first_decay * first_moment + (1.0 - first_decay) * clipped
    second_new = second_decay * second_moment + (1.0 - second_decay) * clipped * clipped
    corrected = first_new / (1.0 - first_decay**STEP)
    spread = second_new / (1.0 - second_decay**STEP)
    weight_new = weight - step_rate * (
        corrected / (jnp.sqrt(spread) + adam_eps) + weight_decay * weight
    )
    return (weight_new, first_new, second_new)


def own_lanes(rows, first, lanes):
    width = rows.shape[1]
    return pltpu.roll(rows, (width - first) % width, 1)[:, :lanes]


def update_kernel(own_ref, payload_ref, a_ref, b_ref, *refs):
    states = [refs[3 * index : 3 * index + 3] for index in range(6)]
    norm_ref = refs[18]
    news = [refs[19 + 3 * index : 22 + 3 * index] for index in range(6)]
    squares = payload_ref[:11, :] * payload_ref[:11, :]
    total = jnp.sum(jnp.sum(squares, 1, keepdims=True), 0, keepdims=True)
    norm = jnp.sqrt(total + payload_ref[11:12, 0:1])
    norm_ref[...] = norm
    factor = jnp.minimum(1.0, clip_norm / (norm + 1e-06))

    def update(index, where, gradient):
        rate = vector_rate if index > 3 else learn_rate
        values = adam_update(*[ref[where] for ref in states[index]], gradient, factor, rate)
        for ref, value in zip(news[index], values):
            ref[where] = value

    width = a_ref.shape[2]
    for piece in range(3):
        update(0, piece, a_ref[piece])
    update(0, 3, b_ref[0])
    for piece in range(2):
        update(1, piece, b_ref[1 + piece])
    chunks = (b_ref.shape[0] - 3) // 2
    step = b_ref.shape[1]
    for chunk in range(chunks):
        update(2, (slice(None), slice(chunk * width, (chunk + 1) * width)), b_ref[3 + chunk])
        update(3, slice(chunk * step, (chunk + 1) * step), b_ref[3 + chunks + chunk])
    own = own_ref[0]
    vec_lanes = states[4][0].shape[1]
    update(4, Ellipsis, own_lanes(payload_ref[0:8, :], own * vec_lanes, vec_lanes)[:7])
    bias_lanes = states[5][0].shape[1]
    first = own * bias_lanes
    line = lax.broadcasted_iota(jnp.int32, (5, width), 0)
    picked = jnp.sum(jnp.where(line == first // width, payload_ref[7:12, :], 0.0), 0, keepdims=True)
    picked = own_lanes(jnp.broadcast_to(picked, (8, width)), first % width, bias_lanes)
    update(5, Ellipsis, picked[0:1])


def update_all(own, payload, total_a, total_b, states):
    flat = [value for state in states for value in state]
    shapes = [jax.ShapeDtypeStruct(value.shape, jnp.float32) for value in flat]
    norm, *news = pl.pallas_call(
        update_kernel,
        in_specs=[smem_spec()] + [vmem_spec() for _ in range(3 + len(flat))],
        out_specs=[vmem_spec() for _ in range(1 + len(flat))],
        out_shape=[jax.ShapeDtypeStruct((1, 1), jnp.float32)] + shapes,
        name="update",
    )(own[None].astype(jnp.int32), payload, total_a, total_b, *flat)
    return norm[0, 0], [news[3 * index : 3 * index + 3] for index in range(len(states))]


def body(
    groups,
    tokens,
    segments,
    positions,
    cotangent,
    attn_weight,
    attn_m,
    attn_v,
    gate_weight,
    gate_m,
    gate_v,
    in_weight,
    in_m,
    in_v,
    out_weight,
    out_m,
    out_v,
    norm_params,
    norm_m,
    norm_v,
    in_bias,
    bias_m,
    bias_v,
):
    count = 2 ** sum(groups)
    own = lax.axis_index(AXES)
    width = 512
    step = attn_weight.shape[1]
    low = lambda value: value.astype(jnp.bfloat16)
    dot = functools.partial(jnp.einsum, preferred_element_type=jnp.float32)
    columns = lambda value: [value[:, width * j : width * (j + 1)] for j in range(4)]
    small = pad_rows(small_shard(norm_params, in_bias, own, count, width), step)
    extra = small.shape[0]
    first_shard = jnp.concatenate([low(attn_weight[:3]), small])
    second_shard = jnp.concatenate(
        [
            low(attn_weight[3:]),
            low(gate_weight),
            jnp.stack(columns(low(in_weight))),
            low(out_weight).reshape(4, step, width),
        ]
    )
    cut = 6
    orders = plane_orders(groups)
    z_first = gather_z(first_shard, groups)
    plane_first = gather_plane(z_first, groups)
    z_second = gather_z(second_shard, groups)
    tied = tie(z_first, z_second[:, :cut], z_second[:, cut:], *plane_first)
    z_first, halves, plane_first = tied[0], tied[1:3], list(tied[3:])
    core_first = gather_core(z_first, plane_first, groups)
    tables = [z_offsets(groups)] * 2
    received = send_halves(halves, orders, 0, groups)
    inputs = tokens.astype(jnp.float32)
    mean_one = jnp.mean(inputs, -1, keepdims=True)
    scale_one = lax.rsqrt(jnp.mean((inputs - mean_one) * (inputs - mean_one), -1, keepdims=True) + norm_eps)
    marks = (segments[None], positions[None])
    core_first, mean_one, scale_one, *tied = tie(core_first, mean_one, scale_one, *marks, *received)
    marks, received = tied[:2], tied[2:]
    last = len(orders[0]) - 1
    for position in range(last):
        tables = [
            table + row
            for table, row in zip(tables, flip_tables(tables, [order[position] for order in orders]))
        ]
        halves = [jnp.concatenate(pair) for pair in zip(halves, received)]
        received = send_halves(halves, orders, position + 1, groups)
    far_tables = flip_tables(tables, [order[last] for order in orders])
    relative = offsets_of(groups)
    normed, queries, keys, values, mixed_heads, log_total, w_qkv, vectors = attend(
        own,
        tokens,
        marks,
        [z_first] + plane_first + [core_first],
        [(row, 0) for row in relative],
        [("stack", 0, 3), ("sum", 3, extra)],
        groups,
    )
    w_qkv = w_qkv.reshape(3, count * step, width)
    core_near = [swap_with(half, 1, count) for half in halves]
    mixed_heads, gain_one, *tied = tie(mixed_heads, vectors[0], *core_near, *received)
    core_near, received = tied[:2], tied[2:]
    core_far = [swap_with(half, 1, count) for half in received]
    unit_one = (inputs - mean_one) * scale_one
    layer_out, grad_mixed, grad_normed, grad_inputs, sums, kept_b, sent_b = ffn(
        own,
        tokens,
        cotangent,
        normed,
        mixed_heads,
        vectors,
        in_weight.shape[1],
        list(halves) + list(received) + list(core_near) + core_far,
        [
            ([offset | core for offset in table], first)
            for core in range(2)
            for half_tables in (tables, far_tables)
            for table, first in zip(half_tables, (0, cut))
        ],
        groups,
    )
    core_b = swap_with(sent_b, 1, count)
    core_b, kept_b, grad_mixed = tie(core_b, kept_b, grad_mixed)
    own_b, parts_b = plane_sums(kept_b, core_b, groups)
    own_b, log_total, *parts_b = tie(own_b, log_total, *parts_b)
    plane_b = plane_send(parts_b, groups)
    kept_a, sent_a, grad_normed = attend_back(
        own, queries, keys, values, grad_mixed, log_total, marks, normed, w_qkv, grad_normed, groups
    )
    kept_a, sent_a, grad_normed, own_b, *plane_b = tie(kept_a, sent_a, grad_normed, own_b, *plane_b)
    core_a = swap_with(sent_a, 1, count)
    own_b, z_b = reduce_z(own_b, plane_b, groups)
    own_a, parts_a = plane_sums(kept_a, core_a, groups)
    grad_normed, own_a, *parts_a = tie(grad_normed, own_a, *parts_a)
    grad_gain_one = jnp.sum(grad_normed * unit_one, 0)
    grad_shift_one = jnp.sum(grad_normed, 0)
    grad_inputs = grad_inputs + normalize_back(grad_normed, unit_one, scale_one, gain_one)
    input_grad = low(grad_inputs)
    plane_a = plane_send(parts_a, groups)
    input_grad, grad_gain_one, grad_shift_one, *plane_a = tie(
        input_grad, grad_gain_one, grad_shift_one, *plane_a
    )
    own_a, z_a = reduce_z(own_a, plane_a, groups)
    total_b = reduce_end(own_b, z_b)
    total_a = reduce_end(own_a, z_a)
    local_squares = jnp.sum(total_b * total_b) + jnp.sum(total_a * total_a)
    line = lax.broadcasted_iota(jnp.int32, sums.shape, 0)
    payload = jnp.where(line == 0, grad_gain_one, jnp.where(line == 1, grad_shift_one, sums))
    payload = jnp.where(line == 11, local_squares, payload)
    payload = sum_all(payload, groups)
    states = (
        (attn_weight, attn_m, attn_v),
        (gate_weight, gate_m, gate_v),
        (in_weight, in_m, in_v),
        (out_weight, out_m, out_v),
        (norm_params, norm_m, norm_v),
        (in_bias[None], bias_m[None], bias_v[None]),
    )
    grad_norm, updated = update_all(own, payload, total_a, total_b, states)
    return (
        layer_out,
        input_grad,
        grad_norm,
        updated[0][0],
        updated[0][1],
        updated[0][2],
        updated[1][0],
        updated[1][1],
        updated[1][2],
        updated[2][0],
        updated[2][1],
        updated[2][2],
        updated[3][0],
        updated[3][1],
        updated[3][2],
        updated[4][0],
        updated[4][1],
        updated[4][2],
        updated[5][0][0],
        updated[5][1][0],
        updated[5][2][0],
    )


def solution(mesh):
    return jax.shard_map(
        functools.partial(body, bit_groups(mesh.shape)),
        mesh=mesh,
        in_specs=(
            P(("dp", "inner"), None),
            P(("dp", "inner")),
            P(("dp", "inner")),
            P(("dp", "inner"), None),
            P(None, ("dp", "inner"), None),
            P(None, ("dp", "inner"), None),
            P(None, ("dp", "inner"), None),
            P(None, ("dp", "inner"), None),
            P(None, ("dp", "inner"), None),
            P(None, ("dp", "inner"), None),
            P(("dp", "inner"), None),
            P(("dp", "inner"), None),
            P(("dp", "inner"), None),
            P(("dp", "inner"), None),
            P(("dp", "inner"), None),
            P(("dp", "inner"), None),
            P(None, ("dp", "inner")),
            P(None, ("dp", "inner")),
            P(None, ("dp", "inner")),
            P(("dp", "inner")),
            P(("dp", "inner")),
            P(("dp", "inner")),
        ),
        out_specs=(
            P(("dp", "inner"), None),
            P(("dp", "inner"), None),
            P(),
            P(None, ("dp", "inner"), None),
            P(None, ("dp", "inner"), None),
            P(None, ("dp", "inner"), None),
            P(None, ("dp", "inner"), None),
            P(None, ("dp", "inner"), None),
            P(None, ("dp", "inner"), None),
            P(("dp", "inner"), None),
            P(("dp", "inner"), None),
            P(("dp", "inner"), None),
            P(("dp", "inner"), None),
            P(("dp", "inner"), None),
            P(("dp", "inner"), None),
            P(None, ("dp", "inner")),
            P(None, ("dp", "inner")),
            P(None, ("dp", "inner")),
            P(("dp", "inner")),
            P(("dp", "inner")),
            P(("dp", "inner")),
        ),
        check_vma=False,
    )
```

```python
import functools
import jax
import jax.numpy as jnp
from jax import lax
from jax.experimental import pallas as pl
from jax.experimental.pallas import tpu as pltpu
from jax.sharding import PartitionSpec as P

AXES = ("dp", "inner")
HEADS = 8
HEAD = 64
STEP = 10
LOG2E = 1.4426950408889634
BLOCK = 256


norm_eps = 1e-05
first_decay = 0.9
second_decay = 0.999
adam_eps = 1e-08
learn_rate = 0.05
vector_rate = 0.8
weight_decay = 0.1
clip_norm = 1.0
masked_score = -1e30


def normalize_parts(values, gain_row, bias_row):
    centred = values - jnp.mean(values, -1, keepdims=True)
    spread = jnp.mean(centred * centred, -1, keepdims=True)
    scale_row = lax.rsqrt(spread + norm_eps)
    unit_rows = centred * scale_row
    return (unit_rows * gain_row + bias_row, unit_rows, scale_row)


def normalize_back(grad_rows, unit_rows, scale_row, gain_row):
    grad_unit = grad_rows * gain_row
    return scale_row * (
        grad_unit
        - jnp.mean(grad_unit, -1, keepdims=True)
        - unit_rows * jnp.mean(grad_unit * unit_rows, -1, keepdims=True)
    )


def bit_groups(sizes):
    dp_bits = sizes["dp"].bit_length() - 1
    inner_bits = sizes["inner"].bit_length() - 1
    y_bits = dp_bits // 2
    plane_bits = (inner_bits - 1) + y_bits
    return (1, plane_bits, dp_bits - y_bits)


def swap_with(array, offset, count):
    return lax.ppermute(array, AXES, [(source, source ^ offset) for source in range(count)])


def stage_bits(groups):
    return ((0, groups[0]), (groups[0], groups[1]), (groups[0] + groups[1], groups[2]))


def gather_z(shard, groups):
    count = 2 ** sum(groups)
    first_bit, bits = stage_bits(groups)[2]
    return jnp.stack([shard] + [swap_with(shard, offset << first_bit, count) for offset in range(1, 2**bits)])


def gather_plane(column, groups):
    count = 2 ** sum(groups)
    first_bit, bits = stage_bits(groups)[1]
    return [swap_with(column, offset << first_bit, count) for offset in range(1, 2**bits)]


def gather_core(column, planes, groups):
    return swap_with(jnp.concatenate([column] + planes), 1, 2 ** sum(groups))


def offsets_of(groups):
    (_, _), (plane_bit, plane_bits), (z_bit, z_bits) = stage_bits(groups)
    table = [
        [(plane << plane_bit) | (z << z_bit) for z in range(2**z_bits)] for plane in range(2**plane_bits)
    ]
    return table + [[offset | 1 for row in table for offset in row]]


def plane_orders(groups):
    _, (first_bit, bits), _ = stage_bits(groups)
    order = list(range(first_bit, first_bit + bits))
    return order, order[bits // 2 :] + order[: bits // 2]


def z_offsets(groups):
    _, _, (first_bit, bits) = stage_bits(groups)
    return [z << first_bit for z in range(2**bits)]


def send_halves(arrays, orders, position, groups):
    count = 2 ** sum(groups)
    return [swap_with(array, 1 << order[position], count) for array, order in zip(arrays, orders)]


def flip_tables(tables, bits):
    return [[offset ^ (1 << bit) for offset in table] for table, bit in zip(tables, bits)]


def vmem_spec():
    return pl.BlockSpec(memory_space=pltpu.VMEM)


def smem_spec():
    return pl.BlockSpec(memory_space=pltpu.SMEM)


def place(own, parts, tables, layout, groups):
    count = 2 ** sum(groups)
    step, width = parts[0].shape[2:]
    firsts = sorted({first for _, first in tables})
    groups_of = []
    for first in firsts:
        chosen = [(part, row) for part, (row, base) in zip(parts, tables) if base == first]
        order = jnp.argsort(jnp.array([o for _, row in chosen for o in row]) ^ own)
        groups_of.append(jnp.concatenate([part for part, _ in chosen])[order])
    full = jnp.concatenate(groups_of, 1)
    result = []
    for kind, first, pieces in layout:
        chosen = full[:, first : first + pieces]
        if kind == "sum":
            result.append(jnp.sum(chosen.astype(jnp.float32), 0).reshape(pieces * step, width))
        elif kind == "stack":
            result.append(jnp.moveaxis(chosen, 0, 1))
        elif kind == "rows":
            result.append(chosen)
        else:
            result.append(jnp.moveaxis(chosen, 1, 2).reshape(count, step, pieces * width))
    return result


def split(own, grads, layout, groups):
    count = 2 ** sum(groups)
    width = 512
    step = grads[0].shape[-2]
    offsets = [offset for row in offsets_of(groups)[:-1] for offset in row]
    pieces_of = []
    for grad, (kind, _, pieces) in zip(grads, layout):
        if kind == "stack":
            grad = jnp.moveaxis(grad, 1, 0)
        elif kind == "columns":
            grad = jnp.moveaxis(grad.reshape(count, step, pieces, width), 2, 1)
        pieces_of.append(grad)
    full = jnp.concatenate(pieces_of, 1)
    order = jnp.array(offsets) ^ own
    return full[order], full[order ^ 1]


def plane_sums(kept, received, groups):
    _, (_, bits), (_, z_bits) = stage_bits(groups)
    shape = (2**bits, 2**z_bits) + kept.shape[1:]
    kept = kept.reshape(shape)
    received = received.reshape(shape)
    total = lambda offset: kept[offset].astype(jnp.float32) + received[offset].astype(jnp.float32)
    return total(0), [total(offset).astype(jnp.bfloat16) for offset in range(1, 2**bits)]


def plane_send(parts, groups):
    first_bit = stage_bits(groups)[1][0]
    return [swap_with(part, offset << first_bit, 2 ** sum(groups)) for offset, part in enumerate(parts, 1)]


def reduce_z(own_part, arrived, groups):
    count = 2 ** sum(groups)
    first_bit, bits = stage_bits(groups)[2]
    total = lambda z: own_part[z] + sum(part[z].astype(jnp.float32) for part in arrived)
    return total(0), [
        swap_with(total(z).astype(jnp.bfloat16), z << first_bit, count) for z in range(2**bits - 1, 0, -1)
    ]


def finish_kernel(sums_ref, gain_ref, shift_ref, *refs):
    *ins, total_a_ref, total_b_ref, payload_ref = refs
    half = len(ins) // 2
    squares = 0.0
    for group, target in ((ins[:half], total_a_ref), (ins[half:], total_b_ref)):
        for piece in range(target.shape[0]):
            total = group[0][piece]
            for arrived in group[1:]:
                total = total + arrived[piece].astype(jnp.float32)
            target[piece] = total
            squares = squares + total * total
    payload_ref[...] = sums_ref[...]
    payload_ref[0:1, :] = gain_ref[...]
    payload_ref[1:2, :] = shift_ref[...]
    payload_ref[11:12, :] = jnp.sum(squares, 0, keepdims=True)


def finish(sums, gain, shift, own_a, z_a, own_b, z_b):
    ins = [sums, gain[None], shift[None], own_a, *z_a, own_b, *z_b]
    return pl.pallas_call(
        finish_kernel,
        in_specs=[vmem_spec() for _ in ins],
        out_specs=[vmem_spec() for _ in range(3)],
        out_shape=[jax.ShapeDtypeStruct(value.shape, jnp.float32) for value in (own_a, own_b, sums)],
        name="finish",
    )(*ins)


def tree_sum(values):
    while len(values) > 1:
        values = [one + two for one, two in zip(values[::2], values[1::2])]
    return values[0]


def sum_all(value, groups):
    count = 2 ** sum(groups)
    values = [value]
    for first_bit, bits in stage_bits(groups):
        value = tree_sum(values)
        values = [value] + [swap_with(value, offset << first_bit, count) for offset in range(1, 2**bits)]
    return values


def tie(*values):
    return lax.optimization_barrier(values)


def small_shard(vec, bias, own, count, width):
    step = vec.shape[1]
    lane = lax.broadcasted_iota(jnp.int32, (7, width), 1)
    rows = jnp.where(lane // step == own, jnp.tile(vec, (1, count)), 0.0)
    place_of = lax.broadcasted_iota(jnp.int32, (4, width), 0) * width + lax.broadcasted_iota(
        jnp.int32, (4, width), 1
    )
    tiled = jnp.tile(bias, width // bias.shape[0])[None]
    bias_rows = jnp.where(place_of // bias.shape[0] == own, tiled, 0.0)
    return jnp.concatenate([rows, bias_rows])


def pad_rows(rows, step):
    pieces = -(-rows.shape[0] // step)
    rows = jnp.pad(rows.astype(jnp.bfloat16), ((0, pieces * step - rows.shape[0]), (0, 0)))
    return rows.reshape(pieces, step, rows.shape[1])


def mat(a,b,dims):
    return lax.dot_general(a,b,(dims,((),())),preferred_element_type=jnp.float32)

def fill_bias(bias_ref, seg_row, pos_row):
    rows = bias_ref.shape[0]
    step = min(BLOCK, rows)
    for first in range(0, rows, step):
        seg_keys, pos_keys = [
            jnp.broadcast_to(ref[:, first : first + step], (8, step)).T[:, 0:1] for ref in (seg_row, pos_row)
        ]
        allowed = (seg_keys == seg_row[:, first:]) & (pos_keys <= pos_row[:, first:])
        bias_ref[first : first + step, first:] = jnp.where(allowed, 0.0, masked_score)


def head_lanes(shape, which):
    lane=lax.broadcasted_iota(jnp.int32,shape,1)
    return (lane//HEAD)==which

def attn_fwd_kernel(direct, tables, layout, own_ref, segr, posr, x_ref, *refs):
    part_count = len(tables) if direct else 2
    parts = refs[:part_count]
    h_ref, q_ref, k_ref, v_ref, o_ref, lse_ref, *rest = refs[part_count:]
    bias_ref, q_all, k_all, v_all = rest[-4:]
    rows = x_ref.shape[0]
    step = min(BLOCK, rows)
    lanes = q_ref.shape[1]
    pair = lanes // HEAD
    const = HEAD**-0.5 * LOG2E
    low = lambda value: value.astype(jnp.bfloat16)
    weights, vectors = rest[:2] if direct else parts
    tile = pl.program_id(0)

    @pl.when(tile == 0)
    def _():
        if direct:
            copy_parts(tables, layout, own_ref[0], parts, [weights, vectors])
        fill_bias(bias_ref, segr, posr)
        for first in range(0, rows, step):
            x = x_ref[first : first + step, :].astype(jnp.float32)
            h_ref[first : first + step, :] = low(normalize_parts(x, vectors[0:1, :], vectors[1:2, :])[0])
        for j, target in enumerate((q_all, k_all, v_all)):
            whole = low(mat(h_ref[...], weights[j].reshape(-1, weights.shape[-1]), ((1,), (0,))))
            for which in range(target.shape[0]):
                target[which] = whole[:, which * lanes : (which + 1) * lanes]

    q_ref[...] = q_all[tile]
    k_ref[...] = k_all[tile]
    v_ref[...] = v_all[tile]
    for first in range(0, rows, step):
        keys = first + step
        q = q_ref[first:keys, :]
        mixed = None
        for which in range(pair):
            own = head_lanes(q.shape, which)
            qh = jnp.where(own, q, jnp.zeros_like(q))
            s = mat(k_ref[:keys, :], qh, ((1,), (1,))) * const + bias_ref[:keys, first:keys]
            m = jnp.max(s, 0, keepdims=True)
            w = jnp.exp2(s - m)
            total = jnp.sum(w, 0, keepdims=True)
            p = (w * (1.0 / total)).astype(jnp.bfloat16)
            o = mat(p, v_ref[:keys, :], ((0,), (0,)))
            mixed = o if mixed is None else jnp.where(own, o, mixed)
            lse_ref[0, which : which + 1, first:keys] = m + jnp.log2(total)
        o_ref[first:keys, :] = mixed.astype(jnp.bfloat16)


def attn_bwd_kernel(
    offsets, own_ref, segr, posr, q_ref, k_ref, v_ref, do_ref, lse_ref, h_ref, w_ref, start_ref, *refs
):
    *outs, dh_ref, bias_ref, dk_acc, dv_acc, ht_ref, dw_ref = refs
    rows = q_ref.shape[0]

    @pl.when(pl.program_id(0) == 0)
    def _():
        fill_bias(bias_ref, segr, posr)
        ht_ref[...] = h_ref[...].T
        dh_ref[...] = start_ref[...]

    step = min(BLOCK, rows)
    pair = q_ref.shape[1] // HEAD
    const = HEAD**-0.5 * LOG2E
    scale = HEAD**-0.5
    dk_acc[...] = jnp.zeros_like(dk_acc)
    dv_acc[...] = jnp.zeros_like(dv_acc)
    dq_parts = []
    for first in range(0, rows, step):
        keys = first + step
        q = q_ref[first:keys, :]
        do = do_ref[first:keys, :]
        dq = None
        for which in range(pair):
            own = head_lanes(q.shape, which)
            qh = jnp.where(own, q, jnp.zeros_like(q))
            doh = jnp.where(own, do, jnp.zeros_like(do))
            s = mat(k_ref[:keys, :], qh, ((1,), (1,)))
            p = jnp.exp2(s * const + (bias_ref[:keys, first:keys] - lse_ref[0, which : which + 1, first:keys]))
            dp = mat(v_ref[:keys, :], doh, ((1,), (1,)))
            inner = jnp.sum(p * dp, 0, keepdims=True)
            ds = (p * (dp - inner)).astype(jnp.bfloat16)
            dv_acc[:keys, :] += mat(p.astype(jnp.bfloat16), doh, ((1,), (0,)))
            dk_acc[:keys, :] += mat(ds, qh, ((1,), (0,)))
            d = mat(ds, k_ref[:keys, :], ((0,), (0,)))
            dq = d if dq is None else jnp.where(own, d, dq)
        dq_parts.append((dq * scale).astype(jnp.bfloat16))
    grads = jnp.concatenate(
        [
            jnp.concatenate(dq_parts, 0),
            (dk_acc[...] * scale).astype(jnp.bfloat16),
            dv_acc[...].astype(jnp.bfloat16),
        ],
        1,
    )
    weights = jnp.concatenate([w_ref[0], w_ref[1], w_ref[2]], 1)
    dh_ref[...] += mat(grads, weights, ((1,), (1,)))
    dw = mat(ht_ref[...], grads, ((1,), (0,))).astype(jnp.bfloat16)
    lanes = q_ref.shape[1]
    if offsets is None:
        for j in range(3):
            outs[0][j] = dw[:, j * lanes : (j + 1) * lanes]
    else:
        dw_ref[...] = dw.reshape(dw_ref.shape)
        for entry, offset in enumerate(offsets):
            for side in range(2):
                owner = own_ref[0] ^ (offset | side)
                for j in range(3):
                    outs[side][entry, j] = dw_ref[owner, :, j * lanes : (j + 1) * lanes]


def const_map(*_): return (0,0)

def attend(own, tokens, marks, parts, tables, layout, groups):
    rows, width = tokens.shape
    count = 2 ** sum(groups)
    step = parts[0].shape[2]
    lanes = 2 * HEAD
    pairs = width // lanes
    low = jnp.bfloat16
    direct = step % 16 == 0
    blk = pl.BlockSpec((rows, lanes), lambda j: (0, j))
    whole = lambda shape: pl.BlockSpec(shape, lambda j: (0,) * len(shape), pipeline_mode=pl.Buffered(1))
    half = jax.ShapeDtypeStruct((rows, width), low)
    out_shape = [half] * 5 + [jax.ShapeDtypeStruct((pairs, 2, rows), jnp.float32)]
    out_specs = [whole((rows, width)), blk, blk, blk, blk, pl.BlockSpec((1, 2, rows), lambda j: (j, 0, 0))]
    if direct:
        extra = [
            jax.ShapeDtypeStruct((3, count, step, width), low),
            jax.ShapeDtypeStruct((step, width), jnp.float32),
        ]
        out_shape += extra
        out_specs += [whole(item.shape) for item in extra]
    else:
        parts = place(own, parts, tables, layout, groups)
    result = pl.pallas_call(
        functools.partial(attn_fwd_kernel, direct, tables, layout),
        grid=(pairs,),
        in_specs=[smem_spec(), whole((1, rows)), whole((1, rows))]
        + [whole((rows, width))]
        + [whole(part.shape) for part in parts],
        out_specs=out_specs,
        out_shape=out_shape,
        scratch_shapes=[pltpu.VMEM((rows, rows), jnp.float32)] + [pltpu.VMEM((pairs, rows, lanes), low)] * 3,
        name="attn_fwd",
    )(own[None].astype(jnp.int32), *marks, tokens, *parts)
    if not direct:
        result = list(result) + list(parts)
    return result


def attend_back(own, q, k, v, do, lse, marks, normed, w_qkv, start, groups):
    rows, width = q.shape
    lanes = 2 * HEAD
    count = 2 ** sum(groups)
    inputs = w_qkv.shape[1]
    step = inputs // count
    blk = pl.BlockSpec((rows, lanes), lambda j: (0, j))
    row = pl.BlockSpec((1, rows), const_map)
    offsets = None
    if step % 16 == 0:
        offsets = [offset for table in offsets_of(groups)[:-1] for offset in table]
        shape = (len(offsets), 3, step, width)
        out_specs = [pl.BlockSpec(shape[:3] + (lanes,), lambda j: (0, 0, 0, j)) for _ in range(2)]
        out_shape = [jax.ShapeDtypeStruct(shape, jnp.bfloat16) for _ in range(2)]
        dw_scratch = pltpu.VMEM((count, step, 3 * lanes), jnp.bfloat16)
    else:
        out_specs = [pl.BlockSpec((3, inputs, lanes), lambda j: (0, 0, j))]
        out_shape = [jax.ShapeDtypeStruct((3, inputs, width), jnp.bfloat16)]
        dw_scratch = pltpu.VMEM((16, lanes), jnp.bfloat16)
    *grads, dh = pl.pallas_call(
        functools.partial(attn_bwd_kernel, offsets),
        grid=(width // lanes,),
        in_specs=[smem_spec(), row, row, blk, blk, blk, blk]
        + [
            pl.BlockSpec((1, 2, rows), lambda j: (j, 0, 0)),
            pl.BlockSpec((rows, inputs), const_map),
            pl.BlockSpec((3, inputs, lanes), lambda j: (0, 0, j)),
            pl.BlockSpec((rows, inputs), const_map),
        ],
        out_specs=out_specs + [pl.BlockSpec((rows, inputs), const_map)],
        out_shape=out_shape + [jax.ShapeDtypeStruct((rows, inputs), jnp.float32)],
        scratch_shapes=[
            pltpu.VMEM((rows, rows), jnp.float32),
            pltpu.VMEM((rows, lanes), jnp.float32),
            pltpu.VMEM((rows, lanes), jnp.float32),
            pltpu.VMEM((inputs, rows), jnp.bfloat16),
            dw_scratch,
        ],
        name="attn_bwd",
    )(own[None].astype(jnp.int32), *marks, q, k, v, do, lse, normed, w_qkv, start)
    if offsets is None:
        grads = split(own, [grads[0].reshape(3, count, step, width)], [("stack", 0, 3)], groups)
    return grads[0], grads[1], dh


def copy_parts(tables, layout, own, parts, outs):
    where_to = [
        (index, kind, piece) for index, (kind, _, pieces) in enumerate(layout) for piece in range(pieces)
    ]
    total = None
    for part, (row, first) in zip(parts, tables):
        width = part.shape[3]
        for entry, offset in enumerate(row):
            owner = own ^ offset
            for source in range(part.shape[1]):
                index, kind, piece = where_to[first + source]
                block = part[entry, source]
                if kind == "sum":
                    block = block.astype(jnp.float32)
                    total = block if total is None else total + block
                elif kind == "stack":
                    outs[index][piece, owner] = block
                elif kind == "rows":
                    outs[index][owner, piece] = block
                else:
                    outs[index][owner, :, piece * width : (piece + 1) * width] = block
    for index, (kind, _, _) in enumerate(layout):
        if kind == "sum":
            outs[index][...] = total


def copy_blocks(offsets, layout, own, ins, kept, sent):
    width = kept.shape[3]
    for entry, offset in enumerate(offsets):
        for side, target in enumerate((kept, sent)):
            owner = own ^ (offset | side)
            for index, (kind, first, pieces) in enumerate(layout):
                for piece in range(pieces):
                    if kind == "stack":
                        block = ins[index][piece, owner]
                    elif kind == "rows":
                        block = ins[index][owner, piece]
                    else:
                        block = ins[index][owner, :, piece * width : (piece + 1) * width]
                    target[entry, first + piece] = block


def ffn_kernel(direct, part_count, tables, offsets, layout, own_ref, x_ref, cot_ref, h_ref, o_ref, vec_ref, *refs):
    low = lambda value: value.astype(jnp.bfloat16)
    parts = refs[:part_count]
    out_count = 5 + (2 if direct else 5)
    outs = refs[part_count : part_count + out_count]
    scratch = refs[part_count + out_count :]
    y_ref, do_ref, dh_ref, dx_ref, dvec_ref = outs[:5]
    r_ref, dz_ref, h2_ref, df_ref, dzf_ref, da_ref, dza_ref = scratch[:7]
    tile = pl.program_id(0)
    if direct:
        weights = targets = scratch[7:]

        @pl.when(tile == 0)
        def _():
            copy_parts(tables, layout, own_ref[0], parts, weights)

    else:
        weights, targets = parts, outs[5:]
    width = x_ref.shape[1]
    size = x_ref.shape[0]
    chunks = r_ref.shape[0]
    load = lambda index: weights[index][...].reshape(-1, weights[index].shape[-1])
    rows = pl.ds(tile * size, size)

    @pl.when(tile == 0)
    def _():
        dvec_ref[...] = jnp.zeros_like(dvec_ref)

    forward = ((1,), (0,))
    backward = ((1,), (1,))
    x = x_ref[...].astype(jnp.float32)
    a = mat(o_ref[rows, :], load(0), forward)
    ga = jax.nn.sigmoid(mat(h_ref[rows, :], load(1), forward) + vec_ref[4:5, :])
    x1 = ga * a + (1.0 - ga) * x
    gain = vec_ref[2:3, :]
    h2_full, n2, s2 = normalize_parts(x1, gain, vec_ref[3:4, :])
    h2 = low(h2_full)
    bias = jnp.concatenate([vec_ref[7 + chunk : 8 + chunk, :] for chunk in range(chunks)], 1)
    z = mat(h2, load(3), forward) + bias
    r = low(jnp.maximum(z, 0.0))
    f = mat(r, load(4), forward) + vec_ref[6:7, :]
    gf = jax.nn.sigmoid(mat(h2, load(2), forward) + vec_ref[5:6, :])
    y_ref[...] = low(gf * f + (1.0 - gf) * x1)
    dy = cot_ref[...].astype(jnp.float32)
    df = dy * gf
    dzf = dy * (f - x1) * gf * (1.0 - gf)
    dx1 = dy * (1.0 - gf)
    dfb = low(df)
    dzfb = low(dzf)
    dz = jnp.where(z > 0.0, mat(dfb, load(4), backward), 0.0)
    dzb = low(dz)
    dh2 = mat(dzb, load(3), backward) + mat(dzfb, load(2), backward)
    dx1 = dx1 + normalize_back(dh2, n2, s2, gain)
    da = low(dx1 * ga)
    dza = dx1 * (a - x) * ga * (1.0 - ga)
    dzab = low(dza)
    dx_ref[...] = dx1 * (1.0 - ga)
    do_ref[...] = low(mat(da, load(0), backward))
    dh_ref[...] = mat(dzab, load(1), backward)
    total = lambda value: jnp.sum(value, 0, keepdims=True)
    sums = [total(dh2 * n2), total(dh2), total(dza), total(dzf), total(df)]
    hidden_sums = total(dz)
    sums += [hidden_sums[:, chunk * width : (chunk + 1) * width] for chunk in range(chunks)]
    for index, value in enumerate(sums):
        dvec_ref[2 + index : 3 + index, :] += value
    for chunk in range(chunks):
        r_ref[chunk, rows, :] = r[:, chunk * width : (chunk + 1) * width]
        dz_ref[chunk, rows, :] = dzb[:, chunk * width : (chunk + 1) * width]
    h2_ref[rows, :] = h2
    df_ref[rows, :] = dfb
    dzf_ref[rows, :] = dzfb
    da_ref[rows, :] = da
    dza_ref[rows, :] = dzab

    @pl.when(tile == pl.num_programs(0) - 1)
    def _():
        across = lambda left, right: low(mat(left, right, forward))
        targets[0][...] = across(o_ref[...].T, da_ref[...]).reshape(targets[0].shape)
        targets[1][...] = across(h_ref[...].T, dza_ref[...]).reshape(targets[1].shape)
        h2_turned = h2_ref[...].T
        targets[2][...] = across(h2_turned, dzf_ref[...]).reshape(targets[2].shape)
        for chunk in range(chunks):
            lanes = slice(chunk * width, (chunk + 1) * width)
            grad_in = across(h2_turned, dz_ref[chunk])
            grad_out = across(r_ref[chunk].T, df_ref[...])
            if direct:
                owners = targets[4].shape[0] // chunks
                targets[3][:, :, lanes] = grad_in.reshape(targets[3].shape[:2] + (width,))
                targets[4][chunk * owners : (chunk + 1) * owners] = grad_out.reshape(
                    (owners,) + targets[4].shape[1:]
                )
            else:
                targets[3][:, lanes] = grad_in
                targets[4][lanes, :] = grad_out
        if direct:
            copy_blocks(offsets, layout, own_ref[0], targets, *outs[5:])


FFN_LAYOUT = [("stack", 0, 1), ("stack", 1, 1), ("stack", 2, 1), ("columns", 3, 4), ("rows", 7, 4)]


def ffn(own, tokens, cotangent, normed, mixed_heads, vectors, hidden, parts, tables, groups):
    rows, width = tokens.shape
    count = 2 ** sum(groups)
    step = parts[0].shape[2]
    chunks = hidden // width
    tile = min(256, rows)
    direct = step % 16 == 0
    offsets = [offset for row in offsets_of(groups)[:-1] for offset in row]
    matrices = [(width, width)] * 3 + [(width, hidden), (hidden, width)]
    low = jnp.bfloat16
    once = dict(pipeline_mode=pl.Buffered(1))
    block = pl.BlockSpec((tile, width), lambda i: (i, 0))
    whole = lambda shape: pl.BlockSpec(shape, lambda i: (0,) * len(shape), **once)
    scratch = [pltpu.VMEM((chunks, rows, width), low)] * 2 + [pltpu.VMEM((rows, width), low)] * 5
    if direct:
        shape = (len(offsets), 3 + 2 * chunks, step, width)
        grads = [jax.ShapeDtypeStruct(shape, low)] * 2
        scratch += [pltpu.VMEM((1, count, step, width), low)] * 3
        scratch += [pltpu.VMEM((count, step, hidden), low), pltpu.VMEM((count, chunks, step, width), low)]
    else:
        placed = place(own, parts, tables, FFN_LAYOUT, groups)
        parts = [weight.reshape(shape) for weight, shape in zip(placed, matrices)]
        grads = [jax.ShapeDtypeStruct(shape, low) for shape in matrices]
    full = jax.ShapeDtypeStruct((rows, width), jnp.float32)
    half = jax.ShapeDtypeStruct((rows, width), low)
    small = [jax.ShapeDtypeStruct((12, width), jnp.float32)]
    result = pl.pallas_call(
        functools.partial(ffn_kernel, direct, len(parts), tables, offsets, FFN_LAYOUT),
        grid=(rows // tile,),
        in_specs=[smem_spec(), block, block, whole((rows, width)), whole((rows, width))]
        + [whole(vectors.shape)]
        + [whole(part.shape) for part in parts],
        out_specs=[block] * 4 + [whole(item.shape) for item in small + grads],
        out_shape=[half, half, full, full] + small + grads,
        scratch_shapes=scratch,
        name="ffn",
    )(own[None].astype(jnp.int32), tokens, cotangent, normed, mixed_heads, vectors, *parts)
    if not direct:
        blocks = [grad.reshape(1, count, step, width) for grad in result[5:8]]
        blocks += [result[8].reshape(count, step, hidden), result[9].reshape(count, chunks, step, width)]
        result = list(result[:5]) + list(split(own, blocks, FFN_LAYOUT, groups))
    return result


def adam_update(weight, first_moment, second_moment, gradient, factor, step_rate):
    clipped = gradient * factor
    first_new = first_decay * first_moment + (1.0 - first_decay) * clipped
    second_new = second_decay * second_moment + (1.0 - second_decay) * clipped * clipped
    corrected = first_new / (1.0 - first_decay**STEP)
    spread = second_new / (1.0 - second_decay**STEP)
    weight_new = weight - step_rate * (
        corrected / (jnp.sqrt(spread) + adam_eps) + weight_decay * weight
    )
    return (weight_new, first_new, second_new)


def own_lanes(rows, first, lanes):
    width = rows.shape[1]
    return pltpu.roll(rows, (width - first) % width, 1)[:, :lanes]


def update_kernel(terms, own_ref, a_ref, b_ref, *refs):
    payload = tree_sum([ref[...] for ref in refs[:terms]])
    refs = refs[terms:]
    states = [refs[3 * index : 3 * index + 3] for index in range(6)]
    norm_ref = refs[18]
    news = [refs[19 + 3 * index : 22 + 3 * index] for index in range(6)]
    line = lax.broadcasted_iota(jnp.int32, payload.shape, 0)
    squares = jnp.where(line == 11, payload, payload * payload)
    norm = jnp.sqrt(jnp.sum(jnp.sum(squares, 1, keepdims=True), 0, keepdims=True))
    norm_ref[...] = norm
    factor = jnp.minimum(1.0, clip_norm / (norm + 1e-06))

    def update(index, where, gradient):
        rate = vector_rate if index > 3 else learn_rate
        values = adam_update(*[ref[where] for ref in states[index]], gradient, factor, rate)
        for ref, value in zip(news[index], values):
            ref[where] = value

    width = a_ref.shape[2]
    for piece in range(3):
        update(0, piece, a_ref[piece])
    update(0, 3, b_ref[0])
    for piece in range(2):
        update(1, piece, b_ref[1 + piece])
    chunks = (b_ref.shape[0] - 3) // 2
    step = b_ref.shape[1]
    for chunk in range(chunks):
        update(2, (slice(None), slice(chunk * width, (chunk + 1) * width)), b_ref[3 + chunk])
        update(3, slice(chunk * step, (chunk + 1) * step), b_ref[3 + chunks + chunk])
    own = own_ref[0]
    vec_lanes = states[4][0].shape[1]
    update(4, Ellipsis, own_lanes(payload[0:8], own * vec_lanes, vec_lanes)[:7])
    bias_lanes = states[5][0].shape[1]
    first = own * bias_lanes
    picked = jnp.sum(jnp.where(line == 7 + first // width, payload, 0.0), 0, keepdims=True)
    picked = own_lanes(jnp.broadcast_to(picked, (8, width)), first % width, bias_lanes)
    update(5, Ellipsis, picked[0:1])


def update_all(own, payload, total_a, total_b, states):
    flat = [value for state in states for value in state]
    shapes = [jax.ShapeDtypeStruct(value.shape, jnp.float32) for value in flat]
    norm, *news = pl.pallas_call(
        functools.partial(update_kernel, len(payload)),
        in_specs=[smem_spec()] + [vmem_spec() for _ in range(2 + len(payload) + len(flat))],
        out_specs=[vmem_spec() for _ in range(1 + len(flat))],
        out_shape=[jax.ShapeDtypeStruct((1, 1), jnp.float32)] + shapes,
        name="update",
    )(own[None].astype(jnp.int32), total_a, total_b, *payload, *flat)
    return norm[0, 0], [news[3 * index : 3 * index + 3] for index in range(len(states))]


def body(
    groups,
    tokens,
    segments,
    positions,
    cotangent,
    attn_weight,
    attn_m,
    attn_v,
    gate_weight,
    gate_m,
    gate_v,
    in_weight,
    in_m,
    in_v,
    out_weight,
    out_m,
    out_v,
    norm_params,
    norm_m,
    norm_v,
    in_bias,
    bias_m,
    bias_v,
):
    count = 2 ** sum(groups)
    own = lax.axis_index(AXES)
    width = 512
    step = attn_weight.shape[1]
    low = lambda value: value.astype(jnp.bfloat16)
    dot = functools.partial(jnp.einsum, preferred_element_type=jnp.float32)
    columns = lambda value: [value[:, width * j : width * (j + 1)] for j in range(4)]
    small = pad_rows(small_shard(norm_params, in_bias, own, count, width), step)
    extra = small.shape[0]
    first_shard = jnp.concatenate([low(attn_weight[:3]), small])
    second_shard = jnp.concatenate(
        [
            low(attn_weight[3:]),
            low(gate_weight),
            jnp.stack(columns(low(in_weight))),
            low(out_weight).reshape(4, step, width),
        ]
    )
    cut = 6
    orders = plane_orders(groups)
    z_first = gather_z(first_shard, groups)
    plane_first = gather_plane(z_first, groups)
    z_second = gather_z(second_shard, groups)
    tied = tie(z_first, z_second[:, :cut], z_second[:, cut:], *plane_first)
    z_first, halves, plane_first = tied[0], tied[1:3], list(tied[3:])
    core_first = gather_core(z_first, plane_first, groups)
    tables = [z_offsets(groups)] * 2
    received = send_halves(halves, orders, 0, groups)
    inputs = tokens.astype(jnp.float32)
    mean_one = jnp.mean(inputs, -1, keepdims=True)
    scale_one = lax.rsqrt(jnp.mean((inputs - mean_one) * (inputs - mean_one), -1, keepdims=True) + norm_eps)
    marks = (segments[None], positions[None])
    core_first, mean_one, scale_one, *tied = tie(core_first, mean_one, scale_one, *marks, *received)
    marks, received = tied[:2], tied[2:]
    last = len(orders[0]) - 1
    for position in range(last):
        tables = [
            table + row
            for table, row in zip(tables, flip_tables(tables, [order[position] for order in orders]))
        ]
        halves = [jnp.concatenate(pair) for pair in zip(halves, received)]
        received = send_halves(halves, orders, position + 1, groups)
    far_tables = flip_tables(tables, [order[last] for order in orders])
    relative = offsets_of(groups)
    normed, queries, keys, values, mixed_heads, log_total, w_qkv, vectors = attend(
        own,
        tokens,
        marks,
        [z_first] + plane_first + [core_first],
        [(row, 0) for row in relative],
        [("stack", 0, 3), ("sum", 3, extra)],
        groups,
    )
    w_qkv = w_qkv.reshape(3, count * step, width)
    core_near = [swap_with(half, 1, count) for half in halves]
    mixed_heads, *tied = tie(mixed_heads, *core_near, *received)
    core_near, received = tied[:2], tied[2:]
    core_far = [swap_with(half, 1, count) for half in received]
    unit_one = (inputs - mean_one) * scale_one
    layer_out, grad_mixed, grad_normed, grad_inputs, sums, kept_b, sent_b = ffn(
        own,
        tokens,
        cotangent,
        normed,
        mixed_heads,
        vectors,
        in_weight.shape[1],
        list(halves) + list(received) + list(core_near) + core_far,
        [
            ([offset | core for offset in table], first)
            for core in range(2)
            for half_tables in (tables, far_tables)
            for table, first in zip(half_tables, (0, cut))
        ],
        groups,
    )
    core_b = swap_with(sent_b, 1, count)
    core_b, kept_b, grad_mixed, gain_one = tie(core_b, kept_b, grad_mixed, vectors[0])
    own_b, parts_b = plane_sums(kept_b, core_b, groups)
    own_b, log_total, *parts_b = tie(own_b, log_total, *parts_b)
    plane_b = plane_send(parts_b, groups)
    kept_a, sent_a, grad_normed = attend_back(
        own, queries, keys, values, grad_mixed, log_total, marks, normed, w_qkv, grad_normed, groups
    )
    kept_a, sent_a, grad_normed, own_b, *plane_b = tie(kept_a, sent_a, grad_normed, own_b, *plane_b)
    core_a = swap_with(sent_a, 1, count)
    own_b, z_b = reduce_z(own_b, plane_b, groups)
    own_a, parts_a = plane_sums(kept_a, core_a, groups)
    grad_normed, own_a, *parts_a = tie(grad_normed, own_a, *parts_a)
    grad_gain_one = jnp.sum(grad_normed * unit_one, 0)
    grad_shift_one = jnp.sum(grad_normed, 0)
    grad_inputs = grad_inputs + normalize_back(grad_normed, unit_one, scale_one, gain_one)
    input_grad = low(grad_inputs)
    plane_a = plane_send(parts_a, groups)
    input_grad, grad_gain_one, grad_shift_one, *plane_a = tie(
        input_grad, grad_gain_one, grad_shift_one, *plane_a
    )
    own_a, z_a = reduce_z(own_a, plane_a, groups)
    total_a, total_b, payload = finish(sums, grad_gain_one, grad_shift_one, own_a, z_a, own_b, z_b)
    payload = sum_all(payload, groups)
    states = (
        (attn_weight, attn_m, attn_v),
        (gate_weight, gate_m, gate_v),
        (in_weight, in_m, in_v),
        (out_weight, out_m, out_v),
        (norm_params, norm_m, norm_v),
        (in_bias[None], bias_m[None], bias_v[None]),
    )
    grad_norm, updated = update_all(own, payload, total_a, total_b, states)
    return (
        layer_out,
        input_grad,
        grad_norm,
        updated[0][0],
        updated[0][1],
        updated[0][2],
        updated[1][0],
        updated[1][1],
        updated[1][2],
        updated[2][0],
        updated[2][1],
        updated[2][2],
        updated[3][0],
        updated[3][1],
        updated[3][2],
        updated[4][0],
        updated[4][1],
        updated[4][2],
        updated[5][0][0],
        updated[5][1][0],
        updated[5][2][0],
    )


def solution(mesh):
    return jax.shard_map(
        functools.partial(body, bit_groups(mesh.shape)),
        mesh=mesh,
        in_specs=(
            P(("dp", "inner"), None),
            P(("dp", "inner")),
            P(("dp", "inner")),
            P(("dp", "inner"), None),
            P(None, ("dp", "inner"), None),
            P(None, ("dp", "inner"), None),
            P(None, ("dp", "inner"), None),
            P(None, ("dp", "inner"), None),
            P(None, ("dp", "inner"), None),
            P(None, ("dp", "inner"), None),
            P(("dp", "inner"), None),
            P(("dp", "inner"), None),
            P(("dp", "inner"), None),
            P(("dp", "inner"), None),
            P(("dp", "inner"), None),
            P(("dp", "inner"), None),
            P(None, ("dp", "inner")),
            P(None, ("dp", "inner")),
            P(None, ("dp", "inner")),
            P(("dp", "inner")),
            P(("dp", "inner")),
            P(("dp", "inner")),
        ),
        out_specs=(
            P(("dp", "inner"), None),
            P(("dp", "inner"), None),
            P(),
            P(None, ("dp", "inner"), None),
            P(None, ("dp", "inner"), None),
            P(None, ("dp", "inner"), None),
            P(None, ("dp", "inner"), None),
            P(None, ("dp", "inner"), None),
            P(None, ("dp", "inner"), None),
            P(("dp", "inner"), None),
            P(("dp", "inner"), None),
            P(("dp", "inner"), None),
            P(("dp", "inner"), None),
            P(("dp", "inner"), None),
            P(("dp", "inner"), None),
            P(None, ("dp", "inner")),
            P(None, ("dp", "inner")),
            P(None, ("dp", "inner")),
            P(("dp", "inner")),
            P(("dp", "inner")),
            P(("dp", "inner")),
        ),
        check_vma=False,
    )
```
